512 devices in a mesh: tm: 128 (over y, x_hi, z), col: 4 (over x_lo, core).
Axes of the slice: x: 4 (x_hi: 2, x_lo: 2; x = x_hi * 2 + x_lo), y: 4, z: 16, core: 2. Of those that a mesh axis runs over, the one named last changes fastest.
Arguments:
- frames: bfloat16 [384, 2, 96, 384], P('tm', None, 'col'), may hold values from -6 to 6
- up_kernel: bfloat16 [10368, 256], P(None, 'tm'), may hold values from -0.109375 to 0.109375
- mix_kernel: bfloat16 [6912, 256], P(None, 'tm'), may hold values from -0.078125 to 0.078125
- cotangent: bfloat16 [768, 2, 96, 256], P('tm', None, 'col'), may hold values from -6 to 6
Outputs:
- decoded: bfloat16 [768, 2, 96, 256], P('tm', None, 'col')
- frames_grad: bfloat16 [384, 2, 96, 384], P('tm', None, 'col')
The draws below stay inside these ranges and needn't reach their ends.
All inputs are finite; a program needn't handle non-finite values.
Results may differ from the reference program's by a relative error of at most 0.005.
Values may be sent and summed in bfloat16 or wider, within the bound.
No kernel may reach another device: no remote copies, remote signals or barrier semaphores. Data moves between devices by JAX's collectives and lax.ppermute only.
A program may use at most 64 MiB of HBM per device.

```python
import jax
import jax.numpy as jnp
from jax import lax

CI = 384
C = 256
H = 2
FRAMES_IN = 384
COLUMNS = 96


def block_levels(stream_key, shape, cuts, low, top_value):
    level = 1.0
    for dim, blocks in cuts:
        steps = jax.random.uniform(jax.random.fold_in(jax.random.fold_in(stream_key, 6), dim), (blocks,), jnp.float32, low / len(cuts), top_value / len(cuts))
        level = level * jnp.repeat(jnp.exp(steps), shape[dim] // blocks).reshape((-1,) + (1,) * (len(shape) - 1 - dim))
    return level


def gaussian(key, shape, scale, limit, split=(), held_as=jnp.bfloat16):
    entries = scale * jax.random.normal(key, shape, jnp.float32)
    if split:
        entries = entries * block_levels(key, shape, split, -0.22, 0.18)
    return jnp.clip(entries, -limit, limit).astype(held_as)


def setup_inputs(seed: int = 0) -> dict:
    key_of = jax.random.split(jax.random.key(seed), 5)
    return {
        "frames": gaussian(key_of[0], (FRAMES_IN, H, COLUMNS, CI), 1.0, 6.0, ((0, 128), (2, 4))),
        "up_kernel": gaussian(key_of[1], (27 * CI, C), (9 * CI) ** -0.5, 0.109375, ((1, 128),)),
        "mix_kernel": gaussian(key_of[2], (27 * C, C), (27 * C) ** -0.5, 0.078125, ((1, 128),)),
        "cotangent": gaussian(key_of[3], (2 * FRAMES_IN, H, COLUMNS, C), 1.0, 6.0, ((0, 128), (2, 4))),
    }


def tap_product(window, matrix):
    return jnp.einsum("thwc,cd->thwd", window, matrix, precision=lax.Precision.HIGHEST)


def reference(frames, up_kernel, mix_kernel, cotangent):
    frame_count = frames.shape[0]
    height = frames.shape[1]
    width = frames.shape[2]
    count = 2 * frame_count
    up_taps = up_kernel.astype(jnp.float32).reshape(3, 3, 3, CI, C)
    mix_taps = mix_kernel.astype(jnp.float32).reshape(3, 3, 3, C, C)
    padded = jnp.pad(frames.astype(jnp.float32), ((0, 0), (1, 1), (1, 1), (0, 0)))
    parts = []
    for tap_t in range(3):
        total = jnp.zeros((frame_count, height, width, C), jnp.float32)
        for tap_h in range(3):
            for tap_w in range(3):
                total = total + tap_product(padded[:, tap_h:tap_h + height, tap_w:tap_w + width], up_taps[tap_t, tap_h, tap_w])
        parts.append(total)
    even = parts[0] + jnp.pad(parts[2], ((1, 0), (0, 0), (0, 0), (0, 0)))[:-1]
    before = jnp.stack((even, parts[1]), axis=1).reshape(count, height, width, C)
    hidden = jax.nn.silu(before).astype(jnp.bfloat16)
    hidden_pad = jnp.pad(hidden.astype(jnp.float32), ((2, 0), (1, 1), (1, 1), (0, 0)))
    cot_pad = jnp.pad(cotangent.astype(jnp.float32), ((0, 2), (1, 1), (1, 1), (0, 0)))
    output = jnp.zeros((count, height, width, C), jnp.float32)
    hidden_grad = jnp.zeros((count, height, width, C), jnp.float32)
    for tap_t in range(3):
        for tap_h in range(3):
            for tap_w in range(3):
                matrix = mix_taps[tap_t, tap_h, tap_w]
                output = output + tap_product(hidden_pad[tap_t:tap_t + count, tap_h:tap_h + height, tap_w:tap_w + width], matrix)
                hidden_grad = hidden_grad + tap_product(cot_pad[2 - tap_t:2 - tap_t + count, 2 - tap_h:2 - tap_h + height, 2 - tap_w:2 - tap_w + width], matrix.T)
    decoded = output.astype(jnp.bfloat16)
    sigma = jax.nn.sigmoid(before)
    before_grad = (hidden_grad * sigma * (1.0 + before * (1.0 - sigma))).astype(jnp.bfloat16)
    pairs = before_grad.astype(jnp.float32).reshape(frame_count, 2, height, width, C)
    evens = pairs[:, 0]
    odds = pairs[:, 1]
    later_evens = jnp.pad(evens, ((0, 1), (0, 0), (0, 0), (0, 0)))[1:]
    sources = (evens, odds, later_evens)
    grad_total = jnp.zeros((frame_count, height, width, CI), jnp.float32)
    for tap_t in range(3):
        source_pad = jnp.pad(sources[tap_t], ((0, 0), (1, 1), (1, 1), (0, 0)))
        for tap_h in range(3):
            for tap_w in range(3):
                grad_total = grad_total + tap_product(source_pad[:, 2 - tap_h:2 - tap_h + height, 2 - tap_w:2 - tap_w + width], up_taps[tap_t, tap_h, tap_w].T)
    return decoded, grad_total.astype(jnp.bfloat16)
```

```python
import jax
import jax.numpy as jnp
from jax import lax
from jax.sharding import Mesh, PartitionSpec as P

PLANES = ("y", "xh", "z")
COLS = ("xl", "core")
LANES = 128


def shift(array, axis, by):
    devices = lax.axis_size(axis)
    pairs = [(i, i + by) for i in range(devices) if 0 <= i + by < devices]
    return lax.ppermute(array, axis, pairs)


def cross(array):
    return lax.ppermute(array, ("xh", "xl"), [(0, 3), (3, 0), (1, 2), (2, 1)])


def swap(array):
    return lax.ppermute(array, "core", [(0, 1), (1, 0)])


def spread(array, axis):
    count = lax.axis_size(axis)
    return lax.all_to_all(
        jnp.broadcast_to(array, (count, *array.shape)), axis, 0, 0, tiled=True
    )


def gather(tiles):
    planes = spread(tiles, "z")
    depth = planes.shape[0]
    rows = planes.transpose(1, 0, 2, 3).reshape(tiles.shape[0], 2 * depth, LANES)
    return spread(rows, "y")


def convolve(field, kernel, strides=(1, 1, 1)):
    return lax.conv_general_dilated(
        field,
        kernel,
        strides,
        ((0, 0), (1, 1), (0, 0)),
        dimension_numbers=("NDHWC", "DHWIO", "NDHWC"),
        preferred_element_type=jnp.float32,
    )


def with_columns(field):
    width = field.shape[2]
    low = shift(field[:, :, width - 2 :], COLS, 1)
    high = shift(field[:, :, :2], COLS, -1)
    return jnp.concatenate((low, field, high), axis=2)


def tiles_of(kernel):
    return kernel.T.reshape(2, -1, LANES).transpose(1, 0, 2)


def shards(frames, up_kernel, mix_kernel, cotangent):
    frame_count, height, width, in_channels = frames.shape
    out_channels = mix_kernel.shape[0] // 27
    half = out_channels // 2
    xh, xl, core = lax.axis_index("xh"), lax.axis_index("xl"), lax.axis_index("core")
    planes_y, planes_z = lax.axis_size("y"), lax.axis_size("z")
    run = out_channels // planes_y // 2

    mix_other = cross(tiles_of(mix_kernel))
    up_tiles = tiles_of(up_kernel)
    up_count = up_tiles.shape[0]
    up_half = (up_count + 1) // 2
    up_part = lax.dynamic_slice_in_dim(up_tiles, core * (up_count - up_half), up_half, 0)
    up_rows = gather(up_part)

    mix_tiles = jnp.where(xh == core, tiles_of(mix_kernel), mix_other)
    source = lax.broadcasted_iota(jnp.int32, (out_channels, half), 0)
    target = lax.broadcasted_iota(jnp.int32, (out_channels, half), 1)
    wanted = (target // run) * (2 * run) + xh * run + target % run
    pick = (source == wanted).astype(jnp.bfloat16).reshape(-1, LANES, half)
    mix_part = jnp.einsum(
        "ktjl,tlm->kjm",
        mix_tiles.reshape(27, -1, 2, LANES),
        pick,
        preferred_element_type=jnp.float32,
    ).astype(jnp.bfloat16)
    mix_rows = gather(mix_part)

    wide_frames = with_columns(frames)
    wide_cot = with_columns(cotangent)
    long_frames = jnp.concatenate(
        (shift(wide_frames[-2:], PLANES, 1), wide_frames, shift(wide_frames[:1], PLANES, -1)),
        axis=0,
    )
    long_cot = jnp.concatenate((wide_cot, shift(wide_cot[:3], PLANES, -1)), axis=0)
    fields = jnp.stack((long_frames, cross(long_frames)))
    cots = jnp.stack((long_cot, cross(long_cot)))

    up_swapped = swap(up_rows)
    up_low = jnp.where(core == 0, up_rows, up_swapped)
    up_high = jnp.where(core == 0, up_swapped, up_rows)
    up_all = jnp.concatenate((up_low, up_high[:, 2 * up_half - up_count :]), axis=1)
    up_taps = up_all.reshape(planes_y, 3, 3, 3, in_channels // LANES, half // planes_y, LANES)
    up_forward = up_taps.transpose(1, 2, 3, 4, 6, 0, 5).reshape(3, 3, 3, in_channels, half)
    up_backward = up_taps.transpose(1, 2, 3, 0, 5, 4, 6).reshape(3, 3, 3, half, in_channels)

    even = convolve(fields, jnp.stack((up_forward[2], up_forward[0])))
    odd = convolve(fields[:, 1 : frame_count + 2], up_forward[1:2])
    odd = jnp.pad(odd, ((0, 0), (0, 1), (0, 0), (0, 0), (0, 0)))
    before = jnp.stack((even, odd), axis=2).reshape(2, -1, *even.shape[2:])[:, :-1]

    columns = lax.axis_size(COLS) * width
    firsts = jnp.stack((2 * xl + core, 2 * (1 - xl) + core)) * width - 1
    place = firsts[:, None] + jnp.arange(width + 2)
    inside = ((place >= 0) & (place < columns))[:, None, None, :, None]

    sigma = jax.nn.sigmoid(before)
    hidden = jnp.where(inside, before * sigma, 0.0)[:, :-1].astype(jnp.bfloat16)

    mix_swapped = swap(mix_rows)
    mix_low = jnp.where(core == 0, mix_rows, mix_swapped)
    mix_high = jnp.where(core == 0, mix_swapped, mix_rows)
    mix_all = jnp.stack((mix_low, mix_high), axis=2)
    mix_taps = mix_all.transpose(1, 0, 2, 3, 4).reshape(3, 3, 3, out_channels, half)

    decoded_parts = convolve(hidden, mix_taps.transpose(0, 1, 2, 4, 3))
    decoded_other = cross(decoded_parts[1].astype(jnp.bfloat16))

    hidden_grad = convolve(cots, mix_taps[::-1, ::-1, ::-1])
    late, sigma = before[:, 2:], sigma[:, 2:]
    slope = sigma * (1.0 + late * (1.0 - sigma))
    before_grad = jnp.where(inside, hidden_grad * slope, 0.0).astype(jnp.bfloat16)
    grad_parts = convolve(before_grad, up_backward[:, ::-1, ::-1], (2, 1, 1))
    grad_other = cross(grad_parts[1].astype(jnp.bfloat16))

    decoded = decoded_parts[0] + decoded_other.astype(jnp.float32)
    frames_grad = grad_parts[0] + grad_other.astype(jnp.float32)
    return decoded.astype(jnp.bfloat16), frames_grad.astype(jnp.bfloat16)


def solution(mesh):
    planes, columns = mesh.devices.shape
    shape = (4, 2, planes // 8, 2, columns // 2)
    fine = Mesh(mesh.devices.reshape(shape), (*PLANES, *COLS))
    placed = P(PLANES, None, COLS, None)
    weights = P(None, PLANES)
    return jax.shard_map(
        shards,
        mesh=fine,
        in_specs=(placed, weights, weights, placed),
        out_specs=(placed, placed),
        check_vma=False,
    )
```

```python
import jax
import jax.numpy as jnp
from jax import lax
from jax.sharding import Mesh, PartitionSpec as P

PLANES = ("y", "xh", "z")
COLS = ("xl", "core")
RING = ("xh", "xl")
LANES = 128


def shift(array, axis, by):
    devices = lax.axis_size(axis)
    pairs = [(i, i + by) for i in range(devices) if 0 <= i + by < devices]
    return lax.ppermute(array, axis, pairs)


def swap(array):
    return lax.ppermute(array, "core", [(0, 1), (1, 0)])


def spread(array, axis):
    count = lax.axis_size(axis)
    return lax.all_to_all(
        jnp.broadcast_to(array, (count, *array.shape)), axis, 0, 0, tiled=True
    )


def convolve(field, kernel, strides=(1, 1, 1)):
    return lax.conv_general_dilated(
        field,
        kernel,
        strides,
        ((0, 0), (1, 1), (0, 0)),
        dimension_numbers=("DHNWC", "DHWIO", "DHNWC"),
        preferred_element_type=jnp.float32,
    )


def with_columns(field):
    width = field.shape[2]
    low = shift(field[:, :, width - 2 :], COLS, 1)
    high = shift(field[:, :, :2], COLS, -1)
    return jnp.concatenate((low, field, high), axis=2)


def tiles_of(kernel):
    return kernel.T.reshape(2, -1, LANES).transpose(1, 0, 2)


def shards(frames, up_kernel, mix_kernel, cotangent):
    frame_count, height, width, in_channels = frames.shape
    out_channels = mix_kernel.shape[0] // 27
    xh, xl, core = lax.axis_index("xh"), lax.axis_index("xl"), lax.axis_index("core")
    ny, nz, nx = lax.axis_size("y"), lax.axis_size("z"), lax.axis_size(RING)
    part = out_channels // nx

    raw_mix = tiles_of(mix_kernel)
    mix_other = lax.ppermute(raw_mix, RING, [(0, 3), (3, 0), (1, 2), (2, 1)])
    wide_frames = with_columns(frames)
    wide_cot = with_columns(cotangent)

    up_column = lax.dynamic_index_in_dim(up_kernel.T, xl, 0, keepdims=False)
    up_tiles = up_column.reshape(-1, LANES)
    up_count = up_tiles.shape[0]
    up_half = (up_count + 1) // 2
    up_part = lax.dynamic_slice_in_dim(up_tiles, core * (up_count - up_half), up_half, 0)
    up_pairs = (up_half + 1) // 2
    up_part = jnp.pad(up_part, ((0, 2 * up_pairs - up_half), (0, 0))).reshape(-1, 2, LANES)

    mix_tiles = jnp.where(xh == core, raw_mix, mix_other).reshape(27, -1, 2, LANES)
    mix_tiles = jnp.pad(mix_tiles, ((0, 1), (0, 0), (0, 0), (0, 0)))
    splits = mix_tiles.shape[1]
    pick_shape = (2, out_channels, 2 * part)
    tap = lax.broadcasted_iota(jnp.int32, pick_shape, 0)
    source = lax.broadcasted_iota(jnp.int32, pick_shape, 1)
    target = lax.broadcasted_iota(jnp.int32, pick_shape, 2)
    place = target % part
    wanted = (place // nz) * (4 * nz) + xh * (2 * nz) + (place % nz) * 2 + xl
    pick = (source == wanted) & (tap == target // part)
    mix_part = jnp.einsum(
        "kptjl,ptlm->kjm",
        mix_tiles.reshape(-1, 2, splits, 2, LANES),
        pick.astype(jnp.bfloat16).reshape(2, splits, LANES, 2 * part),
        preferred_element_type=jnp.float32,
    ).astype(jnp.bfloat16)
    mix_pairs = mix_part.shape[0]

    planes = spread(jnp.concatenate((up_part, mix_part), axis=0), "z")
    up_rows = planes[:, :up_pairs].transpose(1, 2, 0, 3).reshape(-1, LANES)
    mix_rows = planes[:, up_pairs:].transpose(1, 0, 2, 3).reshape(-1, LANES)
    own = spread(jnp.concatenate((up_rows, mix_rows), axis=0), "y")
    swapped = swap(own)
    low = jnp.where(core == 0, own, swapped)
    high = jnp.where(core == 0, swapped, own)
    up_size = up_rows.shape[0]
    up_low = low[:, :up_size].reshape(ny, -1, nz, LANES)[:, :up_half]
    up_high = high[:, :up_size].reshape(ny, -1, nz, LANES)[:, 2 * up_half - up_count : up_half]
    up_all = jnp.concatenate((up_low, up_high), axis=1)
    up_taps = up_all.reshape(ny, 3, 3, 3, in_channels // LANES, nz, LANES)
    up_forward = up_taps.transpose(2, 3, 4, 6, 1, 0, 5).reshape(1, 3, 3, in_channels, 3 * part)
    up_backward = up_taps.transpose(1, 2, 3, 0, 5, 4, 6).reshape(3, 3, 3, part, in_channels)
    mix_all = jnp.stack((low[:, up_size:], high[:, up_size:]), axis=1)
    mix_all = mix_all.reshape(ny, 2, mix_pairs, 2 * nz, 2, part)
    mix_taps = mix_all.transpose(2, 4, 0, 1, 3, 5).reshape(-1, out_channels, part)[:27]
    mix_taps = mix_taps.reshape(3, 3, 3, out_channels, part)
    mix_forward = mix_taps.transpose(0, 1, 2, 4, 3)
    mix_backward = mix_taps[:, ::-1, ::-1].transpose(1, 2, 3, 0, 4)
    mix_backward = mix_backward.reshape(1, 3, 3, out_channels, 3 * part)

    long_frames = jnp.concatenate(
        (shift(wide_frames[-2:], PLANES, 1), wide_frames, shift(wide_frames[:1], PLANES, -1)),
        axis=0,
    )
    long_cot = jnp.concatenate((wide_cot, shift(wide_cot[:3], PLANES, -1)), axis=0)
    fields = spread(long_frames, RING).transpose(1, 2, 0, 3, 4)
    cots = spread(long_cot, RING).transpose(1, 2, 0, 3, 4)

    ups = convolve(fields, up_forward)
    even = ups[1:, ..., :part] + ups[:-1, ..., 2 * part :]
    odd = ups[1:, ..., part : 2 * part]
    before = jnp.stack((even, odd), axis=1).reshape(-1, *even.shape[1:])[:-1]

    columns = lax.axis_size(COLS) * width
    firsts = (2 * (jnp.arange(nx) % 2) + core) * width - 1
    at = firsts[:, None] + jnp.arange(width + 2)
    inside = ((at >= 0) & (at < columns))[None, None, :, :, None]

    sigma = jax.nn.sigmoid(before)
    hidden = jnp.where(inside, before * sigma, 0.0)[:-1].astype(jnp.bfloat16)
    decoded_parts = convolve(hidden, mix_forward).astype(jnp.bfloat16)
    decoded_parts = lax.all_to_all(decoded_parts.transpose(2, 0, 1, 3, 4), RING, 0, 0, tiled=True)

    grads = convolve(cots, mix_backward)
    hidden_grad = (
        grads[2:, ..., :part] + grads[1:-1, ..., part : 2 * part] + grads[:-2, ..., 2 * part :]
    )
    late, sigma = before[2:], sigma[2:]
    slope = sigma * (1.0 + late * (1.0 - sigma))
    before_grad = jnp.where(inside, hidden_grad * slope, 0.0).astype(jnp.bfloat16)
    grad_parts = convolve(before_grad, up_backward[:, ::-1, ::-1], (2, 1, 1)).astype(jnp.bfloat16)
    grad_parts = lax.all_to_all(grad_parts.transpose(2, 0, 1, 3, 4), RING, 0, 0, tiled=True)

    decoded = jnp.sum(decoded_parts.astype(jnp.float32), axis=0)
    frames_grad = jnp.sum(grad_parts.astype(jnp.float32), axis=0)
    return decoded.astype(jnp.bfloat16), frames_grad.astype(jnp.bfloat16)


def solution(mesh):
    planes, columns = mesh.devices.shape
    shape = (4, 2, planes // 8, 2, columns // 2)
    fine = Mesh(mesh.devices.reshape(shape), (*PLANES, *COLS))
    placed = P(PLANES, None, COLS, None)
    weights = P(None, PLANES)
    return jax.shard_map(
        shards,
        mesh=fine,
        in_specs=(placed, weights, weights, placed),
        out_specs=(placed, placed),
        check_vma=False,
    )
```

```python
import functools

import jax
import jax.numpy as jnp
from jax import lax
from jax.experimental import pallas as pl
from jax.experimental.pallas import tpu as pltpu
from jax.sharding import Mesh, PartitionSpec as P

PLANES = ("y", "xh", "z")
COLS = ("xl", "core")
RING = ("xh", "xl")
LANES = 128
PAD = 32


def shift(array, axis, by):
    devices = lax.axis_size(axis)
    pairs = [(i, i + by) for i in range(devices) if 0 <= i + by < devices]
    return lax.ppermute(array, axis, pairs)


def swap(array):
    return lax.ppermute(array, "core", [(0, 1), (1, 0)])


def spread(array, axis):
    count = lax.axis_size(axis)
    return lax.all_to_all(
        jnp.broadcast_to(array, (count, *array.shape)), axis, 0, 0, tiled=True
    )


def later(rows, by):
    if by == 0:
        return rows
    return pltpu.roll(rows, rows.shape[0] - by, 0)


def call(kernel, outs, scratch, flops, *operands):
    space = pl.BlockSpec(memory_space=pltpu.VMEM)
    return pl.pallas_call(
        kernel,
        out_shape=outs,
        in_specs=[space] * len(operands),
        out_specs=jax.tree.map(lambda _: space, outs),
        scratch_shapes=scratch,
        compiler_params=pltpu.CompilerParams(vmem_limit_bytes=48 * 2**20),
        cost_estimate=pl.CostEstimate(flops=flops, bytes_accessed=8 * 2**20, transcendentals=0),
    )(*operands)


def unfold_kernel(sizes, inputs, frame_rows, cot_rows):
    blocks, base = inputs.shape[0], 0
    for out, (times, splits) in zip((frame_rows, cot_rows), sizes, strict=True):

        def step(at, _, out=out, splits=splits, base=base):
            time, block = at // blocks, at % blocks
            target = pl.ds(pl.multiple_of(at * PAD, PAD), PAD)
            for row in range(2):
                for split in range(splits):
                    first = base + ((time * 2 + row) * splits + split) * PAD
                    source = pl.ds(pl.multiple_of(first, PAD), PAD)
                    chunk = inputs[block, source, :].astype(jnp.float32)
                    for tap in range(3):
                        lane = ((row * 3 + tap) * splits + split) * LANES
                        moved = later(chunk, tap).astype(jnp.bfloat16)
                        out[target, lane : lane + LANES] = moved
            return 0

        lax.fori_loop(0, times * blocks, step, 0)
        base += times * 2 * splits * PAD


def readers(layout, first, own, other):
    nz, up_half, up_count, up_size = layout
    lead = first[0] == 0

    def low(start, count):
        rows = slice(start, start + count)
        return jnp.where(lead, own[:, rows], other[:, rows])

    def high(start, count):
        rows = slice(start, start + count)
        return jnp.where(lead, other[:, rows], own[:, rows])

    def up_tile(kt, kh, kw, split, splits):
        tile = ((kt * 3 + kh) * 3 + kw) * splits + split
        if tile < up_half:
            value = low(tile * nz, nz)
        else:
            value = high((tile - (up_count - up_half)) * nz, nz)
        return value.reshape(-1, LANES)

    def mix_tile(kt, kw, pair):
        start = up_size + ((kt * 3 + kw) * 2 + pair) * 2 * nz
        return jnp.stack((low(start, 2 * nz), high(start, 2 * nz)), axis=1).reshape(-1, LANES)

    return up_tile, mix_tile


def forward_kernel(
    layout, first, rows, own, other, mask, decoded, slope, up_w, ups, hidden, mix_w, total
):
    up_tile, mix_tile = readers(layout, first, own, other)
    splits = rows.shape[1] // (6 * LANES)
    part, unit = up_w.shape[0] // 6, mask.shape[0]
    for kt in range(3):
        for out_row in range(2):
            for row in range(2):
                for kw in range(3):
                    for split in range(splits):
                        at = kt * 2 * part + out_row * part
                        lane = ((row * 3 + kw) * splits + split) * LANES
                        up_w[at : at + part, lane : lane + LANES] = up_tile(
                            kt, row - out_row + 1, kw, split, splits
                        )
    step = 2 * LANES
    ups[...] = jnp.zeros_like(ups)

    def product(k, _):
        lanes = pl.ds(pl.multiple_of(k * step, step), step)
        ups[...] += lax.dot_general(
            rows[:, lanes],
            up_w[:, lanes],
            (((1,), (1,)), ((), ())),
            preferred_element_type=jnp.float32,
        )
        return 0

    lax.fori_loop(0, rows.shape[1] // step, product, 0)
    inside = mask[...] > 0
    times = 2 * (rows.shape[0] // unit - 1) - 1
    for time in range(times):
        at = time // 2 * unit
        if time % 2 == 0:
            before = ups[at + unit : at + 2 * unit, :LANES] + ups[at : at + unit, 2 * LANES :]
        else:
            before = ups[at + unit : at + 2 * unit, LANES : 2 * LANES]
        sigma = jax.nn.sigmoid(before)
        if time < times - 1:
            value = jnp.where(inside, before * sigma, 0.0)
            for kw in range(3):
                hidden[time * unit : (time + 1) * unit, kw * LANES : (kw + 1) * LANES] = later(
                    value, kw
                ).astype(jnp.bfloat16)
        if time >= 2:
            slope[(time - 2) * unit : (time - 1) * unit, :] = jnp.where(
                inside, sigma * (1.0 + before * (1.0 - sigma)), 0.0
            )
    channels = mix_w.shape[0] // 2
    for kt in range(3):
        for out_row in range(2):
            for kw in range(3):
                mix_w[
                    out_row * channels : (out_row + 1) * channels,
                    (kt * 3 + kw) * LANES : (kt * 3 + kw + 1) * LANES,
                ] = mix_tile(kt, kw, out_row)
    total[...] = jnp.zeros_like(total)
    for kt in range(3):
        total[...] += lax.dot_general(
            hidden[kt * unit : kt * unit + total.shape[0], :],
            mix_w[:, kt * 3 * LANES : (kt + 1) * 3 * LANES],
            (((1,), (1,)), ((), ())),
            preferred_element_type=jnp.float32,
        )
    store(decoded, total, channels)


def store(out, total, channels):
    blocks, times, _, width, _ = out.shape
    for block in range(blocks):
        for time in range(times):
            at = (time * blocks + block) * PAD
            for out_row in range(2):
                lanes = slice(out_row * channels, (out_row + 1) * channels)
                value = total[at : at + PAD, lanes].astype(jnp.bfloat16)
                out[block, time, out_row] = value[:width]


def backward_kernel(
    layout, first, rows, own, other, slope, grads, mix_w, partial, evens, odds, up_w, total
):
    up_tile, mix_tile = readers(layout, first, own, other)
    channels = rows.shape[1] // 6
    unit = evens.shape[0] - total.shape[0]
    splits = up_w.shape[1] // (2 * LANES)
    part = LANES // 2
    for kt in range(3):
        for row in range(2):
            for shift_w in range(3):
                at = (row * 3 + shift_w) * channels
                mix_w[at : at + channels, kt * LANES : (kt + 1) * LANES] = mix_tile(
                    kt, 2 - shift_w, row
                )
    step = 2 * LANES
    partial[...] = jnp.zeros_like(partial)

    def product(k, _):
        lanes = pl.ds(pl.multiple_of(k * step, step), step)
        partial[...] += jnp.dot(
            rows[:, lanes], mix_w[lanes, :], preferred_element_type=jnp.float32
        )
        return 0

    lax.fori_loop(0, rows.shape[1] // step, product, 0)
    times = rows.shape[0] // unit - 2
    for time in range(times):
        at = time * unit
        hidden_grad = (
            partial[at + 2 * unit : at + 3 * unit, :LANES]
            + partial[at + unit : at + 2 * unit, LANES : 2 * LANES]
            + partial[at : at + unit, 2 * LANES :]
        )
        value = hidden_grad * slope[at : at + unit, :]
        target = evens if time % 2 == 0 else odds
        place = time // 2 * unit
        for shift_w in range(3):
            target[place : place + unit, shift_w * LANES : (shift_w + 1) * LANES] = later(
                value, shift_w
            ).astype(jnp.bfloat16)
    for kt in range(3):
        for shift_w in range(3):
            for row in range(2):
                for out_row in range(2):
                    for split in range(splits):
                        at = (kt * 3 + shift_w) * LANES + row * part
                        lane = (out_row * splits + split) * LANES
                        up_w[at : at + part, lane : lane + LANES] = up_tile(
                            kt, out_row + 1 - row, 2 - shift_w, split, splits
                        )
    count = total.shape[0]
    lhs = (evens[:count, :], odds[:count, :], evens[unit : unit + count, :])
    total[...] = jnp.zeros_like(total)
    for kt in range(3):
        total[...] += jnp.dot(
            lhs[kt],
            up_w[kt * 3 * LANES : (kt + 1) * 3 * LANES, :],
            preferred_element_type=jnp.float32,
        )
    store(grads, total, splits * LANES)


def unfold(inputs, frame_times, cot_times, frame_splits, cot_splits):
    unit = inputs.shape[0] * PAD
    sizes = ((frame_times, frame_splits), (cot_times, cot_splits))
    outs = tuple(
        jax.ShapeDtypeStruct((times * unit, 6 * splits * LANES), jnp.bfloat16)
        for times, splits in sizes
    )
    return call(functools.partial(unfold_kernel, sizes), outs, [], 10**6, inputs)


def forward(layout, first, rows, own, other, mask, width, channels):
    blocks = mask.shape[0] // PAD
    unit = mask.shape[0]
    times = 2 * (rows.shape[0] // unit - 3)
    outs = (
        jax.ShapeDtypeStruct((blocks, times, 2, width, channels), jnp.bfloat16),
        jax.ShapeDtypeStruct(((times + 1) * unit, LANES), jnp.float32),
    )
    scratch = [
        pltpu.VMEM((3 * LANES, rows.shape[1]), jnp.bfloat16),
        pltpu.VMEM((rows.shape[0], 3 * LANES), jnp.float32),
        pltpu.VMEM(((times + 2) * unit, 3 * LANES), jnp.bfloat16),
        pltpu.VMEM((2 * channels, 9 * LANES), jnp.bfloat16),
        pltpu.VMEM((times * unit, 2 * channels), jnp.float32),
    ]
    kernel = functools.partial(forward_kernel, layout)
    return call_scalar(kernel, outs, scratch, 2 * 10**9, first, rows, own, other, mask)


def backward(layout, first, rows, own, other, slope, unit, width, in_channels):
    times = slope.shape[0] // unit
    out = jax.ShapeDtypeStruct((unit // PAD, times // 2, 2, width, in_channels), jnp.bfloat16)
    scratch = [
        pltpu.VMEM((rows.shape[1], 3 * LANES), jnp.bfloat16),
        pltpu.VMEM((rows.shape[0], 3 * LANES), jnp.float32),
        pltpu.VMEM(((times + 1) // 2 * unit, 3 * LANES), jnp.bfloat16),
        pltpu.VMEM((times // 2 * unit, 3 * LANES), jnp.bfloat16),
        pltpu.VMEM((9 * LANES, 2 * in_channels), jnp.bfloat16),
        pltpu.VMEM((times // 2 * unit, 2 * in_channels), jnp.float32),
    ]
    kernel = functools.partial(backward_kernel, layout)
    return call_scalar(kernel, out, scratch, 2 * 10**9, first, rows, own, other, slope)


def call_scalar(kernel, outs, scratch, flops, first, *operands):
    space = pl.BlockSpec(memory_space=pltpu.VMEM)
    return pl.pallas_call(
        kernel,
        out_shape=outs,
        in_specs=[pl.BlockSpec(memory_space=pltpu.SMEM)] + [space] * len(operands),
        out_specs=jax.tree.map(lambda _: space, outs),
        scratch_shapes=scratch,
        compiler_params=pltpu.CompilerParams(vmem_limit_bytes=48 * 2**20),
        cost_estimate=pl.CostEstimate(flops=flops, bytes_accessed=8 * 2**20, transcendentals=0),
    )(first, *operands)


def with_columns(field):
    width = field.shape[2]
    low = shift(field[:, :, width - 2 :], COLS, 1)
    high = shift(field[:, :, :2], COLS, -1)
    return jnp.concatenate((low, field, high), axis=2)


def flat(field):
    padded = jnp.pad(field, ((0, 0), (0, 0), (0, PAD - field.shape[2]), (0, 0)))
    tiles = padded.reshape(*padded.shape[:3], -1, LANES)
    return tiles.transpose(0, 1, 3, 2, 4).reshape(-1, LANES)


def tiles_of(kernel):
    return kernel.T.reshape(2, -1, LANES).transpose(1, 0, 2)


def shards(frames, up_kernel, mix_kernel, cotangent):
    frame_count, height, width, in_channels = frames.shape
    out_channels = mix_kernel.shape[0] // 27
    xh, xl, core = lax.axis_index("xh"), lax.axis_index("xl"), lax.axis_index("core")
    ny, nz, nx = lax.axis_size("y"), lax.axis_size("z"), lax.axis_size(RING)
    part = out_channels // nx

    raw_mix = tiles_of(mix_kernel)
    mix_other = lax.ppermute(raw_mix, RING, [(0, 3), (3, 0), (1, 2), (2, 1)])
    up_column = lax.dynamic_index_in_dim(up_kernel.T, xl, 0, keepdims=False)
    up_tiles = up_column.reshape(-1, LANES)
    up_count = up_tiles.shape[0]
    up_half = (up_count + 1) // 2
    up_part = lax.dynamic_slice_in_dim(up_tiles, core * (up_count - up_half), up_half, 0)
    up_pairs = (up_half + 1) // 2
    up_part = jnp.pad(up_part, ((0, 2 * up_pairs - up_half), (0, 0))).reshape(-1, 2, LANES)

    mix_tiles = jnp.where(xh == core, raw_mix, mix_other)
    splits = out_channels // LANES
    pick_shape = (3, out_channels, 4 * part)
    tap = lax.broadcasted_iota(jnp.int32, pick_shape, 0)
    source = lax.broadcasted_iota(jnp.int32, pick_shape, 1)
    target = lax.broadcasted_iota(jnp.int32, pick_shape, 2)
    pair, side, place = target // (2 * part), target // part % 2, target % part
    wanted = (place // nz) * (4 * nz) + xh * (2 * nz) + (place % nz) * 2 + xl
    pick = (source == wanted) & (tap == side + 1 - pair)
    mix_part = jnp.einsum(
        "thwsjl,hslm->twjm",
        mix_tiles.reshape(3, 3, 3, splits, 2, LANES),
        pick.astype(jnp.bfloat16).reshape(3, splits, LANES, 4 * part),
        preferred_element_type=jnp.float32,
    ).astype(jnp.bfloat16)
    mix_part = mix_part.reshape(9, 2, 2, 2 * part).transpose(0, 2, 1, 3).reshape(-1, 2, LANES)

    planes = spread(jnp.concatenate((up_part, mix_part), axis=0), "z")
    wide_frames, wide_cot = with_columns(frames), with_columns(cotangent)
    fields = jnp.concatenate(
        (shift(wide_frames[-2:], PLANES, 1), wide_frames, shift(wide_frames[:1], PLANES, -1)),
        axis=0,
    )
    cots = jnp.concatenate((wide_cot, shift(wide_cot[:3], PLANES, -1)), axis=0)
    planes, fields, cots = lax.optimization_barrier((planes, fields, cots))
    inputs = jnp.concatenate((flat(fields), flat(cots)), axis=0)
    inputs = lax.all_gather(inputs, RING, axis=0)

    up_rows = planes[:, :up_pairs].transpose(1, 2, 0, 3).reshape(-1, LANES)
    mix_rows = planes[:, up_pairs:].transpose(1, 0, 2, 3).reshape(-1, LANES)
    own = spread(jnp.concatenate((up_rows, mix_rows), axis=0), "y")
    other = swap(own)
    layout = (nz, up_half, up_count, up_rows.shape[0])

    frame_rows, cot_rows = unfold(
        inputs, fields.shape[0], cots.shape[0], in_channels // LANES, splits
    )
    columns = lax.axis_size(COLS) * width
    firsts = (2 * (jnp.arange(nx) % 2) + core) * width - 1
    at = firsts[:, None] + jnp.arange(PAD)
    inside = ((at >= 0) & (at < columns)).astype(jnp.float32).reshape(-1, 1)
    mask = jnp.broadcast_to(inside, (nx * PAD, LANES))
    first = core.reshape(1)

    decoded_parts, slope = forward(
        layout, first, frame_rows, own, other, mask, width, out_channels
    )
    decoded_parts = lax.all_to_all(decoded_parts, RING, 0, 0, tiled=True)
    grad_parts = backward(
        layout, first, cot_rows, own, other, slope, nx * PAD, width, in_channels
    )
    grad_parts = lax.all_to_all(grad_parts, RING, 0, 0, tiled=True)
    decoded = jnp.sum(decoded_parts.astype(jnp.float32), axis=0)
    frames_grad = jnp.sum(grad_parts.astype(jnp.float32), axis=0)
    return decoded.astype(jnp.bfloat16), frames_grad.astype(jnp.bfloat16)


def solution(mesh):
    planes, columns = mesh.devices.shape
    shape = (4, 2, planes // 8, 2, columns // 2)
    fine = Mesh(mesh.devices.reshape(shape), (*PLANES, *COLS))
    placed = P(PLANES, None, COLS, None)
    weights = P(None, PLANES)
    return jax.shard_map(
        shards,
        mesh=fine,
        in_specs=(placed, weights, weights, placed),
        out_specs=(placed, placed),
        check_vma=False,
    )
```

```python
import functools

import jax
import jax.numpy as jnp
from jax import lax
from jax.experimental import pallas as pl
from jax.experimental.pallas import tpu as pltpu
from jax.sharding import Mesh, PartitionSpec as P

PLANES = ("y", "xh", "z")
COLS = ("xl", "core")
RING = ("xh", "xl")
LANES = 128
PAD = 32
OFFSETS = (0, 3, 1, 2)


def shift(array, axis, by):
    devices = lax.axis_size(axis)
    pairs = [(i, i + by) for i in range(devices) if 0 <= i + by < devices]
    return lax.ppermute(array, axis, pairs)


def swap(array):
    return lax.ppermute(array, "core", [(0, 1), (1, 0)])


def spread(array, axis):
    count = lax.axis_size(axis)
    return lax.all_to_all(
        jnp.broadcast_to(array, (count, *array.shape)), axis, 0, 0, tiled=True
    )


def later(rows, by):
    if by == 0:
        return rows
    return pltpu.roll(rows, rows.shape[0] - by, 0)


def unfold_kernel(sizes, place, own, other, frame_rows, cot_rows):
    _, xl, core = place[0], place[1], place[2]
    blocks, base = own.shape[0], 0
    for out, (times, splits, width) in zip((frame_rows, cot_rows), sizes, strict=True):

        def step(at, _, out=out, splits=splits, width=width, base=base):
            time, block = at // blocks, at % blocks
            side = (xl + (block + 1) // 2) % 2
            partner = jnp.where(xl == 0, (block + 2) % 4, block + 1 - 2 * (block % 2))
            left = jnp.where(core == 1, block, partner)
            right = jnp.where(core == 0, block, partner)
            has_left = 2 * side + core > 0
            has_right = 2 * side + core < 3
            target = pl.ds(pl.multiple_of(at * PAD, PAD), PAD)
            for row in range(2):
                for split in range(splits):
                    first = base + ((time * 2 + row) * splits + split) * width
                    rows = pl.ds(pl.multiple_of(first, 8), width)
                    head = pl.ds(pl.multiple_of(first, 8), 8)
                    tail = pl.ds(pl.multiple_of(first + width - 8, 8), 8)
                    low = other[left, tail, :].astype(jnp.float32)
                    middle = own[block, rows, :].astype(jnp.float32)
                    high = other[right, head, :].astype(jnp.float32)
                    low = jnp.where(has_left, low, 0.0)
                    high = jnp.where(has_right, high, 0.0)
                    chunk = jnp.concatenate((low, middle, high), axis=0)
                    for tap in range(3):
                        lane = ((row * 3 + tap) * splits + split) * LANES
                        moved = chunk[6 + tap : 6 + tap + PAD].astype(jnp.bfloat16)
                        out[target, lane : lane + LANES] = moved
            return 0

        lax.fori_loop(0, times * blocks, step, 0)
        base += times * 2 * splits * width


def readers(layout, place, own, other):
    nz, up_half, up_count, up_size = layout
    lead = place[2] == 0

    def low(start, count):
        rows = slice(start, start + count)
        return jnp.where(lead, own[:, rows], other[:, rows])

    def high(start, count):
        rows = slice(start, start + count)
        return jnp.where(lead, other[:, rows], own[:, rows])

    def up_tile(kt, kh, kw, split, splits):
        tile = ((kt * 3 + kh) * 3 + kw) * splits + split
        if tile < up_half:
            value = low(tile * nz, nz)
        else:
            value = high((tile - (up_count - up_half)) * nz, nz)
        return value.reshape(-1, LANES)

    def mix_tile(kt, kw, pair):
        start = up_size + ((kt * 3 + kw) * 2 + pair) * 2 * nz
        return jnp.stack((low(start, 2 * nz), high(start, 2 * nz)), axis=1).reshape(-1, LANES)

    return up_tile, mix_tile


def forward_kernel(
    layout, place, rows, own, other, decoded, slope, up_w, ups, mask, hidden, mix_w, total
):
    up_tile, mix_tile = readers(layout, place, own, other)
    splits = rows.shape[1] // (6 * LANES)
    part, unit = up_w.shape[0] // 6, mask.shape[0]
    width = decoded.shape[3]
    column = lax.broadcasted_iota(jnp.int32, (PAD, LANES), 0) - 1
    for block in range(decoded.shape[0]):
        side = (place[1] + (block + 1) // 2) % 2
        at = (2 * side + place[2]) * width + column
        inside = (at >= 0) & (at < 4 * width)
        mask[block * PAD : (block + 1) * PAD, :] = inside.astype(jnp.float32)
    for kt in range(3):
        for out_row in range(2):
            for row in range(2):
                for kw in range(3):
                    for split in range(splits):
                        at = kt * 2 * part + out_row * part
                        lane = ((row * 3 + kw) * splits + split) * LANES
                        up_w[at : at + part, lane : lane + LANES] = up_tile(
                            kt, row - out_row + 1, kw, split, splits
                        )
    step = 2 * LANES
    ups[...] = jnp.zeros_like(ups)

    def product(k, _):
        lanes = pl.ds(pl.multiple_of(k * step, step), step)
        ups[...] += lax.dot_general(
            rows[:, lanes],
            up_w[:, lanes],
            (((1,), (1,)), ((), ())),
            preferred_element_type=jnp.float32,
        )
        return 0

    lax.fori_loop(0, rows.shape[1] // step, product, 0)
    inside = mask[...] > 0
    times = 2 * (rows.shape[0] // unit - 1) - 1
    for time in range(times):
        at = time // 2 * unit
        if time % 2 == 0:
            before = ups[at + unit : at + 2 * unit, :LANES] + ups[at : at + unit, 2 * LANES :]
        else:
            before = ups[at + unit : at + 2 * unit, LANES : 2 * LANES]
        sigma = jax.nn.sigmoid(before)
        if time < times - 1:
            value = jnp.where(inside, before * sigma, 0.0)
            for kw in range(3):
                hidden[time * unit : (time + 1) * unit, kw * LANES : (kw + 1) * LANES] = later(
                    value, kw
                ).astype(jnp.bfloat16)
        if time >= 2:
            slope[(time - 2) * unit : (time - 1) * unit, :] = jnp.where(
                inside, sigma * (1.0 + before * (1.0 - sigma)), 0.0
            )
    channels = mix_w.shape[0] // 2
    for kt in range(3):
        for out_row in range(2):
            for kw in range(3):
                mix_w[
                    out_row * channels : (out_row + 1) * channels,
                    (kt * 3 + kw) * LANES : (kt * 3 + kw + 1) * LANES,
                ] = mix_tile(kt, kw, out_row)
    total[...] = jnp.zeros_like(total)
    for kt in range(3):
        total[...] += lax.dot_general(
            hidden[kt * unit : kt * unit + total.shape[0], :],
            mix_w[:, kt * 3 * LANES : (kt + 1) * 3 * LANES],
            (((1,), (1,)), ((), ())),
            preferred_element_type=jnp.float32,
        )
    store(place, decoded, total, channels)


def store(place, out, total, channels):
    blocks, times, _, width, _ = out.shape
    for block in range(blocks):
        member = (2 * place[0] + place[1] + OFFSETS[block]) % 4
        for time in range(times):
            at = (time * blocks + block) * PAD
            for out_row in range(2):
                lanes = slice(out_row * channels, (out_row + 1) * channels)
                value = total[at : at + PAD, lanes].astype(jnp.bfloat16)
                out[member, time, out_row] = value[:width]


def backward_kernel(
    layout, place, rows, own, other, slope, grads, mix_w, partial, evens, odds, up_w, total
):
    up_tile, mix_tile = readers(layout, place, own, other)
    channels = rows.shape[1] // 6
    unit = evens.shape[0] - total.shape[0]
    splits = up_w.shape[1] // (2 * LANES)
    part = LANES // 2
    for kt in range(3):
        for row in range(2):
            for shift_w in range(3):
                at = (row * 3 + shift_w) * channels
                mix_w[at : at + channels, kt * LANES : (kt + 1) * LANES] = mix_tile(
                    kt, 2 - shift_w, row
                )
    step = 2 * LANES
    partial[...] = jnp.zeros_like(partial)

    def product(k, _):
        lanes = pl.ds(pl.multiple_of(k * step, step), step)
        partial[...] += jnp.dot(
            rows[:, lanes], mix_w[lanes, :], preferred_element_type=jnp.float32
        )
        return 0

    lax.fori_loop(0, rows.shape[1] // step, product, 0)
    times = rows.shape[0] // unit - 2
    for time in range(times):
        at = time * unit
        hidden_grad = (
            partial[at + 2 * unit : at + 3 * unit, :LANES]
            + partial[at + unit : at + 2 * unit, LANES : 2 * LANES]
            + partial[at : at + unit, 2 * LANES :]
        )
        value = hidden_grad * slope[at : at + unit, :]
        target = evens if time % 2 == 0 else odds
        spot = time // 2 * unit
        for shift_w in range(3):
            target[spot : spot + unit, shift_w * LANES : (shift_w + 1) * LANES] = later(
                value, shift_w
            ).astype(jnp.bfloat16)
    for kt in range(3):
        for shift_w in range(3):
            for row in range(2):
                for out_row in range(2):
                    for split in range(splits):
                        at = (kt * 3 + shift_w) * LANES + row * part
                        lane = (out_row * splits + split) * LANES
                        up_w[at : at + part, lane : lane + LANES] = up_tile(
                            kt, out_row + 1 - row, 2 - shift_w, split, splits
                        )
    count = total.shape[0]
    lhs = (evens[:count, :], odds[:count, :], evens[unit : unit + count, :])
    total[...] = jnp.zeros_like(total)
    for kt in range(3):
        total[...] += jnp.dot(
            lhs[kt],
            up_w[kt * 3 * LANES : (kt + 1) * 3 * LANES, :],
            preferred_element_type=jnp.float32,
        )
    store(place, grads, total, splits * LANES)


def call(kernel, outs, scratch, flops, megabytes, place, *operands):
    space = pl.BlockSpec(memory_space=pltpu.VMEM)
    return pl.pallas_call(
        kernel,
        out_shape=outs,
        in_specs=[pl.BlockSpec(memory_space=pltpu.SMEM)] + [space] * len(operands),
        out_specs=jax.tree.map(lambda _: space, outs),
        scratch_shapes=scratch,
        compiler_params=pltpu.CompilerParams(vmem_limit_bytes=megabytes * 2**20),
        cost_estimate=pl.CostEstimate(flops=flops, bytes_accessed=8 * 2**20, transcendentals=0),
    )(place, *operands)


def unfold(place, own, other, sizes):
    unit = own.shape[0] * PAD
    outs = tuple(
        jax.ShapeDtypeStruct((times * unit, 6 * splits * LANES), jnp.bfloat16)
        for times, splits, _ in sizes
    )
    return call(functools.partial(unfold_kernel, sizes), outs, [], 10**9, 14, place, own, other)


def forward(layout, place, rows, own, other, width, channels):
    blocks = own.shape[0]
    unit = blocks * PAD
    times = 2 * (rows.shape[0] // unit - 3)
    outs = (
        jax.ShapeDtypeStruct((blocks, times, 2, width, channels), jnp.bfloat16),
        jax.ShapeDtypeStruct(((times + 1) * unit, LANES), jnp.float32),
    )
    scratch = [
        pltpu.VMEM((3 * LANES, rows.shape[1]), jnp.bfloat16),
        pltpu.VMEM((rows.shape[0], 3 * LANES), jnp.float32),
        pltpu.VMEM((unit, LANES), jnp.float32),
        pltpu.VMEM(((times + 2) * unit, 3 * LANES), jnp.bfloat16),
        pltpu.VMEM((2 * channels, 9 * LANES), jnp.bfloat16),
        pltpu.VMEM((times * unit, 2 * channels), jnp.float32),
    ]
    kernel = functools.partial(forward_kernel, layout)
    return call(kernel, outs, scratch, 2 * 10**9, 14, place, rows, own, other)


def backward(layout, place, rows, own, other, slope, unit, width, in_channels):
    times = slope.shape[0] // unit
    out = jax.ShapeDtypeStruct((unit // PAD, times // 2, 2, width, in_channels), jnp.bfloat16)
    scratch = [
        pltpu.VMEM((rows.shape[1], 3 * LANES), jnp.bfloat16),
        pltpu.VMEM((rows.shape[0], 3 * LANES), jnp.float32),
        pltpu.VMEM(((times + 1) // 2 * unit, 3 * LANES), jnp.bfloat16),
        pltpu.VMEM((times // 2 * unit, 3 * LANES), jnp.bfloat16),
        pltpu.VMEM((9 * LANES, 2 * in_channels), jnp.bfloat16),
        pltpu.VMEM((times // 2 * unit, 2 * in_channels), jnp.float32),
    ]
    kernel = functools.partial(backward_kernel, layout)
    return call(kernel, out, scratch, 2 * 10**9, 14, place, rows, own, other, slope)


def ring(array, by):
    return lax.ppermute(array, RING, [(i, (i + by) % 4) for i in range(4)])


def flat(field):
    tiles = field.reshape(*field.shape[:3], -1, LANES)
    return tiles.transpose(0, 1, 3, 2, 4).reshape(-1, LANES)


def tiles_of(kernel):
    return kernel.T.reshape(2, -1, LANES).transpose(1, 0, 2)


def shards(frames, up_kernel, mix_kernel, cotangent):
    frame_count, height, width, in_channels = frames.shape
    out_channels = mix_kernel.shape[0] // 27
    xh, xl, core = lax.axis_index("xh"), lax.axis_index("xl"), lax.axis_index("core")
    ny, nz, nx = lax.axis_size("y"), lax.axis_size("z"), lax.axis_size(RING)
    part = out_channels // nx

    raw_mix = tiles_of(mix_kernel)
    mix_other = lax.ppermute(raw_mix, RING, [(0, 3), (3, 0), (1, 2), (2, 1)])
    up_column = lax.dynamic_index_in_dim(up_kernel.T, xl, 0, keepdims=False)
    up_tiles = up_column.reshape(-1, LANES)
    up_count = up_tiles.shape[0]
    up_half = (up_count + 1) // 2
    up_part = lax.dynamic_slice_in_dim(up_tiles, core * (up_count - up_half), up_half, 0)
    up_pairs = (up_half + 1) // 2
    up_part = jnp.pad(up_part, ((0, 2 * up_pairs - up_half), (0, 0))).reshape(-1, 2, LANES)

    mix_tiles = jnp.where(xh == core, raw_mix, mix_other)
    splits = out_channels // LANES
    pick_shape = (3, out_channels, 4 * part)
    tap = lax.broadcasted_iota(jnp.int32, pick_shape, 0)
    source = lax.broadcasted_iota(jnp.int32, pick_shape, 1)
    target = lax.broadcasted_iota(jnp.int32, pick_shape, 2)
    pair, side, place = target // (2 * part), target // part % 2, target % part
    wanted = (place // nz) * (4 * nz) + xh * (2 * nz) + (place % nz) * 2 + xl
    pick = (source == wanted) & (tap == side + 1 - pair)
    mix_part = jnp.einsum(
        "thwsjl,hslm->twjm",
        mix_tiles.reshape(3, 3, 3, splits, 2, LANES),
        pick.astype(jnp.bfloat16).reshape(3, splits, LANES, 4 * part),
        preferred_element_type=jnp.float32,
    ).astype(jnp.bfloat16)
    mix_part = mix_part.reshape(9, 2, 2, 2 * part).transpose(0, 2, 1, 3).reshape(-1, 2, LANES)

    planes = spread(jnp.concatenate((up_part, mix_part), axis=0), "z")
    fields = jnp.concatenate(
        (shift(frames[-2:], PLANES, 1), frames, shift(frames[:1], PLANES, -1)), axis=0
    )
    cots = jnp.concatenate((cotangent, shift(cotangent[:3], PLANES, -1)), axis=0)
    block = jnp.concatenate((flat(fields), flat(cots)), axis=0)
    blocks = (block, ring(block, 1), ring(block, -1), ring(block, 2))
    planes, block = lax.optimization_barrier((planes, block))
    blocks = jnp.stack(blocks)
    others = swap(blocks)

    up_rows = planes[:, :up_pairs].transpose(1, 2, 0, 3).reshape(-1, LANES)
    mix_rows = planes[:, up_pairs:].transpose(1, 0, 2, 3).reshape(-1, LANES)
    own = spread(jnp.concatenate((up_rows, mix_rows), axis=0), "y")
    other = swap(own)
    layout = (nz, up_half, up_count, up_rows.shape[0])

    place = jnp.stack((xh, xl, core))
    sizes = (
        (fields.shape[0], in_channels // LANES, width),
        (cots.shape[0], splits, width),
    )
    frame_rows, cot_rows = unfold(place, blocks, others, sizes)
    decoded_parts, slope = forward(layout, place, frame_rows, own, other, width, out_channels)
    decoded_parts = lax.all_to_all(decoded_parts, RING, 0, 0, tiled=True)
    grad_parts = backward(
        layout, place, cot_rows, own, other, slope, nx * PAD, width, in_channels
    )
    decoded_parts, grad_parts = lax.optimization_barrier((decoded_parts, grad_parts))
    grad_parts = lax.all_to_all(grad_parts, RING, 0, 0, tiled=True)
    decoded = jnp.sum(decoded_parts.astype(jnp.float32), axis=0)
    frames_grad = jnp.sum(grad_parts.astype(jnp.float32), axis=0)
    return decoded.astype(jnp.bfloat16), frames_grad.astype(jnp.bfloat16)


def solution(mesh):
    planes, columns = mesh.devices.shape
    shape = (4, 2, planes // 8, 2, columns // 2)
    fine = Mesh(mesh.devices.reshape(shape), (*PLANES, *COLS))
    placed = P(PLANES, None, COLS, None)
    weights = P(None, PLANES)
    return jax.shard_map(
        shards,
        mesh=fine,
        in_specs=(placed, weights, weights, placed),
        out_specs=(placed, placed),
        check_vma=False,
    )
```

```python
import functools

import jax
import jax.numpy as jnp
from jax import lax
from jax.experimental import pallas as pl
from jax.experimental.pallas import tpu as pltpu
from jax.sharding import Mesh, PartitionSpec as P

PLANES = ("y", "xh", "z")
COLS = ("xl", "core")
RING = ("xh", "xl")
LANES = 128
PAD = 32
OFFSETS = (0, 3, 1, 2)


def shift(array, axis, by):
    devices = lax.axis_size(axis)
    pairs = [(i, i + by) for i in range(devices) if 0 <= i + by < devices]
    return lax.ppermute(array, axis, pairs)


def swap(array):
    return lax.ppermute(array, "core", [(0, 1), (1, 0)])


def spread(array, axis):
    count = lax.axis_size(axis)
    return lax.all_to_all(
        jnp.broadcast_to(array, (count, *array.shape)), axis, 0, 0, tiled=True
    )


def later(rows, by):
    if by == 0:
        return rows
    return pltpu.roll(rows, rows.shape[0] - by, 0)


def unfold_kernel(sizes, place, own, other, frame_rows, cot_rows):
    _, xl, core = place[0], place[1], place[2]
    blocks, base = own.shape[0], 0
    for out, (times, splits, width) in zip((frame_rows, cot_rows), sizes, strict=True):

        def step(at, _, out=out, splits=splits, width=width, base=base):
            time, block = at // blocks, at % blocks
            side = (xl + (block + 1) // 2) % 2
            partner = jnp.where(xl == 0, (block + 2) % 4, block + 1 - 2 * (block % 2))
            left = jnp.where(core == 1, block, partner)
            right = jnp.where(core == 0, block, partner)
            has_left = 2 * side + core > 0
            has_right = 2 * side + core < 3
            target = pl.ds(pl.multiple_of(at * PAD, PAD), PAD)
            for row in range(2):
                for split in range(splits):
                    first = base + ((time * 2 + row) * splits + split) * width
                    rows = pl.ds(pl.multiple_of(first, 8), width)
                    head = pl.ds(pl.multiple_of(first, 8), 8)
                    tail = pl.ds(pl.multiple_of(first + width - 8, 8), 8)
                    low = other[left, tail, :].astype(jnp.float32)
                    middle = own[block, rows, :].astype(jnp.float32)
                    high = other[right, head, :].astype(jnp.float32)
                    low = jnp.where(has_left, low, 0.0)
                    high = jnp.where(has_right, high, 0.0)
                    chunk = jnp.concatenate((low, middle, high), axis=0)
                    for tap in range(3):
                        lane = ((row * 3 + tap) * splits + split) * LANES
                        moved = chunk[6 + tap : 6 + tap + PAD].astype(jnp.bfloat16)
                        out[target, lane : lane + LANES] = moved
            return 0

        lax.fori_loop(0, times * blocks, step, 0)
        base += times * 2 * splits * width


def readers(layout, place, own, other):
    nz, up_half, up_count, up_size = layout
    lead = place[2] == 0

    def low(start, count):
        rows = slice(start, start + count)
        return jnp.where(lead, own[:, rows], other[:, rows])

    def high(start, count):
        rows = slice(start, start + count)
        return jnp.where(lead, other[:, rows], own[:, rows])

    def up_tile(kt, kh, kw, split, splits):
        tile = ((kt * 3 + kh) * 3 + kw) * splits + split
        if tile < up_half:
            value = low(tile * nz, nz)
        else:
            value = high((tile - (up_count - up_half)) * nz, nz)
        return value.reshape(-1, LANES)

    def mix_tile(kt, kw, pair):
        start = up_size + ((kt * 3 + kw) * 2 + pair) * 2 * nz
        return jnp.stack((low(start, 2 * nz), high(start, 2 * nz)), axis=1).reshape(-1, LANES)

    return up_tile, mix_tile


def forward_kernel(
    layout, width, place, rows, own, other, out, slope, up_w, ups, mask, hidden, mix_w, total
):
    up_tile, mix_tile = readers(layout, place, own, other)
    splits = rows.shape[1] // (6 * LANES)
    part, unit = up_w.shape[0] // 6, mask.shape[0]
    column = lax.broadcasted_iota(jnp.int32, (PAD, LANES), 0) - 1
    for block in range(out.shape[0]):
        side = (place[1] + (block + 1) // 2) % 2
        at = (2 * side + place[2]) * width + column
        inside = (at >= 0) & (at < 4 * width)
        mask[block * PAD : (block + 1) * PAD, :] = inside.astype(jnp.float32)
    for kt in range(3):
        for out_row in range(2):
            for row in range(2):
                for kw in range(3):
                    for split in range(splits):
                        at = kt * 2 * part + out_row * part
                        lane = ((row * 3 + kw) * splits + split) * LANES
                        up_w[at : at + part, lane : lane + LANES] = up_tile(
                            kt, row - out_row + 1, kw, split, splits
                        )
    step = 2 * LANES
    ups[...] = jnp.zeros_like(ups)

    def product(k, _):
        lanes = pl.ds(pl.multiple_of(k * step, step), step)
        ups[...] += lax.dot_general(
            rows[:, lanes],
            up_w[:, lanes],
            (((1,), (1,)), ((), ())),
            preferred_element_type=jnp.float32,
        )
        return 0

    lax.fori_loop(0, rows.shape[1] // step, product, 0)
    inside = mask[...] > 0
    times = 2 * (rows.shape[0] // unit - 1) - 1
    for time in range(times):
        at = time // 2 * unit
        if time % 2 == 0:
            before = ups[at + unit : at + 2 * unit, :LANES] + ups[at : at + unit, 2 * LANES :]
        else:
            before = ups[at + unit : at + 2 * unit, LANES : 2 * LANES]
        sigma = jax.nn.sigmoid(before)
        if time < times - 1:
            value = jnp.where(inside, before * sigma, 0.0)
            for kw in range(3):
                hidden[time * unit : (time + 1) * unit, kw * LANES : (kw + 1) * LANES] = later(
                    value, kw
                ).astype(jnp.bfloat16)
        if time >= 2:
            slope[(time - 2) * unit : (time - 1) * unit, :] = jnp.where(
                inside, sigma * (1.0 + before * (1.0 - sigma)), 0.0
            )
    channels = mix_w.shape[0] // 2
    for kt in range(3):
        for out_row in range(2):
            for kw in range(3):
                mix_w[
                    out_row * channels : (out_row + 1) * channels,
                    (kt * 3 + kw) * LANES : (kt * 3 + kw + 1) * LANES,
                ] = mix_tile(kt, kw, out_row)
    total[...] = jnp.zeros_like(total)
    for kt in range(3):
        total[...] += lax.dot_general(
            hidden[kt * unit : kt * unit + total.shape[0], :],
            mix_w[:, kt * 3 * LANES : (kt + 1) * 3 * LANES],
            (((1,), (1,)), ((), ())),
            preferred_element_type=jnp.float32,
        )
    store(place, out, total, 0, total.shape[0] // unit, channels, width)


def store(place, out, total, base, times, channels, width):
    splits = channels // LANES
    for block in range(out.shape[0]):
        member = (2 * place[0] + place[1] + OFFSETS[block]) % 4
        for time in range(times):
            at = (time * out.shape[0] + block) * PAD
            for tile in range(2 * splits):
                first = base + (time * 2 * splits + tile) * width
                value = total[at : at + width, tile * LANES : (tile + 1) * LANES]
                out[member, first : first + width, :] = value.astype(jnp.bfloat16)


def add_kernel(sizes, parts, *outs):
    first = 0
    for out, (times, splits, width) in zip(outs, sizes, strict=True):
        for time in range(times):
            for row in range(2):
                for split in range(splits):
                    rows = slice(first, first + width)
                    total = parts[0, rows, :].astype(jnp.float32)
                    for member in range(1, parts.shape[0]):
                        total = total + parts[member, rows, :].astype(jnp.float32)
                    lanes = slice(split * LANES, (split + 1) * LANES)
                    out[time, row, :, lanes] = total.astype(jnp.bfloat16)
                    first += width


def backward_kernel(
    layout, width, place, rows, own, other, out, base, slope, mix_w, partial, evens, odds, up_w, total
):
    up_tile, mix_tile = readers(layout, place, own, other)
    channels = rows.shape[1] // 6
    unit = evens.shape[0] - total.shape[0]
    splits = up_w.shape[1] // (2 * LANES)
    part = LANES // 2
    for kt in range(3):
        for row in range(2):
            for shift_w in range(3):
                at = (row * 3 + shift_w) * channels
                mix_w[at : at + channels, kt * LANES : (kt + 1) * LANES] = mix_tile(
                    kt, 2 - shift_w, row
                )
    step = 2 * LANES
    partial[...] = jnp.zeros_like(partial)

    def product(k, _):
        lanes = pl.ds(pl.multiple_of(k * step, step), step)
        partial[...] += jnp.dot(
            rows[:, lanes], mix_w[lanes, :], preferred_element_type=jnp.float32
        )
        return 0

    lax.fori_loop(0, rows.shape[1] // step, product, 0)
    times = rows.shape[0] // unit - 2
    for time in range(times):
        at = time * unit
        hidden_grad = (
            partial[at + 2 * unit : at + 3 * unit, :LANES]
            + partial[at + unit : at + 2 * unit, LANES : 2 * LANES]
            + partial[at : at + unit, 2 * LANES :]
        )
        value = hidden_grad * slope[at : at + unit, :]
        target = evens if time % 2 == 0 else odds
        spot = time // 2 * unit
        for shift_w in range(3):
            target[spot : spot + unit, shift_w * LANES : (shift_w + 1) * LANES] = later(
                value, shift_w
            ).astype(jnp.bfloat16)
    for kt in range(3):
        for shift_w in range(3):
            for row in range(2):
                for out_row in range(2):
                    for split in range(splits):
                        at = (kt * 3 + shift_w) * LANES + row * part
                        lane = (out_row * splits + split) * LANES
                        up_w[at : at + part, lane : lane + LANES] = up_tile(
                            kt, out_row + 1 - row, 2 - shift_w, split, splits
                        )
    count = total.shape[0]
    lhs = (evens[:count, :], odds[:count, :], evens[unit : unit + count, :])
    total[...] = jnp.zeros_like(total)
    for kt in range(3):
        total[...] += jnp.dot(
            lhs[kt],
            up_w[kt * 3 * LANES : (kt + 1) * 3 * LANES, :],
            preferred_element_type=jnp.float32,
        )
    store(place, out, total, base, count // unit, splits * LANES, width)


def compute_kernel(
    layout, width, base, place, frame_rows, cot_rows, own, other, out, slope, *scratch
):
    forward_kernel(layout, width, place, frame_rows, own, other, out, slope, *scratch[:6])
    backward_kernel(layout, width, place, cot_rows, own, other, out, base, slope, *scratch[6:])


def call(kernel, outs, scratch, flops, megabytes, place, *operands):
    space = pl.BlockSpec(memory_space=pltpu.VMEM)
    return pl.pallas_call(
        kernel,
        out_shape=outs,
        in_specs=[pl.BlockSpec(memory_space=pltpu.SMEM)] + [space] * len(operands),
        out_specs=jax.tree.map(lambda _: space, outs),
        scratch_shapes=scratch,
        compiler_params=pltpu.CompilerParams(vmem_limit_bytes=megabytes * 2**20),
        cost_estimate=pl.CostEstimate(flops=flops, bytes_accessed=8 * 2**20, transcendentals=0),
    )(place, *operands)


def unfold(place, own, other, sizes):
    unit = own.shape[0] * PAD
    outs = tuple(
        jax.ShapeDtypeStruct((times * unit, 6 * splits * LANES), jnp.bfloat16)
        for times, splits, _ in sizes
    )
    return call(functools.partial(unfold_kernel, sizes), outs, [], 10**9, 14, place, own, other)


def compute(layout, place, frame_rows, cot_rows, own, other, width, channels, in_channels):
    blocks = own.shape[0]
    unit = blocks * PAD
    times = 2 * (frame_rows.shape[0] // unit - 3)
    base = times * 2 * (channels // LANES) * width
    rows = base + times * (in_channels // LANES) * width
    scratch = [
        pltpu.VMEM(((times + 1) * unit, LANES), jnp.float32),
        pltpu.VMEM((3 * LANES, frame_rows.shape[1]), jnp.bfloat16),
        pltpu.VMEM((frame_rows.shape[0], 3 * LANES), jnp.float32),
        pltpu.VMEM((unit, LANES), jnp.float32),
        pltpu.VMEM(((times + 2) * unit, 3 * LANES), jnp.bfloat16),
        pltpu.VMEM((2 * channels, 9 * LANES), jnp.bfloat16),
        pltpu.VMEM((times * unit, 2 * channels), jnp.float32),
        pltpu.VMEM((cot_rows.shape[1], 3 * LANES), jnp.bfloat16),
        pltpu.VMEM((cot_rows.shape[0], 3 * LANES), jnp.float32),
        pltpu.VMEM((times // 2 * unit + unit, 3 * LANES), jnp.bfloat16),
        pltpu.VMEM((times // 2 * unit, 3 * LANES), jnp.bfloat16),
        pltpu.VMEM((9 * LANES, 2 * in_channels), jnp.bfloat16),
        pltpu.VMEM((times // 2 * unit, 2 * in_channels), jnp.float32),
    ]
    kernel = functools.partial(compute_kernel, layout, width, base)
    out = jax.ShapeDtypeStruct((blocks, rows, LANES), jnp.bfloat16)
    return call(kernel, out, scratch, 4 * 10**9, 32, place, frame_rows, cot_rows, own, other)


def add_parts(parts, sizes):
    space = pl.BlockSpec(memory_space=pltpu.VMEM)
    return pl.pallas_call(
        functools.partial(add_kernel, sizes),
        out_shape=tuple(
            jax.ShapeDtypeStruct((times, 2, width, splits * LANES), jnp.bfloat16)
            for times, splits, width in sizes
        ),
        in_specs=[space],
        out_specs=(space, space),
        compiler_params=pltpu.CompilerParams(vmem_limit_bytes=8 * 2**20),
    )(parts)


def ring(array, by):
    return lax.ppermute(array, RING, [(i, (i + by) % 4) for i in range(4)])


def flat(field):
    tiles = field.reshape(*field.shape[:3], -1, LANES)
    return tiles.transpose(0, 1, 3, 2, 4).reshape(-1, LANES)


def tiles_of(kernel):
    return kernel.T.reshape(2, -1, LANES).transpose(1, 0, 2)


def shards(frames, up_kernel, mix_kernel, cotangent):
    frame_count, height, width, in_channels = frames.shape
    out_channels = mix_kernel.shape[0] // 27
    xh, xl, core = lax.axis_index("xh"), lax.axis_index("xl"), lax.axis_index("core")
    ny, nz, nx = lax.axis_size("y"), lax.axis_size("z"), lax.axis_size(RING)
    part = out_channels // nx

    raw_mix = tiles_of(mix_kernel)
    mix_other = lax.ppermute(raw_mix, RING, [(0, 3), (3, 0), (1, 2), (2, 1)])
    up_column = lax.dynamic_index_in_dim(up_kernel.T, xl, 0, keepdims=False)
    up_tiles = up_column.reshape(-1, LANES)
    up_count = up_tiles.shape[0]
    up_half = (up_count + 1) // 2
    up_part = lax.dynamic_slice_in_dim(up_tiles, core * (up_count - up_half), up_half, 0)
    up_pairs = (up_half + 1) // 2
    up_part = jnp.pad(up_part, ((0, 2 * up_pairs - up_half), (0, 0))).reshape(-1, 2, LANES)

    mix_tiles = jnp.where(xh == core, raw_mix, mix_other)
    splits = out_channels // LANES
    pick_shape = (3, out_channels, 4 * part)
    tap = lax.broadcasted_iota(jnp.int32, pick_shape, 0)
    source = lax.broadcasted_iota(jnp.int32, pick_shape, 1)
    target = lax.broadcasted_iota(jnp.int32, pick_shape, 2)
    pair, side, place = target // (2 * part), target // part % 2, target % part
    wanted = (place // nz) * (4 * nz) + xh * (2 * nz) + (place % nz) * 2 + xl
    pick = (source == wanted) & (tap == side + 1 - pair)
    mix_part = jnp.einsum(
        "thwsjl,hslm->twjm",
        mix_tiles.reshape(3, 3, 3, splits, 2, LANES),
        pick.astype(jnp.bfloat16).reshape(3, splits, LANES, 4 * part),
        preferred_element_type=jnp.float32,
    ).astype(jnp.bfloat16)
    mix_part = mix_part.reshape(9, 2, 2, 2 * part).transpose(0, 2, 1, 3).reshape(-1, 2, LANES)

    payload, *halos = lax.optimization_barrier(
        (
            jnp.concatenate((up_part, mix_part), axis=0),
            shift(frames[-2:], PLANES, 1),
            shift(frames[:1], PLANES, -1),
            shift(cotangent[:3], PLANES, -1),
        )
    )
    planes = spread(payload, "z")
    fields = jnp.concatenate((halos[0], frames, halos[1]), axis=0)
    cots = jnp.concatenate((cotangent, halos[2]), axis=0)
    block = jnp.concatenate((flat(fields), flat(cots)), axis=0)
    blocks = (block, ring(block, 1), ring(block, -1), ring(block, 2))
    planes, block = lax.optimization_barrier((planes, block))
    blocks = jnp.stack(blocks)
    others = swap(blocks)

    up_rows = planes[:, :up_pairs].transpose(1, 2, 0, 3).reshape(-1, LANES)
    mix_rows = planes[:, up_pairs:].transpose(1, 0, 2, 3).reshape(-1, LANES)
    own = spread(jnp.concatenate((up_rows, mix_rows), axis=0), "y")
    other = swap(own)
    layout = (nz, up_half, up_count, up_rows.shape[0])

    place = jnp.stack((xh, xl, core))
    sizes = (
        (fields.shape[0], in_channels // LANES, width),
        (cots.shape[0], splits, width),
    )
    frame_rows, cot_rows = unfold(place, blocks, others, sizes)
    parts = compute(
        layout, place, frame_rows, cot_rows, own, other, width, out_channels, in_channels
    )
    parts = lax.all_to_all(parts, RING, 0, 0, tiled=True)
    outs = ((2 * frame_count, splits, width), (frame_count, in_channels // LANES, width))
    return add_parts(parts, outs)


def solution(mesh):
    planes, columns = mesh.devices.shape
    shape = (4, 2, planes // 8, 2, columns // 2)
    fine = Mesh(mesh.devices.reshape(shape), (*PLANES, *COLS))
    placed = P(PLANES, None, COLS, None)
    weights = P(None, PLANES)
    return jax.shard_map(
        shards,
        mesh=fine,
        in_specs=(placed, weights, weights, placed),
        out_specs=(placed, placed),
        check_vma=False,
    )
```

```python
import functools

import jax
import jax.numpy as jnp
import numpy as np
from jax import lax
from jax.experimental import pallas as pl
from jax.experimental.pallas import tpu as pltpu
from jax.sharding import Mesh, PartitionSpec as P

PLANES = ("y", "xh", "z")
COLS = ("xl", "core")
RING = ("xh", "xl")
LANES = 128
PAD = 32
OFFSETS = (0, 3, 1, 2)


def shift(array, axis, by):
    devices = lax.axis_size(axis)
    pairs = [(i, i + by) for i in range(devices) if 0 <= i + by < devices]
    return lax.ppermute(array, axis, pairs)


def swap(array):
    return lax.ppermute(array, "core", [(0, 1), (1, 0)])


def spread(array, axis):
    count = lax.axis_size(axis)
    return lax.all_to_all(
        jnp.broadcast_to(array, (count, *array.shape)), axis, 0, 0, tiled=True
    )


def later(rows, by):
    if by == 0:
        return rows
    return pltpu.roll(rows, rows.shape[0] - by, 0)


def unfold_kernel(sizes, width, place, own, other, frame_rows, cot_rows):
    xl, core = place[1], place[2]
    blocks = own.shape[0]

    def step(block, _):
        side = (xl + (block + 1) // 2) % 2
        partner = jnp.where(xl == 0, (block + 2) % 4, block + 1 - 2 * (block % 2))
        left = jnp.where(core == 1, block, partner)
        right = jnp.where(core == 0, block, partner)
        has_left = 2 * side + core > 0
        has_right = 2 * side + core < 3
        for out, (starts, splits) in zip((frame_rows, cot_rows), sizes, strict=True):
            for time, start in enumerate(starts):
                target = pl.ds(pl.multiple_of((time * blocks + block) * PAD, PAD), PAD)
                for tile in range(2 * splits):
                    row, split = tile // splits, tile % splits
                    first = start + tile * width
                    low = other[left, first + width - 8 : first + width, :].astype(jnp.float32)
                    middle = own[block, first : first + width, :].astype(jnp.float32)
                    high = other[right, first : first + 8, :].astype(jnp.float32)
                    low = jnp.where(has_left, low, 0.0)
                    high = jnp.where(has_right, high, 0.0)
                    chunk = jnp.concatenate((low, middle, high), axis=0)
                    for tap in range(3):
                        lane = ((row * 3 + tap) * splits + split) * LANES
                        moved = chunk[6 + tap : 6 + tap + PAD].astype(jnp.bfloat16)
                        out[target, lane : lane + LANES] = moved
        return 0

    lax.fori_loop(0, blocks, step, 0)


def readers(layout, place, own, other):
    nz, up_half, up_count, up_size = layout
    lead = place[2] == 0

    def low(start, count):
        rows = slice(start, start + count)
        return jnp.where(lead, own[:, rows], other[:, rows])

    def high(start, count):
        rows = slice(start, start + count)
        return jnp.where(lead, other[:, rows], own[:, rows])

    def up_tile(kt, kh, kw, split, splits):
        tile = ((kt * 3 + kh) * 3 + kw) * splits + split
        if tile < up_half:
            value = low(tile * nz, nz)
        else:
            value = high((tile - (up_count - up_half)) * nz, nz)
        return value.reshape(-1, LANES)

    def mix_tile(kt, kw, pair):
        start = up_size + ((kt * 3 + kw) * 2 + pair) * 2 * nz
        return jnp.stack((low(start, 2 * nz), high(start, 2 * nz)), axis=1).reshape(-1, LANES)

    return up_tile, mix_tile


def forward_kernel(
    layout, width, place, rows, own, other, out, slope, up_w, ups, mask, hidden, mix_w, total
):
    up_tile, mix_tile = readers(layout, place, own, other)
    splits = rows.shape[1] // (6 * LANES)
    part, unit = up_w.shape[0] // 6, mask.shape[0]
    column = lax.broadcasted_iota(jnp.int32, (PAD, LANES), 0) - 1
    for block in range(out.shape[0]):
        side = (place[1] + (block + 1) // 2) % 2
        at = (2 * side + place[2]) * width + column
        inside = (at >= 0) & (at < 4 * width)
        mask[block * PAD : (block + 1) * PAD, :] = inside.astype(jnp.float32)
    for kt in range(3):
        for out_row in range(2):
            for row in range(2):
                for kw in range(3):
                    for split in range(splits):
                        at = kt * 2 * part + out_row * part
                        lane = ((row * 3 + kw) * splits + split) * LANES
                        up_w[at : at + part, lane : lane + LANES] = up_tile(
                            kt, row - out_row + 1, kw, split, splits
                        )
    step = 2 * LANES
    ups[...] = jnp.zeros_like(ups)

    def product(k, _):
        lanes = pl.ds(pl.multiple_of(k * step, step), step)
        ups[...] += lax.dot_general(
            rows[:, lanes],
            up_w[:, lanes],
            (((1,), (1,)), ((), ())),
            preferred_element_type=jnp.float32,
        )
        return 0

    lax.fori_loop(0, rows.shape[1] // step, product, 0)
    inside = mask[...] > 0
    times = 2 * (rows.shape[0] // unit - 1) - 1
    for time in range(times):
        at = time // 2 * unit
        if time % 2 == 0:
            before = ups[at + unit : at + 2 * unit, :LANES] + ups[at : at + unit, 2 * LANES :]
        else:
            before = ups[at + unit : at + 2 * unit, LANES : 2 * LANES]
        sigma = jax.nn.sigmoid(before)
        if time < times - 1:
            value = jnp.where(inside, before * sigma, 0.0)
            for kw in range(3):
                hidden[time * unit : (time + 1) * unit, kw * LANES : (kw + 1) * LANES] = later(
                    value, kw
                ).astype(jnp.bfloat16)
        if time >= 2:
            slope[(time - 2) * unit : (time - 1) * unit, :] = jnp.where(
                inside, sigma * (1.0 + before * (1.0 - sigma)), 0.0
            )
    channels = mix_w.shape[0] // 2
    for kt in range(3):
        for out_row in range(2):
            for kw in range(3):
                mix_w[
                    out_row * channels : (out_row + 1) * channels,
                    (kt * 3 + kw) * LANES : (kt * 3 + kw + 1) * LANES,
                ] = mix_tile(kt, kw, out_row)
    total[...] = jnp.zeros_like(total)
    for kt in range(3):
        total[...] += lax.dot_general(
            hidden[kt * unit : kt * unit + total.shape[0], :],
            mix_w[:, kt * 3 * LANES : (kt + 1) * 3 * LANES],
            (((1,), (1,)), ((), ())),
            preferred_element_type=jnp.float32,
        )
    store(place, out, total, 0, total.shape[0] // unit, channels, width)


def store(place, out, total, base, times, channels, width):
    splits = channels // LANES
    for block in range(out.shape[0]):
        member = (2 * place[0] + place[1] + OFFSETS[block]) % 4
        for time in range(times):
            at = (time * out.shape[0] + block) * PAD
            for tile in range(2 * splits):
                first = base + (time * 2 * splits + tile) * width
                value = total[at : at + width, tile * LANES : (tile + 1) * LANES]
                out[member, first : first + width, :] = value.astype(jnp.bfloat16)


def add_kernel(sizes, parts, *outs):
    first = 0
    for out, (times, splits, width) in zip(outs, sizes, strict=True):
        for time in range(times):
            for row in range(2):
                for split in range(splits):
                    rows = slice(first, first + width)
                    total = parts[0, rows, :].astype(jnp.float32)
                    for member in range(1, parts.shape[0]):
                        total = total + parts[member, rows, :].astype(jnp.float32)
                    lanes = slice(split * LANES, (split + 1) * LANES)
                    out[time, row, :, lanes] = total.astype(jnp.bfloat16)
                    first += width


def backward_kernel(
    layout, width, place, rows, own, other, out, base, slope, mix_w, partial, evens, odds, up_w, total
):
    up_tile, mix_tile = readers(layout, place, own, other)
    channels = rows.shape[1] // 6
    unit = evens.shape[0] - total.shape[0]
    splits = up_w.shape[1] // (2 * LANES)
    part = LANES // 2
    for kt in range(3):
        for row in range(2):
            for shift_w in range(3):
                at = (row * 3 + shift_w) * channels
                mix_w[at : at + channels, kt * LANES : (kt + 1) * LANES] = mix_tile(
                    kt, 2 - shift_w, row
                )
    step = 2 * LANES
    partial[...] = jnp.zeros_like(partial)

    def product(k, _):
        lanes = pl.ds(pl.multiple_of(k * step, step), step)
        partial[...] += jnp.dot(
            rows[:, lanes], mix_w[lanes, :], preferred_element_type=jnp.float32
        )
        return 0

    lax.fori_loop(0, rows.shape[1] // step, product, 0)
    times = rows.shape[0] // unit - 2
    for time in range(times):
        at = time * unit
        hidden_grad = (
            partial[at + 2 * unit : at + 3 * unit, :LANES]
            + partial[at + unit : at + 2 * unit, LANES : 2 * LANES]
            + partial[at : at + unit, 2 * LANES :]
        )
        value = hidden_grad * slope[at : at + unit, :]
        target = evens if time % 2 == 0 else odds
        spot = time // 2 * unit
        for shift_w in range(3):
            target[spot : spot + unit, shift_w * LANES : (shift_w + 1) * LANES] = later(
                value, shift_w
            ).astype(jnp.bfloat16)
    for kt in range(3):
        for shift_w in range(3):
            for row in range(2):
                for out_row in range(2):
                    for split in range(splits):
                        at = (kt * 3 + shift_w) * LANES + row * part
                        lane = (out_row * splits + split) * LANES
                        up_w[at : at + part, lane : lane + LANES] = up_tile(
                            kt, out_row + 1 - row, 2 - shift_w, split, splits
                        )
    count = total.shape[0]
    lhs = (evens[:count, :], odds[:count, :], evens[unit : unit + count, :])
    total[...] = jnp.zeros_like(total)
    for kt in range(3):
        total[...] += jnp.dot(
            lhs[kt],
            up_w[kt * 3 * LANES : (kt + 1) * 3 * LANES, :],
            preferred_element_type=jnp.float32,
        )
    store(place, out, total, base, count // unit, splits * LANES, width)


def compute_kernel(
    layout, width, base, place, frame_rows, cot_rows, own, other, out, slope, *scratch
):
    forward_kernel(layout, width, place, frame_rows, own, other, out, slope, *scratch[:6])
    backward_kernel(layout, width, place, cot_rows, own, other, out, base, slope, *scratch[6:])


def call(kernel, outs, scratch, flops, megabytes, place, *operands):
    space = pl.BlockSpec(memory_space=pltpu.VMEM)
    return pl.pallas_call(
        kernel,
        out_shape=outs,
        in_specs=[pl.BlockSpec(memory_space=pltpu.SMEM)] + [space] * len(operands),
        out_specs=jax.tree.map(lambda _: space, outs),
        scratch_shapes=scratch,
        compiler_params=pltpu.CompilerParams(vmem_limit_bytes=megabytes * 2**20),
        cost_estimate=pl.CostEstimate(flops=flops, bytes_accessed=8 * 2**20, transcendentals=0),
    )(place, *operands)


def unfold(place, own, other, sizes, width):
    unit = own.shape[0] * PAD
    outs = tuple(
        jax.ShapeDtypeStruct((len(starts) * unit, 6 * splits * LANES), jnp.bfloat16)
        for starts, splits in sizes
    )
    kernel = functools.partial(unfold_kernel, sizes, width)
    return call(kernel, outs, [], 10**9, 14, place, own, other)


def beside(blocks, xh, z, by):
    axes = ("y", "xh", "z", "xl")
    dims = tuple(lax.axis_size(axis) for axis in axes)
    edge = dims[2] - 1 if by > 0 else 0
    near, wrap = [], []
    for target in np.ndindex(*dims):
        ty, tx, tz, tl = target
        to = int(np.ravel_multi_index(target, dims))
        if tz != edge:
            near.append((int(np.ravel_multi_index((ty, tx, tz + by, tl), dims)), to))
            continue
        far = dims[2] - 1 - edge
        near.append((int(np.ravel_multi_index((ty, 1 - tx, far, tl), dims)), to))
        if 0 <= ty + by < dims[0]:
            wrap.append((int(np.ravel_multi_index((ty + by, 1 - tx, far, tl), dims)), to))
    beyond = lax.ppermute(blocks, axes, wrap)
    side = (xh * 2 + lax.axis_index("xl") + jnp.array(OFFSETS)) % 4 // 2
    turned = (z == edge) & (side == (1 if by > 0 else 0))
    return jnp.where(turned[:, None, None], beyond, lax.ppermute(blocks, axes, near))


def compute(layout, place, frame_rows, cot_rows, own, other, width, channels, in_channels):
    blocks = own.shape[0]
    unit = blocks * PAD
    times = 2 * (frame_rows.shape[0] // unit - 3)
    base = times * 2 * (channels // LANES) * width
    rows = base + times * (in_channels // LANES) * width
    scratch = [
        pltpu.VMEM(((times + 1) * unit, LANES), jnp.float32),
        pltpu.VMEM((3 * LANES, frame_rows.shape[1]), jnp.bfloat16),
        pltpu.VMEM((frame_rows.shape[0], 3 * LANES), jnp.float32),
        pltpu.VMEM((unit, LANES), jnp.float32),
        pltpu.VMEM(((times + 2) * unit, 3 * LANES), jnp.bfloat16),
        pltpu.VMEM((2 * channels, 9 * LANES), jnp.bfloat16),
        pltpu.VMEM((times * unit, 2 * channels), jnp.float32),
        pltpu.VMEM((cot_rows.shape[1], 3 * LANES), jnp.bfloat16),
        pltpu.VMEM((cot_rows.shape[0], 3 * LANES), jnp.float32),
        pltpu.VMEM((times // 2 * unit + unit, 3 * LANES), jnp.bfloat16),
        pltpu.VMEM((times // 2 * unit, 3 * LANES), jnp.bfloat16),
        pltpu.VMEM((9 * LANES, 2 * in_channels), jnp.bfloat16),
        pltpu.VMEM((times // 2 * unit, 2 * in_channels), jnp.float32),
    ]
    kernel = functools.partial(compute_kernel, layout, width, base)
    out = jax.ShapeDtypeStruct((blocks, rows, LANES), jnp.bfloat16)
    return call(kernel, out, scratch, 4 * 10**9, 32, place, frame_rows, cot_rows, own, other)


def add_parts(parts, sizes):
    space = pl.BlockSpec(memory_space=pltpu.VMEM)
    return pl.pallas_call(
        functools.partial(add_kernel, sizes),
        out_shape=tuple(
            jax.ShapeDtypeStruct((times, 2, width, splits * LANES), jnp.bfloat16)
            for times, splits, width in sizes
        ),
        in_specs=[space],
        out_specs=(space, space),
        compiler_params=pltpu.CompilerParams(vmem_limit_bytes=8 * 2**20),
    )(parts)


def ring(array, by):
    return lax.ppermute(array, RING, [(i, (i + by) % 4) for i in range(4)])


def flat(field):
    tiles = field.reshape(*field.shape[:3], -1, LANES)
    return tiles.transpose(0, 1, 3, 2, 4).reshape(-1, LANES)


def tiles_of(kernel):
    return kernel.T.reshape(2, -1, LANES).transpose(1, 0, 2)


def shards(frames, up_kernel, mix_kernel, cotangent):
    frame_count, height, width, in_channels = frames.shape
    out_channels = mix_kernel.shape[0] // 27
    xh, xl, core = lax.axis_index("xh"), lax.axis_index("xl"), lax.axis_index("core")
    ny, nz, nx = lax.axis_size("y"), lax.axis_size("z"), lax.axis_size(RING)
    part = out_channels // nx

    raw_mix = tiles_of(mix_kernel)
    mix_other = lax.ppermute(raw_mix, RING, [(0, 3), (3, 0), (1, 2), (2, 1)])
    up_column = lax.dynamic_index_in_dim(up_kernel.T, xl, 0, keepdims=False)
    up_tiles = up_column.reshape(-1, LANES)
    up_count = up_tiles.shape[0]
    up_half = (up_count + 1) // 2
    up_part = lax.dynamic_slice_in_dim(up_tiles, core * (up_count - up_half), up_half, 0)
    up_pairs = (up_half + 1) // 2
    up_part = jnp.pad(up_part, ((0, 2 * up_pairs - up_half), (0, 0))).reshape(-1, 2, LANES)

    mix_tiles = jnp.where(xh == core, raw_mix, mix_other)
    splits = out_channels // LANES
    pick_shape = (3, out_channels, 4 * part)
    tap = lax.broadcasted_iota(jnp.int32, pick_shape, 0)
    source = lax.broadcasted_iota(jnp.int32, pick_shape, 1)
    target = lax.broadcasted_iota(jnp.int32, pick_shape, 2)
    pair, side, place = target // (2 * part), target // part % 2, target % part
    wanted = (place // nz) * (4 * nz) + xh * (2 * nz) + (place % nz) * 2 + xl
    pick = (source == wanted) & (tap == side + 1 - pair)
    mix_part = jnp.einsum(
        "thwsjl,hslm->twjm",
        mix_tiles.reshape(3, 3, 3, splits, 2, LANES),
        pick.astype(jnp.bfloat16).reshape(3, splits, LANES, 4 * part),
        preferred_element_type=jnp.float32,
    ).astype(jnp.bfloat16)
    mix_part = mix_part.reshape(9, 2, 2, 2 * part).transpose(0, 2, 1, 3).reshape(-1, 2, LANES)

    frame_size, cot_size = 2 * (in_channels // LANES) * width, 2 * splits * width
    count = 2 * frame_count
    block = jnp.concatenate((flat(cotangent[3:]), flat(cotangent[:3]), flat(frames)), axis=0)
    payload, *rest = lax.optimization_barrier(
        (
            jnp.concatenate((up_part, mix_part), axis=0),
            ring(block, 1),
            ring(block, -1),
            ring(block, 2),
        )
    )
    planes = spread(payload, "z")
    blocks = jnp.stack((block, *rest))
    z = lax.axis_index("z")
    early = (count - 3) * cot_size
    following = beside(blocks[:, early : count * cot_size + frame_size], xh, z, 1)
    previous = beside(blocks[:, block.shape[0] - 2 * frame_size :], xh, z, -1)
    blocks = jnp.concatenate((blocks, following, previous), axis=1)
    others = swap(blocks)
    first = block.shape[0]
    last = first + 3 * cot_size + frame_size
    cot_starts = [early + time * cot_size for time in range(3)]
    cot_starts += [time * cot_size for time in range(count - 3)]
    cot_starts += [first + time * cot_size for time in range(3)]
    frame_starts = [last + time * frame_size for time in range(2)]
    frame_starts += [count * cot_size + time * frame_size for time in range(frame_count)]
    frame_starts += [first + 3 * cot_size]

    up_rows = planes[:, :up_pairs].transpose(1, 2, 0, 3).reshape(-1, LANES)
    mix_rows = planes[:, up_pairs:].transpose(1, 0, 2, 3).reshape(-1, LANES)
    own = spread(jnp.concatenate((up_rows, mix_rows), axis=0), "y")
    other = swap(own)
    layout = (nz, up_half, up_count, up_rows.shape[0])

    place = jnp.stack((xh, xl, core))
    sizes = ((tuple(frame_starts), in_channels // LANES), (tuple(cot_starts), splits))
    frame_rows, cot_rows = unfold(place, blocks, others, sizes, width)
    parts = compute(
        layout, place, frame_rows, cot_rows, own, other, width, out_channels, in_channels
    )
    parts = lax.all_to_all(parts, RING, 0, 0, tiled=True)
    outs = ((count, splits, width), (frame_count, in_channels // LANES, width))
    return add_parts(parts, outs)


def solution(mesh):
    planes, columns = mesh.devices.shape
    shape = (4, 2, planes // 8, 2, columns // 2)
    fine = Mesh(mesh.devices.reshape(shape), (*PLANES, *COLS))
    placed = P(PLANES, None, COLS, None)
    weights = P(None, PLANES)
    return jax.shard_map(
        shards,
        mesh=fine,
        in_specs=(placed, weights, weights, placed),
        out_specs=(placed, placed),
        check_vma=False,
    )
```

```python
import functools

import jax
import jax.numpy as jnp
from jax import lax
from jax.experimental import pallas as pl
from jax.experimental.pallas import tpu as pltpu
from jax.sharding import Mesh, PartitionSpec as P

PLANES = ("y", "xh", "z")
COLS = ("xl", "core")
RING = ("xh", "xl")
LANES = 128
PAD = 32
OFFSETS = (0, 3, 1, 2)


def shift(array, axis, by):
    devices = lax.axis_size(axis)
    pairs = [(i, i + by) for i in range(devices) if 0 <= i + by < devices]
    return lax.ppermute(array, axis, pairs)


def swap(array):
    return lax.ppermute(array, "core", [(0, 1), (1, 0)])


def spread(array, axis):
    count = lax.axis_size(axis)
    return lax.all_to_all(
        jnp.broadcast_to(array, (count, *array.shape)), axis, 0, 0, tiled=True
    )


def later(rows, by):
    if by == 0:
        return rows
    return pltpu.roll(rows, rows.shape[0] - by, 0)


def unfold_kernel(sizes, width, place, own, other, frame_rows, cot_rows):
    xl, core = place[1], place[2]
    blocks = own.shape[0]

    def step(block, _):
        side = (xl + (block + 1) // 2) % 2
        partner = jnp.where(xl == 0, (block + 2) % 4, block + 1 - 2 * (block % 2))
        left = jnp.where(core == 1, block, partner)
        right = jnp.where(core == 0, block, partner)
        has_left = 2 * side + core > 0
        has_right = 2 * side + core < 3
        for out, (starts, splits) in zip((frame_rows, cot_rows), sizes, strict=True):
            for time, start in enumerate(starts):
                target = pl.ds(pl.multiple_of((time * blocks + block) * PAD, PAD), PAD)
                for tile in range(2 * splits):
                    row, split = tile // splits, tile % splits
                    first = start + tile * width
                    low = other[left, first + width - 8 : first + width, :].astype(jnp.float32)
                    middle = own[block, first : first + width, :].astype(jnp.float32)
                    high = other[right, first : first + 8, :].astype(jnp.float32)
                    low = jnp.where(has_left, low, 0.0)
                    high = jnp.where(has_right, high, 0.0)
                    chunk = jnp.concatenate((low, middle, high), axis=0)
                    for tap in range(3):
                        lane = ((row * 3 + tap) * splits + split) * LANES
                        moved = chunk[6 + tap : 6 + tap + PAD].astype(jnp.bfloat16)
                        out[target, lane : lane + LANES] = moved
        return 0

    lax.fori_loop(0, blocks, step, 0)


def readers(layout, place, own, other):
    nz, up_half, up_count, up_size = layout
    lead = place[2] == 0

    def low(start, count):
        rows = slice(start, start + count)
        return jnp.where(lead, own[:, rows], other[:, rows])

    def high(start, count):
        rows = slice(start, start + count)
        return jnp.where(lead, other[:, rows], own[:, rows])

    def up_tile(kt, kh, kw, split, splits):
        tile = ((kt * 3 + kh) * 3 + kw) * splits + split
        if tile < up_half:
            value = low(tile * nz, nz)
        else:
            value = high((tile - (up_count - up_half)) * nz, nz)
        return value.reshape(-1, LANES)

    def mix_tile(kt, kw, pair):
        start = up_size + ((kt * 3 + kw) * 2 + pair) * 2 * nz
        return jnp.stack((low(start, 2 * nz), high(start, 2 * nz)), axis=1).reshape(-1, LANES)

    return up_tile, mix_tile


def forward_kernel(
    layout, width, place, rows, own, other, out, slope, up_w, ups, mask, hidden, mix_w, total
):
    up_tile, mix_tile = readers(layout, place, own, other)
    splits = rows.shape[1] // (6 * LANES)
    part, unit = up_w.shape[0] // 6, mask.shape[0]
    column = lax.broadcasted_iota(jnp.int32, (PAD, LANES), 0) - 1
    for block in range(out.shape[0]):
        side = (place[1] + (block + 1) // 2) % 2
        at = (2 * side + place[2]) * width + column
        inside = (at >= 0) & (at < 4 * width)
        mask[block * PAD : (block + 1) * PAD, :] = inside.astype(jnp.float32)
    for kt in range(3):
        for out_row in range(2):
            for row in range(2):
                for kw in range(3):
                    for split in range(splits):
                        at = kt * 2 * part + out_row * part
                        lane = ((row * 3 + kw) * splits + split) * LANES
                        up_w[at : at + part, lane : lane + LANES] = up_tile(
                            kt, row - out_row + 1, kw, split, splits
                        )
    step = 2 * LANES
    ups[...] = jnp.zeros_like(ups)

    def product(k, _):
        lanes = pl.ds(pl.multiple_of(k * step, step), step)
        ups[...] += lax.dot_general(
            rows[:, lanes],
            up_w[:, lanes],
            (((1,), (1,)), ((), ())),
            preferred_element_type=jnp.float32,
        )
        return 0

    lax.fori_loop(0, rows.shape[1] // step, product, 0)
    inside = mask[...] > 0
    times = 2 * (rows.shape[0] // unit - 1) - 1
    for time in range(times):
        at = time // 2 * unit
        if time % 2 == 0:
            before = ups[at + unit : at + 2 * unit, :LANES] + ups[at : at + unit, 2 * LANES :]
        else:
            before = ups[at + unit : at + 2 * unit, LANES : 2 * LANES]
        sigma = jax.nn.sigmoid(before)
        if time < times - 1:
            value = jnp.where(inside, before * sigma, 0.0)
            for kw in range(3):
                hidden[time * unit : (time + 1) * unit, kw * LANES : (kw + 1) * LANES] = later(
                    value, kw
                ).astype(jnp.bfloat16)
        if time >= 2:
            slope[(time - 2) * unit : (time - 1) * unit, :] = jnp.where(
                inside, sigma * (1.0 + before * (1.0 - sigma)), 0.0
            )
    channels = mix_w.shape[0] // 2
    for kt in range(3):
        for out_row in range(2):
            for kw in range(3):
                mix_w[
                    out_row * channels : (out_row + 1) * channels,
                    (kt * 3 + kw) * LANES : (kt * 3 + kw + 1) * LANES,
                ] = mix_tile(kt, kw, out_row)
    total[...] = jnp.zeros_like(total)
    for kt in range(3):
        total[...] += lax.dot_general(
            hidden[kt * unit : kt * unit + total.shape[0], :],
            mix_w[:, kt * 3 * LANES : (kt + 1) * 3 * LANES],
            (((1,), (1,)), ((), ())),
            preferred_element_type=jnp.float32,
        )
    store(place, out, total, 0, total.shape[0] // unit, channels, width)


def store(place, out, total, base, times, channels, width):
    splits = channels // LANES
    for block in range(out.shape[0]):
        member = (2 * place[0] + place[1] + OFFSETS[block]) % 4
        for time in range(times):
            at = (time * out.shape[0] + block) * PAD
            for tile in range(2 * splits):
                first = base + (time * 2 * splits + tile) * width
                value = total[at : at + width, tile * LANES : (tile + 1) * LANES]
                out[member, first : first + width, :] = value.astype(jnp.bfloat16)


def add_kernel(sizes, parts, *outs):
    first = 0
    for out, (times, splits, width) in zip(outs, sizes, strict=True):
        for time in range(times):
            for row in range(2):
                for split in range(splits):
                    rows = slice(first, first + width)
                    total = parts[0, rows, :].astype(jnp.float32)
                    for member in range(1, parts.shape[0]):
                        total = total + parts[member, rows, :].astype(jnp.float32)
                    lanes = slice(split * LANES, (split + 1) * LANES)
                    out[time, row, :, lanes] = total.astype(jnp.bfloat16)
                    first += width


def backward_kernel(
    layout, width, place, rows, own, other, out, base, slope, mix_w, partial, evens, odds, up_w, total
):
    up_tile, mix_tile = readers(layout, place, own, other)
    channels = rows.shape[1] // 6
    unit = evens.shape[0] - total.shape[0]
    splits = up_w.shape[1] // (2 * LANES)
    part = LANES // 2
    for kt in range(3):
        for row in range(2):
            for shift_w in range(3):
                at = (row * 3 + shift_w) * channels
                mix_w[at : at + channels, kt * LANES : (kt + 1) * LANES] = mix_tile(
                    kt, 2 - shift_w, row
                )
    step = 2 * LANES
    partial[...] = jnp.zeros_like(partial)

    def product(k, _):
        lanes = pl.ds(pl.multiple_of(k * step, step), step)
        partial[...] += jnp.dot(
            rows[:, lanes], mix_w[lanes, :], preferred_element_type=jnp.float32
        )
        return 0

    lax.fori_loop(0, rows.shape[1] // step, product, 0)
    times = rows.shape[0] // unit - 2
    for time in range(times):
        at = time * unit
        hidden_grad = (
            partial[at + 2 * unit : at + 3 * unit, :LANES]
            + partial[at + unit : at + 2 * unit, LANES : 2 * LANES]
            + partial[at : at + unit, 2 * LANES :]
        )
        value = hidden_grad * slope[at : at + unit, :]
        target = evens if time % 2 == 0 else odds
        spot = time // 2 * unit
        for shift_w in range(3):
            target[spot : spot + unit, shift_w * LANES : (shift_w + 1) * LANES] = later(
                value, shift_w
            ).astype(jnp.bfloat16)
    for kt in range(3):
        for shift_w in range(3):
            for row in range(2):
                for out_row in range(2):
                    for split in range(splits):
                        at = (kt * 3 + shift_w) * LANES + row * part
                        lane = (out_row * splits + split) * LANES
                        up_w[at : at + part, lane : lane + LANES] = up_tile(
                            kt, out_row + 1 - row, 2 - shift_w, split, splits
                        )
    count = total.shape[0]
    lhs = (evens[:count, :], odds[:count, :], evens[unit : unit + count, :])
    total[...] = jnp.zeros_like(total)
    for kt in range(3):
        total[...] += jnp.dot(
            lhs[kt],
            up_w[kt * 3 * LANES : (kt + 1) * 3 * LANES, :],
            preferred_element_type=jnp.float32,
        )
    store(place, out, total, base, count // unit, splits * LANES, width)


def compute_kernel(
    layout, width, base, place, frame_rows, cot_rows, own, other, out, slope, *scratch
):
    forward_kernel(layout, width, place, frame_rows, own, other, out, slope, *scratch[:6])
    backward_kernel(layout, width, place, cot_rows, own, other, out, base, slope, *scratch[6:])


def call(kernel, outs, scratch, flops, megabytes, place, *operands):
    space = pl.BlockSpec(memory_space=pltpu.VMEM)
    return pl.pallas_call(
        kernel,
        out_shape=outs,
        in_specs=[pl.BlockSpec(memory_space=pltpu.SMEM)] + [space] * len(operands),
        out_specs=jax.tree.map(lambda _: space, outs),
        scratch_shapes=scratch,
        compiler_params=pltpu.CompilerParams(vmem_limit_bytes=megabytes * 2**20),
        cost_estimate=pl.CostEstimate(flops=flops, bytes_accessed=8 * 2**20, transcendentals=0),
    )(place, *operands)


def unfold(place, own, other, sizes, width):
    unit = own.shape[0] * PAD
    outs = tuple(
        jax.ShapeDtypeStruct((len(starts) * unit, 6 * splits * LANES), jnp.bfloat16)
        for starts, splits in sizes
    )
    kernel = functools.partial(unfold_kernel, sizes, width)
    return call(kernel, outs, [], 10**9, 14, place, own, other)


def compute(layout, place, frame_rows, cot_rows, own, other, width, channels, in_channels):
    blocks = own.shape[0]
    unit = blocks * PAD
    times = 2 * (frame_rows.shape[0] // unit - 3)
    base = times * 2 * (channels // LANES) * width
    rows = base + times * (in_channels // LANES) * width
    scratch = [
        pltpu.VMEM(((times + 1) * unit, LANES), jnp.float32),
        pltpu.VMEM((3 * LANES, frame_rows.shape[1]), jnp.bfloat16),
        pltpu.VMEM((frame_rows.shape[0], 3 * LANES), jnp.float32),
        pltpu.VMEM((unit, LANES), jnp.float32),
        pltpu.VMEM(((times + 2) * unit, 3 * LANES), jnp.bfloat16),
        pltpu.VMEM((2 * channels, 9 * LANES), jnp.bfloat16),
        pltpu.VMEM((times * unit, 2 * channels), jnp.float32),
        pltpu.VMEM((cot_rows.shape[1], 3 * LANES), jnp.bfloat16),
        pltpu.VMEM((cot_rows.shape[0], 3 * LANES), jnp.float32),
        pltpu.VMEM((times // 2 * unit + unit, 3 * LANES), jnp.bfloat16),
        pltpu.VMEM((times // 2 * unit, 3 * LANES), jnp.bfloat16),
        pltpu.VMEM((9 * LANES, 2 * in_channels), jnp.bfloat16),
        pltpu.VMEM((times // 2 * unit, 2 * in_channels), jnp.float32),
    ]
    kernel = functools.partial(compute_kernel, layout, width, base)
    out = jax.ShapeDtypeStruct((blocks, rows, LANES), jnp.bfloat16)
    return call(kernel, out, scratch, 4 * 10**9, 32, place, frame_rows, cot_rows, own, other)


def add_parts(parts, sizes):
    space = pl.BlockSpec(memory_space=pltpu.VMEM)
    return pl.pallas_call(
        functools.partial(add_kernel, sizes),
        out_shape=tuple(
            jax.ShapeDtypeStruct((times, 2, width, splits * LANES), jnp.bfloat16)
            for times, splits, width in sizes
        ),
        in_specs=[space],
        out_specs=(space, space),
        compiler_params=pltpu.CompilerParams(vmem_limit_bytes=8 * 2**20),
    )(parts)


def ring(array, by):
    return lax.ppermute(array, RING, [(i, (i + by) % 4) for i in range(4)])


def flat(field):
    tiles = field.reshape(*field.shape[:3], -1, LANES)
    return tiles.transpose(0, 1, 3, 2, 4).reshape(-1, LANES)


def tiles_of(kernel):
    return kernel.T.reshape(2, -1, LANES).transpose(1, 0, 2)


def shards(frames, up_kernel, mix_kernel, cotangent):
    frame_count, height, width, in_channels = frames.shape
    out_channels = mix_kernel.shape[0] // 27
    xh, xl, core = lax.axis_index("xh"), lax.axis_index("xl"), lax.axis_index("core")
    ny, nz, nx = lax.axis_size("y"), lax.axis_size("z"), lax.axis_size(RING)
    part = out_channels // nx

    raw_mix = tiles_of(mix_kernel)
    mix_other = lax.ppermute(raw_mix, RING, [(0, 3), (3, 0), (1, 2), (2, 1)])
    up_column = lax.dynamic_index_in_dim(up_kernel.T, xl, 0, keepdims=False)
    up_tiles = up_column.reshape(-1, LANES)
    up_count = up_tiles.shape[0]
    up_half = (up_count + 1) // 2
    up_part = lax.dynamic_slice_in_dim(up_tiles, core * (up_count - up_half), up_half, 0)
    up_pairs = (up_half + 1) // 2
    up_part = jnp.pad(up_part, ((0, 2 * up_pairs - up_half), (0, 0))).reshape(-1, 2, LANES)

    mix_tiles = jnp.where(xh == core, raw_mix, mix_other)
    splits = out_channels // LANES
    pick_shape = (3, out_channels, 4 * part)
    tap = lax.broadcasted_iota(jnp.int32, pick_shape, 0)
    source = lax.broadcasted_iota(jnp.int32, pick_shape, 1)
    target = lax.broadcasted_iota(jnp.int32, pick_shape, 2)
    pair, side, place = target // (2 * part), target // part % 2, target % part
    wanted = (place // nz) * (4 * nz) + xh * (2 * nz) + (place % nz) * 2 + xl
    pick = (source == wanted) & (tap == side + 1 - pair)
    mix_part = jnp.einsum(
        "thwsjl,hslm->twjm",
        mix_tiles.reshape(3, 3, 3, splits, 2, LANES),
        pick.astype(jnp.bfloat16).reshape(3, splits, LANES, 4 * part),
        preferred_element_type=jnp.float32,
    ).astype(jnp.bfloat16)
    mix_part = mix_part.reshape(9, 2, 2, 2 * part).transpose(0, 2, 1, 3).reshape(-1, 2, LANES)

    frame_size, cot_size = 2 * (in_channels // LANES) * width, 2 * splits * width
    count = 2 * frame_count
    block = jnp.concatenate((flat(cotangent[3:]), flat(cotangent[:3]), flat(frames)), axis=0)
    planes = spread(jnp.concatenate((up_part, mix_part), axis=0), "z")
    early = (count - 3) * cot_size
    first = block.shape[0]
    following = shift(block[early : count * cot_size + frame_size], PLANES, -1)
    previous = shift(block[first - 2 * frame_size :], PLANES, 1)
    block = jnp.concatenate((block, following, previous), axis=0)
    blocks = (block, ring(block, 1), ring(block, -1), ring(block, 2))
    planes, block = lax.optimization_barrier((planes, block))
    blocks = jnp.stack(blocks)
    others = swap(blocks)
    last = first + 3 * cot_size + frame_size
    cot_starts = [early + time * cot_size for time in range(3)]
    cot_starts += [time * cot_size for time in range(count - 3)]
    cot_starts += [first + time * cot_size for time in range(3)]
    frame_starts = [last + time * frame_size for time in range(2)]
    frame_starts += [count * cot_size + time * frame_size for time in range(frame_count)]
    frame_starts += [first + 3 * cot_size]

    up_rows = planes[:, :up_pairs].transpose(1, 2, 0, 3).reshape(-1, LANES)
    mix_rows = planes[:, up_pairs:].transpose(1, 0, 2, 3).reshape(-1, LANES)
    own = spread(jnp.concatenate((up_rows, mix_rows), axis=0), "y")
    other = swap(own)
    layout = (nz, up_half, up_count, up_rows.shape[0])

    place = jnp.stack((xh, xl, core))
    sizes = ((tuple(frame_starts), in_channels // LANES), (tuple(cot_starts), splits))
    frame_rows, cot_rows = unfold(place, blocks, others, sizes, width)
    parts = compute(
        layout, place, frame_rows, cot_rows, own, other, width, out_channels, in_channels
    )
    parts = lax.all_to_all(parts, RING, 0, 0, tiled=True)
    outs = ((count, splits, width), (frame_count, in_channels // LANES, width))
    return add_parts(parts, outs)


def solution(mesh):
    planes, columns = mesh.devices.shape
    shape = (4, 2, planes // 8, 2, columns // 2)
    fine = Mesh(mesh.devices.reshape(shape), (*PLANES, *COLS))
    placed = P(PLANES, None, COLS, None)
    weights = P(None, PLANES)
    return jax.shard_map(
        shards,
        mesh=fine,
        in_specs=(placed, weights, weights, placed),
        out_specs=(placed, placed),
        check_vma=False,
    )
```

```python
import functools

import jax
import jax.numpy as jnp
from jax import lax
from jax.experimental import pallas as pl
from jax.experimental.pallas import tpu as pltpu
from jax.sharding import Mesh, PartitionSpec as P

PLANES = ("y", "xh", "z")
COLS = ("xl", "core")
RING = ("xh", "xl")
LANES = 128
PAD = 32
OFFSETS = (0, 3, 1, 2)


def shift(array, axis, by):
    devices = lax.axis_size(axis)
    pairs = [(i, i + by) for i in range(devices) if 0 <= i + by < devices]
    return lax.ppermute(array, axis, pairs)


def swap(array):
    return lax.ppermute(array, "core", [(0, 1), (1, 0)])


def spread(array, axis):
    count = lax.axis_size(axis)
    return lax.all_to_all(
        jnp.broadcast_to(array, (count, *array.shape)), axis, 0, 0, tiled=True
    )


def later(rows, by):
    if by == 0:
        return rows
    return pltpu.roll(rows, rows.shape[0] - by, 0)


def unfold_kernel(sizes, width, place, own, other, frame_rows, cot_rows):
    xl, core = place[1], place[2]
    blocks = own.shape[0]

    def step(block, _):
        side = (xl + (block + 1) // 2) % 2
        partner = jnp.where(xl == 0, (block + 2) % 4, block + 1 - 2 * (block % 2))
        left = jnp.where(core == 1, block, partner)
        right = jnp.where(core == 0, block, partner)
        has_left = 2 * side + core > 0
        has_right = 2 * side + core < 3
        for out, (starts, splits) in zip((frame_rows, cot_rows), sizes, strict=True):
            for time, start in enumerate(starts):
                target = pl.ds(pl.multiple_of((time * blocks + block) * PAD, PAD), PAD)
                for tile in range(2 * splits):
                    row, split = tile // splits, tile % splits
                    first = start + tile * width
                    low = other[left, first + width - 8 : first + width, :].astype(jnp.float32)
                    middle = own[block, first : first + width, :].astype(jnp.float32)
                    high = other[right, first : first + 8, :].astype(jnp.float32)
                    low = jnp.where(has_left, low, 0.0)
                    high = jnp.where(has_right, high, 0.0)
                    chunk = jnp.concatenate((low, middle, high), axis=0)
                    for tap in range(3):
                        lane = ((row * 3 + tap) * splits + split) * LANES
                        moved = chunk[6 + tap : 6 + tap + PAD].astype(jnp.bfloat16)
                        out[target, lane : lane + LANES] = moved
        return 0

    lax.fori_loop(0, blocks, step, 0)


def readers(layout, place, own, other):
    nz, up_half, up_count, up_size = layout
    lead = place[2] == 0

    def low(start, count):
        rows = slice(start, start + count)
        return jnp.where(lead, own[:, rows], other[:, rows])

    def high(start, count):
        rows = slice(start, start + count)
        return jnp.where(lead, other[:, rows], own[:, rows])

    def up_tile(kt, kh, kw, split, splits):
        tile = ((kt * 3 + kh) * 3 + kw) * splits + split
        if tile < up_half:
            value = low(tile * nz, nz)
        else:
            value = high((tile - (up_count - up_half)) * nz, nz)
        return value.reshape(-1, LANES)

    def mix_tile(kt, kw, pair):
        start = up_size + ((kt * 3 + kw) * 2 + pair) * 2 * nz
        return jnp.stack((low(start, 2 * nz), high(start, 2 * nz)), axis=1).reshape(-1, LANES)

    return up_tile, mix_tile


def forward_kernel(
    layout, width, place, rows, own, other, out, slope, up_w, ups, mask, hidden, mix_w, total
):
    up_tile, mix_tile = readers(layout, place, own, other)
    splits = rows.shape[1] // (6 * LANES)
    part, unit = up_w.shape[0] // 6, mask.shape[0]
    column = lax.broadcasted_iota(jnp.int32, (PAD, LANES), 0) - 1
    for block in range(out.shape[0]):
        side = (place[1] + (block + 1) // 2) % 2
        at = (2 * side + place[2]) * width + column
        inside = (at >= 0) & (at < 4 * width)
        mask[block * PAD : (block + 1) * PAD, :] = inside.astype(jnp.float32)
    for kt in range(3):
        for out_row in range(2):
            for row in range(2):
                for kw in range(3):
                    for split in range(splits):
                        at = kt * 2 * part + out_row * part
                        lane = ((row * 3 + kw) * splits + split) * LANES
                        up_w[at : at + part, lane : lane + LANES] = up_tile(
                            kt, row - out_row + 1, kw, split, splits
                        )
    step = 3 * unit

    def product(k, _):
        at = pl.ds(pl.multiple_of(k * step, step), step)
        ups[at, :] = lax.dot_general(
            rows[at, :], up_w[...], (((1,), (1,)), ((), ())), preferred_element_type=jnp.float32
        )
        return 0

    lax.fori_loop(0, rows.shape[0] // step, product, 0)
    inside = mask[...] > 0
    times = 2 * (rows.shape[0] // unit - 1) - 1
    for time in range(times):
        at = time // 2 * unit
        if time % 2 == 0:
            before = ups[at + unit : at + 2 * unit, :LANES] + ups[at : at + unit, 2 * LANES :]
        else:
            before = ups[at + unit : at + 2 * unit, LANES : 2 * LANES]
        sigma = jax.nn.sigmoid(before)
        if time < times - 1:
            value = jnp.where(inside, before * sigma, 0.0)
            for kw in range(3):
                hidden[time * unit : (time + 1) * unit, kw * LANES : (kw + 1) * LANES] = later(
                    value, kw
                ).astype(jnp.bfloat16)
        if time >= 2:
            slope[(time - 2) * unit : (time - 1) * unit, :] = jnp.where(
                inside, sigma * (1.0 + before * (1.0 - sigma)), 0.0
            )
    channels = mix_w.shape[0] // 2
    for kt in range(3):
        for out_row in range(2):
            for kw in range(3):
                mix_w[
                    out_row * channels : (out_row + 1) * channels,
                    (kt * 3 + kw) * LANES : (kt * 3 + kw + 1) * LANES,
                ] = mix_tile(kt, kw, out_row)
    total[...] = jnp.zeros_like(total)
    for kt in range(3):
        total[...] += lax.dot_general(
            hidden[kt * unit : kt * unit + total.shape[0], :],
            mix_w[:, kt * 3 * LANES : (kt + 1) * 3 * LANES],
            (((1,), (1,)), ((), ())),
            preferred_element_type=jnp.float32,
        )
    store(place, out, total, 0, total.shape[0] // unit, channels, width)


def store(place, out, total, base, times, channels, width):
    splits = channels // LANES
    for block in range(out.shape[0]):
        member = (2 * place[0] + place[1] + OFFSETS[block]) % 4
        for time in range(times):
            at = (time * out.shape[0] + block) * PAD
            for tile in range(2 * splits):
                first = base + (time * 2 * splits + tile) * width
                value = total[at : at + width, tile * LANES : (tile + 1) * LANES]
                out[member, first : first + width, :] = value.astype(jnp.bfloat16)


def add_kernel(sizes, parts, *outs):
    first = 0
    for out, (times, splits, width) in zip(outs, sizes, strict=True):
        for time in range(times):
            for row in range(2):
                for split in range(splits):
                    rows = slice(first, first + width)
                    total = parts[0, rows, :].astype(jnp.float32)
                    for member in range(1, parts.shape[0]):
                        total = total + parts[member, rows, :].astype(jnp.float32)
                    lanes = slice(split * LANES, (split + 1) * LANES)
                    out[time, row, :, lanes] = total.astype(jnp.bfloat16)
                    first += width


def backward_kernel(
    layout, width, place, rows, own, other, out, base, slope, mix_w, partial, evens, odds, up_w, total
):
    up_tile, mix_tile = readers(layout, place, own, other)
    channels = rows.shape[1] // 6
    unit = evens.shape[0] - total.shape[0]
    splits = up_w.shape[1] // (2 * LANES)
    part = LANES // 2
    for kt in range(3):
        for row in range(2):
            for shift_w in range(3):
                at = (row * 3 + shift_w) * channels
                mix_w[at : at + channels, kt * LANES : (kt + 1) * LANES] = mix_tile(
                    kt, 2 - shift_w, row
                )
    step = 3 * unit

    def product(k, _):
        at = pl.ds(pl.multiple_of(k * step, step), step)
        partial[at, :] = jnp.dot(rows[at, :], mix_w[...], preferred_element_type=jnp.float32)
        return 0

    lax.fori_loop(0, rows.shape[0] // step, product, 0)
    times = rows.shape[0] // unit - 2
    for time in range(times):
        at = time * unit
        hidden_grad = (
            partial[at + 2 * unit : at + 3 * unit, :LANES]
            + partial[at + unit : at + 2 * unit, LANES : 2 * LANES]
            + partial[at : at + unit, 2 * LANES :]
        )
        value = hidden_grad * slope[at : at + unit, :]
        target = evens if time % 2 == 0 else odds
        spot = time // 2 * unit
        for shift_w in range(3):
            target[spot : spot + unit, shift_w * LANES : (shift_w + 1) * LANES] = later(
                value, shift_w
            ).astype(jnp.bfloat16)
    for kt in range(3):
        for shift_w in range(3):
            for row in range(2):
                for out_row in range(2):
                    for split in range(splits):
                        at = (kt * 3 + shift_w) * LANES + row * part
                        lane = (out_row * splits + split) * LANES
                        up_w[at : at + part, lane : lane + LANES] = up_tile(
                            kt, out_row + 1 - row, 2 - shift_w, split, splits
                        )
    count = total.shape[0]
    lhs = (evens[:count, :], odds[:count, :], evens[unit : unit + count, :])
    total[...] = jnp.zeros_like(total)
    for kt in range(3):
        total[...] += jnp.dot(
            lhs[kt],
            up_w[kt * 3 * LANES : (kt + 1) * 3 * LANES, :],
            preferred_element_type=jnp.float32,
        )
    store(place, out, total, base, count // unit, splits * LANES, width)


def compute_kernel(
    layout, width, base, place, frame_rows, cot_rows, own, other, out, slope, *scratch
):
    forward_kernel(layout, width, place, frame_rows, own, other, out, slope, *scratch[:6])
    backward_kernel(layout, width, place, cot_rows, own, other, out, base, slope, *scratch[6:])


def call(kernel, outs, scratch, flops, megabytes, place, *operands):
    space = pl.BlockSpec(memory_space=pltpu.VMEM)
    return pl.pallas_call(
        kernel,
        out_shape=outs,
        in_specs=[pl.BlockSpec(memory_space=pltpu.SMEM)] + [space] * len(operands),
        out_specs=jax.tree.map(lambda _: space, outs),
        scratch_shapes=scratch,
        compiler_params=pltpu.CompilerParams(vmem_limit_bytes=megabytes * 2**20),
        cost_estimate=pl.CostEstimate(flops=flops, bytes_accessed=8 * 2**20, transcendentals=0),
    )(place, *operands)


def unfold(place, own, other, sizes, width):
    unit = own.shape[0] * PAD
    outs = tuple(
        jax.ShapeDtypeStruct((len(starts) * unit, 6 * splits * LANES), jnp.bfloat16)
        for starts, splits in sizes
    )
    kernel = functools.partial(unfold_kernel, sizes, width)
    return call(kernel, outs, [], 10**9, 14, place, own, other)


def compute(layout, place, frame_rows, cot_rows, own, other, width, channels, in_channels):
    blocks = own.shape[0]
    unit = blocks * PAD
    times = 2 * (frame_rows.shape[0] // unit - 3)
    base = times * 2 * (channels // LANES) * width
    rows = base + times * (in_channels // LANES) * width
    scratch = [
        pltpu.VMEM(((times + 1) * unit, LANES), jnp.float32),
        pltpu.VMEM((3 * LANES, frame_rows.shape[1]), jnp.bfloat16),
        pltpu.VMEM((frame_rows.shape[0], 3 * LANES), jnp.float32),
        pltpu.VMEM((unit, LANES), jnp.float32),
        pltpu.VMEM(((times + 2) * unit, 3 * LANES), jnp.bfloat16),
        pltpu.VMEM((2 * channels, 9 * LANES), jnp.bfloat16),
        pltpu.VMEM((times * unit, 2 * channels), jnp.float32),
        pltpu.VMEM((cot_rows.shape[1], 3 * LANES), jnp.bfloat16),
        pltpu.VMEM((cot_rows.shape[0], 3 * LANES), jnp.float32),
        pltpu.VMEM((times // 2 * unit + unit, 3 * LANES), jnp.bfloat16),
        pltpu.VMEM((times // 2 * unit, 3 * LANES), jnp.bfloat16),
        pltpu.VMEM((9 * LANES, 2 * in_channels), jnp.bfloat16),
        pltpu.VMEM((times // 2 * unit, 2 * in_channels), jnp.float32),
    ]
    kernel = functools.partial(compute_kernel, layout, width, base)
    out = jax.ShapeDtypeStruct((blocks, rows, LANES), jnp.bfloat16)
    return call(kernel, out, scratch, 4 * 10**9, 32, place, frame_rows, cot_rows, own, other)


def add_parts(parts, sizes):
    space = pl.BlockSpec(memory_space=pltpu.VMEM)
    return pl.pallas_call(
        functools.partial(add_kernel, sizes),
        out_shape=tuple(
            jax.ShapeDtypeStruct((times, 2, width, splits * LANES), jnp.bfloat16)
            for times, splits, width in sizes
        ),
        in_specs=[space],
        out_specs=(space, space),
        compiler_params=pltpu.CompilerParams(vmem_limit_bytes=8 * 2**20),
    )(parts)


def ring(array, by):
    return lax.ppermute(array, RING, [(i, (i + by) % 4) for i in range(4)])


def flat(field):
    tiles = field.reshape(*field.shape[:3], -1, LANES)
    return tiles.transpose(0, 1, 3, 2, 4).reshape(-1, LANES)


def tiles_of(kernel):
    return kernel.T.reshape(2, -1, LANES).transpose(1, 0, 2)


def shards(frames, up_kernel, mix_kernel, cotangent):
    frame_count, height, width, in_channels = frames.shape
    out_channels = mix_kernel.shape[0] // 27
    xh, xl, core = lax.axis_index("xh"), lax.axis_index("xl"), lax.axis_index("core")
    ny, nz, nx = lax.axis_size("y"), lax.axis_size("z"), lax.axis_size(RING)
    part = out_channels // nx

    raw_mix = tiles_of(mix_kernel)
    mix_other = lax.ppermute(raw_mix, RING, [(0, 3), (3, 0), (1, 2), (2, 1)])
    up_column = lax.dynamic_index_in_dim(up_kernel.T, xl, 0, keepdims=False)
    up_tiles = up_column.reshape(-1, LANES)
    up_count = up_tiles.shape[0]
    up_half = (up_count + 1) // 2
    up_part = lax.dynamic_slice_in_dim(up_tiles, core * (up_count - up_half), up_half, 0)
    up_pairs = (up_half + 1) // 2
    up_part = jnp.pad(up_part, ((0, 2 * up_pairs - up_half), (0, 0))).reshape(-1, 2, LANES)

    mix_tiles = jnp.where(xh == core, raw_mix, mix_other)
    splits = out_channels // LANES
    pick_shape = (3, out_channels, 4 * part)
    tap = lax.broadcasted_iota(jnp.int32, pick_shape, 0)
    source = lax.broadcasted_iota(jnp.int32, pick_shape, 1)
    target = lax.broadcasted_iota(jnp.int32, pick_shape, 2)
    pair, side, place = target // (2 * part), target // part % 2, target % part
    wanted = (place // nz) * (4 * nz) + xh * (2 * nz) + (place % nz) * 2 + xl
    pick = (source == wanted) & (tap == side + 1 - pair)
    mix_part = jnp.einsum(
        "thwsjl,hslm->twjm",
        mix_tiles.reshape(3, 3, 3, splits, 2, LANES),
        pick.astype(jnp.bfloat16).reshape(3, splits, LANES, 4 * part),
        preferred_element_type=jnp.float32,
    ).astype(jnp.bfloat16)
    mix_part = mix_part.reshape(9, 2, 2, 2 * part).transpose(0, 2, 1, 3).reshape(-1, 2, LANES)

    frame_size, cot_size = 2 * (in_channels // LANES) * width, 2 * splits * width
    count = 2 * frame_count
    block = jnp.concatenate((flat(cotangent[3:]), flat(cotangent[:3]), flat(frames)), axis=0)
    early = (count - 3) * cot_size
    first = block.shape[0]
    payload, following, previous = lax.optimization_barrier(
        (
            jnp.concatenate((up_part, mix_part), axis=0),
            shift(block[early : count * cot_size + frame_size], PLANES, -1),
            shift(block[first - 2 * frame_size :], PLANES, 1),
        )
    )
    planes = spread(payload, "z")
    block = jnp.concatenate((block, following, previous), axis=0)
    blocks = (block, ring(block, 1), ring(block, -1), ring(block, 2))
    planes, block = lax.optimization_barrier((planes, block))
    blocks = jnp.stack(blocks)
    others = swap(blocks)
    last = first + 3 * cot_size + frame_size
    cot_starts = [early + time * cot_size for time in range(3)]
    cot_starts += [time * cot_size for time in range(count - 3)]
    cot_starts += [first + time * cot_size for time in range(3)]
    frame_starts = [last + time * frame_size for time in range(2)]
    frame_starts += [count * cot_size + time * frame_size for time in range(frame_count)]
    frame_starts += [first + 3 * cot_size]

    up_rows = planes[:, :up_pairs].transpose(1, 2, 0, 3).reshape(-1, LANES)
    mix_rows = planes[:, up_pairs:].transpose(1, 0, 2, 3).reshape(-1, LANES)
    own = spread(jnp.concatenate((up_rows, mix_rows), axis=0), "y")
    other = swap(own)
    layout = (nz, up_half, up_count, up_rows.shape[0])

    place = jnp.stack((xh, xl, core))
    sizes = ((tuple(frame_starts), in_channels // LANES), (tuple(cot_starts), splits))
    frame_rows, cot_rows = unfold(place, blocks, others, sizes, width)
    parts = compute(
        layout, place, frame_rows, cot_rows, own, other, width, out_channels, in_channels
    )
    parts = lax.all_to_all(parts, RING, 0, 0, tiled=True)
    outs = ((count, splits, width), (frame_count, in_channels // LANES, width))
    return add_parts(parts, outs)


def solution(mesh):
    planes, columns = mesh.devices.shape
    shape = (4, 2, planes // 8, 2, columns // 2)
    fine = Mesh(mesh.devices.reshape(shape), (*PLANES, *COLS))
    placed = P(PLANES, None, COLS, None)
    weights = P(None, PLANES)
    return jax.shard_map(
        shards,
        mesh=fine,
        in_specs=(placed, weights, weights, placed),
        out_specs=(placed, placed),
        check_vma=False,
    )
```

```python
import functools

import jax
import jax.numpy as jnp
from jax import lax
from jax.experimental import pallas as pl
from jax.experimental.pallas import tpu as pltpu
from jax.sharding import Mesh, PartitionSpec as P

PLANES = ("y", "xh", "z")
COLS = ("xl", "core")
RING = ("xh", "xl")
LANES = 128
PAD = 32
OFFSETS = (0, 3, 1, 2)


def shift(array, axis, by):
    devices = lax.axis_size(axis)
    pairs = [(i, i + by) for i in range(devices) if 0 <= i + by < devices]
    return lax.ppermute(array, axis, pairs)


def swap(array):
    return lax.ppermute(array, "core", [(0, 1), (1, 0)])


def spread(array, axis):
    count = lax.axis_size(axis)
    return lax.all_to_all(
        jnp.broadcast_to(array, (count, *array.shape)), axis, 0, 0, tiled=True
    )


def later(rows, by):
    if by == 0:
        return rows
    return pltpu.roll(rows, rows.shape[0] - by, 0)


def unfold_kernel(sizes, width, place, own, other, frame_rows, cot_rows):
    xl, core = place[1], place[2]
    blocks = own.shape[0]

    def step(block, _):
        side = (xl + (block + 1) // 2) % 2
        partner = jnp.where(xl == 0, (block + 2) % 4, block + 1 - 2 * (block % 2))
        left = jnp.where(core == 1, block, partner)
        right = jnp.where(core == 0, block, partner)
        has_left = 2 * side + core > 0
        has_right = 2 * side + core < 3
        for out, (starts, splits) in zip((frame_rows, cot_rows), sizes, strict=True):
            for time, start in enumerate(starts):
                target = pl.ds(pl.multiple_of((time * blocks + block) * PAD, PAD), PAD)
                for tile in range(2 * splits):
                    row, split = tile // splits, tile % splits
                    first = start + tile * width
                    low = other[left, first + width - 8 : first + width, :].astype(jnp.float32)
                    middle = own[block, first : first + width, :].astype(jnp.float32)
                    high = other[right, first : first + 8, :].astype(jnp.float32)
                    low = jnp.where(has_left, low, 0.0)
                    high = jnp.where(has_right, high, 0.0)
                    chunk = jnp.concatenate((low, middle, high), axis=0)
                    for tap in range(3):
                        lane = ((row * 3 + tap) * splits + split) * LANES
                        moved = chunk[6 + tap : 6 + tap + PAD].astype(jnp.bfloat16)
                        out[target, lane : lane + LANES] = moved
        return 0

    lax.fori_loop(0, blocks, step, 0)


def readers(layout, place, own, other):
    nz, up_half, up_count, up_size = layout
    lead = place[2] == 0

    def low(start, count):
        rows = slice(start, start + count)
        return jnp.where(lead, own[:, rows], other[:, rows])

    def high(start, count):
        rows = slice(start, start + count)
        return jnp.where(lead, other[:, rows], own[:, rows])

    def up_tile(kt, kh, kw, split, splits):
        tile = ((kt * 3 + kh) * 3 + kw) * splits + split
        if tile < up_half:
            value = low(tile * nz, nz)
        else:
            value = high((tile - (up_count - up_half)) * nz, nz)
        return value.reshape(-1, LANES)

    def both(tile):
        start = up_size + tile * 2 * nz
        return jnp.stack((low(start, 2 * nz), high(start, 2 * nz)), axis=1).reshape(-1, LANES)

    def mix_tile(kt, kw, pair):
        at = kt * 3 + kw
        if pair == 1:
            return both(at)
        ahead = pltpu.roll(both(at).astype(jnp.float32), LANES // 2, 1)
        last = both(9 + at // 2).astype(jnp.float32)
        if at % 2 == 0:
            last = pltpu.roll(last, LANES // 2, 1)
        lane = lax.broadcasted_iota(jnp.int32, ahead.shape, 1)
        return jnp.where(lane < LANES // 2, ahead, last).astype(jnp.bfloat16)

    return up_tile, mix_tile


def forward_kernel(
    layout, width, place, rows, own, other, out, slope, up_w, ups, mask, hidden, mix_w, total
):
    up_tile, mix_tile = readers(layout, place, own, other)
    splits = rows.shape[1] // (6 * LANES)
    part, unit = up_w.shape[0] // 6, mask.shape[0]
    column = lax.broadcasted_iota(jnp.int32, (PAD, LANES), 0) - 1
    for block in range(out.shape[0]):
        side = (place[1] + (block + 1) // 2) % 2
        at = (2 * side + place[2]) * width + column
        inside = (at >= 0) & (at < 4 * width)
        mask[block * PAD : (block + 1) * PAD, :] = inside.astype(jnp.float32)
    for kt in range(3):
        for out_row in range(2):
            for row in range(2):
                for kw in range(3):
                    for split in range(splits):
                        at = kt * 2 * part + out_row * part
                        lane = ((row * 3 + kw) * splits + split) * LANES
                        up_w[at : at + part, lane : lane + LANES] = up_tile(
                            kt, row - out_row + 1, kw, split, splits
                        )
    step = 3 * unit

    def product(k, _):
        at = pl.ds(pl.multiple_of(k * step, step), step)
        ups[at, :] = lax.dot_general(
            rows[at, :], up_w[...], (((1,), (1,)), ((), ())), preferred_element_type=jnp.float32
        )
        return 0

    lax.fori_loop(0, rows.shape[0] // step, product, 0)
    inside = mask[...] > 0
    times = 2 * (rows.shape[0] // unit - 1) - 1
    for time in range(times):
        at = time // 2 * unit
        if time % 2 == 0:
            before = ups[at + unit : at + 2 * unit, :LANES] + ups[at : at + unit, 2 * LANES :]
        else:
            before = ups[at + unit : at + 2 * unit, LANES : 2 * LANES]
        sigma = jax.nn.sigmoid(before)
        if time < times - 1:
            value = jnp.where(inside, before * sigma, 0.0)
            for kw in range(3):
                hidden[time * unit : (time + 1) * unit, kw * LANES : (kw + 1) * LANES] = later(
                    value, kw
                ).astype(jnp.bfloat16)
        if time >= 2:
            slope[(time - 2) * unit : (time - 1) * unit, :] = jnp.where(
                inside, sigma * (1.0 + before * (1.0 - sigma)), 0.0
            )
    channels = mix_w.shape[0] // 2
    for kt in range(3):
        for out_row in range(2):
            for kw in range(3):
                mix_w[
                    out_row * channels : (out_row + 1) * channels,
                    (kt * 3 + kw) * LANES : (kt * 3 + kw + 1) * LANES,
                ] = mix_tile(kt, kw, out_row)
    total[...] = jnp.zeros_like(total)
    for kt in range(3):
        total[...] += lax.dot_general(
            hidden[kt * unit : kt * unit + total.shape[0], :],
            mix_w[:, kt * 3 * LANES : (kt + 1) * 3 * LANES],
            (((1,), (1,)), ((), ())),
            preferred_element_type=jnp.float32,
        )
    store(place, out, total, 0, total.shape[0] // unit, channels, width)


def store(place, out, total, base, times, channels, width):
    splits = channels // LANES
    for block in range(out.shape[0]):
        member = (2 * place[0] + place[1] + OFFSETS[block]) % 4
        for time in range(times):
            at = (time * out.shape[0] + block) * PAD
            for tile in range(2 * splits):
                first = base + (time * 2 * splits + tile) * width
                value = total[at : at + width, tile * LANES : (tile + 1) * LANES]
                out[member, first : first + width, :] = value.astype(jnp.bfloat16)


def add_kernel(sizes, parts, *outs):
    first = 0
    for out, (times, splits, width) in zip(outs, sizes, strict=True):
        for time in range(times):
            for row in range(2):
                for split in range(splits):
                    rows = slice(first, first + width)
                    total = parts[0, rows, :].astype(jnp.float32)
                    for member in range(1, parts.shape[0]):
                        total = total + parts[member, rows, :].astype(jnp.float32)
                    lanes = slice(split * LANES, (split + 1) * LANES)
                    out[time, row, :, lanes] = total.astype(jnp.bfloat16)
                    first += width


def backward_kernel(
    layout, width, place, rows, own, other, out, base, slope, forward_w, mix_w, partial, evens, odds, up_w, total
):
    up_tile, _ = readers(layout, place, own, other)
    channels = rows.shape[1] // 6
    unit = evens.shape[0] - total.shape[0]
    splits = up_w.shape[1] // (2 * LANES)
    part = LANES // 2
    for kt in range(3):
        for row in range(2):
            for shift_w in range(3):
                at = (row * 3 + shift_w) * channels
                lane = (kt * 3 + 2 - shift_w) * LANES
                mix_w[at : at + channels, kt * LANES : (kt + 1) * LANES] = forward_w[
                    row * channels : (row + 1) * channels, lane : lane + LANES
                ]
    step = 3 * unit

    def product(k, _):
        at = pl.ds(pl.multiple_of(k * step, step), step)
        partial[at, :] = jnp.dot(rows[at, :], mix_w[...], preferred_element_type=jnp.float32)
        return 0

    lax.fori_loop(0, rows.shape[0] // step, product, 0)
    times = rows.shape[0] // unit - 2
    for time in range(times):
        at = time * unit
        hidden_grad = (
            partial[at + 2 * unit : at + 3 * unit, :LANES]
            + partial[at + unit : at + 2 * unit, LANES : 2 * LANES]
            + partial[at : at + unit, 2 * LANES :]
        )
        value = hidden_grad * slope[at : at + unit, :]
        target = evens if time % 2 == 0 else odds
        spot = time // 2 * unit
        for shift_w in range(3):
            target[spot : spot + unit, shift_w * LANES : (shift_w + 1) * LANES] = later(
                value, shift_w
            ).astype(jnp.bfloat16)
    for kt in range(3):
        for shift_w in range(3):
            for row in range(2):
                for out_row in range(2):
                    for split in range(splits):
                        at = (kt * 3 + shift_w) * LANES + row * part
                        lane = (out_row * splits + split) * LANES
                        up_w[at : at + part, lane : lane + LANES] = up_tile(
                            kt, out_row + 1 - row, 2 - shift_w, split, splits
                        )
    count = total.shape[0]
    lhs = (evens[:count, :], odds[:count, :], evens[unit : unit + count, :])
    total[...] = jnp.zeros_like(total)
    for kt in range(3):
        total[...] += jnp.dot(
            lhs[kt],
            up_w[kt * 3 * LANES : (kt + 1) * 3 * LANES, :],
            preferred_element_type=jnp.float32,
        )
    store(place, out, total, base, count // unit, splits * LANES, width)


def compute_kernel(
    layout, width, base, place, frame_rows, cot_rows, own, other, out, slope, *scratch
):
    forward_kernel(layout, width, place, frame_rows, own, other, out, slope, *scratch[:6])
    backward_kernel(
        layout, width, place, cot_rows, own, other, out, base, slope, scratch[4], *scratch[6:]
    )


def call(kernel, outs, scratch, flops, megabytes, place, *operands):
    space = pl.BlockSpec(memory_space=pltpu.VMEM)
    return pl.pallas_call(
        kernel,
        out_shape=outs,
        in_specs=[pl.BlockSpec(memory_space=pltpu.SMEM)] + [space] * len(operands),
        out_specs=jax.tree.map(lambda _: space, outs),
        scratch_shapes=scratch,
        compiler_params=pltpu.CompilerParams(vmem_limit_bytes=megabytes * 2**20),
        cost_estimate=pl.CostEstimate(flops=flops, bytes_accessed=8 * 2**20, transcendentals=0),
    )(place, *operands)


def unfold(place, own, other, sizes, width):
    unit = own.shape[0] * PAD
    outs = tuple(
        jax.ShapeDtypeStruct((len(starts) * unit, 6 * splits * LANES), jnp.bfloat16)
        for starts, splits in sizes
    )
    kernel = functools.partial(unfold_kernel, sizes, width)
    return call(kernel, outs, [], 10**9, 14, place, own, other)


def compute(layout, place, frame_rows, cot_rows, own, other, width, channels, in_channels):
    blocks = own.shape[0]
    unit = blocks * PAD
    times = 2 * (frame_rows.shape[0] // unit - 3)
    base = times * 2 * (channels // LANES) * width
    rows = base + times * (in_channels // LANES) * width
    scratch = [
        pltpu.VMEM(((times + 1) * unit, LANES), jnp.float32),
        pltpu.VMEM((3 * LANES, frame_rows.shape[1]), jnp.bfloat16),
        pltpu.VMEM((frame_rows.shape[0], 3 * LANES), jnp.float32),
        pltpu.VMEM((unit, LANES), jnp.float32),
        pltpu.VMEM(((times + 2) * unit, 3 * LANES), jnp.bfloat16),
        pltpu.VMEM((2 * channels, 9 * LANES), jnp.bfloat16),
        pltpu.VMEM((times * unit, 2 * channels), jnp.float32),
        pltpu.VMEM((cot_rows.shape[1], 3 * LANES), jnp.bfloat16),
        pltpu.VMEM((cot_rows.shape[0], 3 * LANES), jnp.float32),
        pltpu.VMEM((times // 2 * unit + unit, 3 * LANES), jnp.bfloat16),
        pltpu.VMEM((times // 2 * unit, 3 * LANES), jnp.bfloat16),
        pltpu.VMEM((9 * LANES, 2 * in_channels), jnp.bfloat16),
        pltpu.VMEM((times // 2 * unit, 2 * in_channels), jnp.float32),
    ]
    kernel = functools.partial(compute_kernel, layout, width, base)
    out = jax.ShapeDtypeStruct((blocks, rows, LANES), jnp.bfloat16)
    return call(kernel, out, scratch, 4 * 10**9, 32, place, frame_rows, cot_rows, own, other)


def add_parts(parts, sizes):
    space = pl.BlockSpec(memory_space=pltpu.VMEM)
    return pl.pallas_call(
        functools.partial(add_kernel, sizes),
        out_shape=tuple(
            jax.ShapeDtypeStruct((times, 2, width, splits * LANES), jnp.bfloat16)
            for times, splits, width in sizes
        ),
        in_specs=[space],
        out_specs=(space, space),
        compiler_params=pltpu.CompilerParams(vmem_limit_bytes=8 * 2**20),
    )(parts)


def ring(array, by):
    return lax.ppermute(array, RING, [(i, (i + by) % 4) for i in range(4)])


def flat(field):
    tiles = field.reshape(*field.shape[:3], -1, LANES)
    return tiles.transpose(0, 1, 3, 2, 4).reshape(-1, LANES)


def tiles_of(kernel):
    return kernel.reshape(-1, LANES, 2).transpose(0, 2, 1)


def shards(frames, up_kernel, mix_kernel, cotangent):
    frame_count, height, width, in_channels = frames.shape
    out_channels = mix_kernel.shape[0] // 27
    xh, xl, core = lax.axis_index("xh"), lax.axis_index("xl"), lax.axis_index("core")
    ny, nz, nx = lax.axis_size("y"), lax.axis_size("z"), lax.axis_size(RING)
    part = out_channels // nx

    raw_mix = tiles_of(mix_kernel)
    mix_other = lax.ppermute(raw_mix, RING, [(0, 3), (3, 0), (1, 2), (2, 1)])
    up_column = lax.dynamic_index_in_dim(up_kernel.T, xl, 0, keepdims=False)
    up_tiles = up_column.reshape(-1, LANES)
    up_count = up_tiles.shape[0]
    up_half = (up_count + 1) // 2
    up_part = lax.dynamic_slice_in_dim(up_tiles, core * (up_count - up_half), up_half, 0)
    up_pairs = (up_half + 1) // 2
    up_part = jnp.pad(up_part, ((0, 2 * up_pairs - up_half), (0, 0))).reshape(-1, 2, LANES)

    mix_tiles = jnp.where(xh == core, raw_mix, mix_other)
    splits = out_channels // LANES
    pick_shape = (2, out_channels, 2 * part)
    slot = lax.broadcasted_iota(jnp.int32, pick_shape, 0)
    source = lax.broadcasted_iota(jnp.int32, pick_shape, 1)
    target = lax.broadcasted_iota(jnp.int32, pick_shape, 2)
    side, spot = target // part, target % part
    wanted = (spot // nz) * (4 * nz) + xh * (2 * nz) + (spot % nz) * 2 + xl
    pick = ((source == wanted) & (slot == side)).astype(jnp.bfloat16)
    pick = pick.reshape(2, splits, LANES, 2 * part)
    taps = mix_tiles.reshape(3, 3, 3, splits, 2, LANES).transpose(0, 2, 1, 3, 4, 5)
    taps = taps.reshape(9, 3, splits, 2, LANES)
    last = jnp.pad(taps[:, 2], ((0, 1), (0, 0), (0, 0), (0, 0))).reshape(5, 2, splits, 2, LANES)
    mix_part = jnp.einsum(
        "thsjl,hslm->tjm",
        jnp.concatenate((taps[:, :2], last), axis=0),
        pick,
        preferred_element_type=jnp.float32,
    ).astype(jnp.bfloat16)

    frame_size, cot_size = 2 * (in_channels // LANES) * width, 2 * splits * width
    count = 2 * frame_count
    block = jnp.concatenate((flat(cotangent[3:]), flat(cotangent[:3]), flat(frames)), axis=0)
    early = (count - 3) * cot_size
    first = block.shape[0]
    payload, following, previous = lax.optimization_barrier(
        (
            jnp.concatenate((up_part, mix_part), axis=0),
            shift(block[early : count * cot_size + frame_size], PLANES, -1),
            shift(block[first - 2 * frame_size :], PLANES, 1),
        )
    )
    planes = spread(payload, "z")
    block = jnp.concatenate((block, following, previous), axis=0)
    blocks = (block, ring(block, 1), ring(block, -1), ring(block, 2))
    planes, block = lax.optimization_barrier((planes, block))
    blocks = jnp.stack(blocks)
    others = swap(blocks)
    last = first + 3 * cot_size + frame_size
    cot_starts = [early + time * cot_size for time in range(3)]
    cot_starts += [time * cot_size for time in range(count - 3)]
    cot_starts += [first + time * cot_size for time in range(3)]
    frame_starts = [last + time * frame_size for time in range(2)]
    frame_starts += [count * cot_size + time * frame_size for time in range(frame_count)]
    frame_starts += [first + 3 * cot_size]

    up_rows = planes[:, :up_pairs].transpose(1, 2, 0, 3).reshape(-1, LANES)
    mix_rows = planes[:, up_pairs:].transpose(1, 0, 2, 3).reshape(-1, LANES)
    own = spread(jnp.concatenate((up_rows, mix_rows), axis=0), "y")
    other = swap(own)
    layout = (nz, up_half, up_count, up_rows.shape[0])

    place = jnp.stack((xh, xl, core))
    sizes = ((tuple(frame_starts), in_channels // LANES), (tuple(cot_starts), splits))
    frame_rows, cot_rows = unfold(place, blocks, others, sizes, width)
    parts = compute(
        layout, place, frame_rows, cot_rows, own, other, width, out_channels, in_channels
    )
    parts = lax.all_to_all(parts, RING, 0, 0, tiled=True)
    outs = ((count, splits, width), (frame_count, in_channels // LANES, width))
    return add_parts(parts, outs)


def solution(mesh):
    planes, columns = mesh.devices.shape
    shape = (4, 2, planes // 8, 2, columns // 2)
    fine = Mesh(mesh.devices.reshape(shape), (*PLANES, *COLS))
    placed = P(PLANES, None, COLS, None)
    weights = P(None, PLANES)
    return jax.shard_map(
        shards,
        mesh=fine,
        in_specs=(placed, weights, weights, placed),
        out_specs=(placed, placed),
        check_vma=False,
    )
```

```python
import functools

import jax
import jax.numpy as jnp
from jax import lax
from jax.experimental import pallas as pl
from jax.experimental.pallas import tpu as pltpu
from jax.sharding import Mesh, PartitionSpec as P

PLANES = ("y", "xh", "z")
COLS = ("xl", "core")
RING = ("xh", "xl")
LANES = 128
PAD = 32


def shift(array, axis, by):
    devices = lax.axis_size(axis)
    pairs = [(i, i + by) for i in range(devices) if 0 <= i + by < devices]
    return lax.ppermute(array, axis, pairs)


def swap(array):
    return lax.ppermute(array, "core", [(0, 1), (1, 0)])


def spread(array, axis):
    count = lax.axis_size(axis)
    return lax.all_to_all(
        jnp.broadcast_to(array, (count, *array.shape)), axis, 0, 0, tiled=True
    )


def later(rows, by):
    if by == 0:
        return rows
    return pltpu.roll(rows, rows.shape[0] - by, 0)


def unfold_kernel(sizes, width, place, own, other, frame_rows, cot_rows):
    xl, core = place[1], place[2]
    blocks = own.shape[0]

    def step(block, _):
        side = (xl + (block + 1) // 2) % 2
        partner = jnp.where(xl == 0, (block + 2) % 4, block + 1 - 2 * (block % 2))
        left = jnp.where(core == 1, block, partner)
        right = jnp.where(core == 0, block, partner)
        has_left = 2 * side + core > 0
        has_right = 2 * side + core < 3
        for out, (starts, splits) in zip((frame_rows, cot_rows), sizes, strict=True):
            for time, start in enumerate(starts):
                target = pl.ds(pl.multiple_of((time * blocks + block) * PAD, PAD), PAD)
                for tile in range(2 * splits):
                    row, split = tile // splits, tile % splits
                    first = start + tile * width
                    low = other[left, first + width - 8 : first + width, :].astype(jnp.float32)
                    middle = own[block, first : first + width, :].astype(jnp.float32)
                    high = other[right, first : first + 8, :].astype(jnp.float32)
                    low = jnp.where(has_left, low, 0.0)
                    high = jnp.where(has_right, high, 0.0)
                    chunk = jnp.concatenate((low, middle, high), axis=0)
                    for tap in range(3):
                        lane = ((row * 3 + tap) * splits + split) * LANES
                        moved = chunk[6 + tap : 6 + tap + PAD].astype(jnp.bfloat16)
                        out[target, lane : lane + LANES] = moved
        return 0

    lax.fori_loop(0, blocks, step, 0)


def readers(layout, place, own, other):
    nz, up_half, up_count, up_size = layout
    lead = place[2] == 0

    def low(start, count):
        rows = slice(start, start + count)
        return jnp.where(lead, own[:, rows], other[:, rows])

    def high(start, count):
        rows = slice(start, start + count)
        return jnp.where(lead, other[:, rows], own[:, rows])

    def up_tile(kt, kh, kw, split, splits):
        tile = ((kt * 3 + kh) * 3 + kw) * splits + split
        if tile < up_half:
            value = low(tile * nz, nz)
        else:
            value = high((tile - (up_count - up_half)) * nz, nz)
        return value.reshape(-1, LANES)

    def both(tile):
        start = up_size + tile * 2 * nz
        return jnp.stack((low(start, 2 * nz), high(start, 2 * nz)), axis=1).reshape(-1, LANES)

    def mix_tile(kt, kw, pair):
        at = kt * 3 + kw
        if pair == 1:
            return both(at)
        ahead = pltpu.roll(both(at).astype(jnp.float32), LANES // 2, 1)
        last = both(9 + at // 2).astype(jnp.float32)
        if at % 2 == 0:
            last = pltpu.roll(last, LANES // 2, 1)
        lane = lax.broadcasted_iota(jnp.int32, ahead.shape, 1)
        return jnp.where(lane < LANES // 2, ahead, last).astype(jnp.bfloat16)

    return up_tile, mix_tile


def forward_kernel(
    layout, width, place, rows, own, other, outs, slope, up_w, ups, mask, hidden, mix_w, total
):
    up_tile, mix_tile = readers(layout, place, own, other)
    splits = rows.shape[1] // (6 * LANES)
    part, unit = up_w.shape[0] // 6, mask.shape[0]
    column = lax.broadcasted_iota(jnp.int32, (PAD, LANES), 0) - 1
    for block in range(len(outs)):
        side = (place[1] + (block + 1) // 2) % 2
        at = (2 * side + place[2]) * width + column
        inside = (at >= 0) & (at < 4 * width)
        mask[block * PAD : (block + 1) * PAD, :] = inside.astype(jnp.float32)
    for kt in range(3):
        for out_row in range(2):
            for row in range(2):
                for kw in range(3):
                    for split in range(splits):
                        at = kt * 2 * part + out_row * part
                        lane = ((row * 3 + kw) * splits + split) * LANES
                        up_w[at : at + part, lane : lane + LANES] = up_tile(
                            kt, row - out_row + 1, kw, split, splits
                        )
    step = 3 * unit

    def product(k, _):
        at = pl.ds(pl.multiple_of(k * step, step), step)
        ups[at, :] = lax.dot_general(
            rows[at, :], up_w[...], (((1,), (1,)), ((), ())), preferred_element_type=jnp.float32
        )
        return 0

    lax.fori_loop(0, rows.shape[0] // step, product, 0)
    inside = mask[...] > 0
    times = 2 * (rows.shape[0] // unit - 1) - 1
    for time in range(times):
        at = time // 2 * unit
        if time % 2 == 0:
            before = ups[at + unit : at + 2 * unit, :LANES] + ups[at : at + unit, 2 * LANES :]
        else:
            before = ups[at + unit : at + 2 * unit, LANES : 2 * LANES]
        sigma = jax.nn.sigmoid(before)
        if time < times - 1:
            value = jnp.where(inside, before * sigma, 0.0)
            for kw in range(3):
                hidden[time * unit : (time + 1) * unit, kw * LANES : (kw + 1) * LANES] = later(
                    value, kw
                ).astype(jnp.bfloat16)
        if time >= 2:
            slope[(time - 2) * unit : (time - 1) * unit, :] = jnp.where(
                inside, sigma * (1.0 + before * (1.0 - sigma)), 0.0
            )
    channels = mix_w.shape[0] // 2
    for kt in range(3):
        for out_row in range(2):
            for kw in range(3):
                mix_w[
                    out_row * channels : (out_row + 1) * channels,
                    (kt * 3 + kw) * LANES : (kt * 3 + kw + 1) * LANES,
                ] = mix_tile(kt, kw, out_row)
    total[...] = jnp.zeros_like(total)
    for kt in range(3):
        total[...] += lax.dot_general(
            hidden[kt * unit : kt * unit + total.shape[0], :],
            mix_w[:, kt * 3 * LANES : (kt + 1) * 3 * LANES],
            (((1,), (1,)), ((), ())),
            preferred_element_type=jnp.float32,
        )
    store(outs, total, 0, total.shape[0] // unit, channels, width)


def store(outs, total, base, times, channels, width):
    splits = channels // LANES
    for block, out in enumerate(outs):
        for time in range(times):
            at = (time * len(outs) + block) * PAD
            for tile in range(2 * splits):
                first = base + (time * 2 * splits + tile) * width
                value = total[at : at + width, tile * LANES : (tile + 1) * LANES]
                out[first : first + width, :] = value.astype(jnp.bfloat16)


def add_kernel(sizes, *refs):
    parts, outs = refs[:4], refs[4:]
    first = 0
    for out, (times, splits, width) in zip(outs, sizes, strict=True):
        for time in range(times):
            for row in range(2):
                for split in range(splits):
                    rows = slice(first, first + width)
                    total = parts[0][rows, :].astype(jnp.float32)
                    for part in parts[1:]:
                        total = total + part[rows, :].astype(jnp.float32)
                    lanes = slice(split * LANES, (split + 1) * LANES)
                    out[time, row, :, lanes] = total.astype(jnp.bfloat16)
                    first += width


def backward_kernel(
    layout, width, place, rows, own, other, outs, base, slope, forward_w, mix_w, partial, evens, odds, up_w, total
):
    up_tile, _ = readers(layout, place, own, other)
    channels = rows.shape[1] // 6
    unit = evens.shape[0] - total.shape[0]
    splits = up_w.shape[1] // (2 * LANES)
    part = LANES // 2
    for kt in range(3):
        for row in range(2):
            for shift_w in range(3):
                at = (row * 3 + shift_w) * channels
                lane = (kt * 3 + 2 - shift_w) * LANES
                mix_w[at : at + channels, kt * LANES : (kt + 1) * LANES] = forward_w[
                    row * channels : (row + 1) * channels, lane : lane + LANES
                ]
    step = 3 * unit

    def product(k, _):
        at = pl.ds(pl.multiple_of(k * step, step), step)
        partial[at, :] = jnp.dot(rows[at, :], mix_w[...], preferred_element_type=jnp.float32)
        return 0

    lax.fori_loop(0, rows.shape[0] // step, product, 0)
    times = rows.shape[0] // unit - 2
    for time in range(times):
        at = time * unit
        hidden_grad = (
            partial[at + 2 * unit : at + 3 * unit, :LANES]
            + partial[at + unit : at + 2 * unit, LANES : 2 * LANES]
            + partial[at : at + unit, 2 * LANES :]
        )
        value = hidden_grad * slope[at : at + unit, :]
        target = evens if time % 2 == 0 else odds
        spot = time // 2 * unit
        for shift_w in range(3):
            target[spot : spot + unit, shift_w * LANES : (shift_w + 1) * LANES] = later(
                value, shift_w
            ).astype(jnp.bfloat16)
    for kt in range(3):
        for shift_w in range(3):
            for row in range(2):
                for out_row in range(2):
                    for split in range(splits):
                        at = (kt * 3 + shift_w) * LANES + row * part
                        lane = (out_row * splits + split) * LANES
                        up_w[at : at + part, lane : lane + LANES] = up_tile(
                            kt, out_row + 1 - row, 2 - shift_w, split, splits
                        )
    count = total.shape[0]
    lhs = (evens[:count, :], odds[:count, :], evens[unit : unit + count, :])
    total[...] = jnp.zeros_like(total)
    for kt in range(3):
        total[...] += jnp.dot(
            lhs[kt],
            up_w[kt * 3 * LANES : (kt + 1) * 3 * LANES, :],
            preferred_element_type=jnp.float32,
        )
    store(outs, total, base, count // unit, splits * LANES, width)


def compute_kernel(layout, width, base, place, frame_rows, cot_rows, own, other, *refs):
    outs, slope, scratch = refs[:4], refs[4], refs[5:]
    forward_kernel(layout, width, place, frame_rows, own, other, outs, slope, *scratch[:6])
    backward_kernel(
        layout, width, place, cot_rows, own, other, outs, base, slope, scratch[4], *scratch[6:]
    )


def call(kernel, outs, scratch, flops, megabytes, place, *operands):
    space = pl.BlockSpec(memory_space=pltpu.VMEM)
    return pl.pallas_call(
        kernel,
        out_shape=outs,
        in_specs=[pl.BlockSpec(memory_space=pltpu.SMEM)] + [space] * len(operands),
        out_specs=jax.tree.map(lambda _: space, outs),
        scratch_shapes=scratch,
        compiler_params=pltpu.CompilerParams(vmem_limit_bytes=megabytes * 2**20),
        cost_estimate=pl.CostEstimate(flops=flops, bytes_accessed=8 * 2**20, transcendentals=0),
    )(place, *operands)


def unfold(place, own, other, sizes, width):
    unit = own.shape[0] * PAD
    outs = tuple(
        jax.ShapeDtypeStruct((len(starts) * unit, 6 * splits * LANES), jnp.bfloat16)
        for starts, splits in sizes
    )
    kernel = functools.partial(unfold_kernel, sizes, width)
    return call(kernel, outs, [], 10**9, 14, place, own, other)


def compute(layout, place, frame_rows, cot_rows, own, other, width, channels, in_channels):
    blocks = own.shape[0]
    unit = blocks * PAD
    times = 2 * (frame_rows.shape[0] // unit - 3)
    base = times * 2 * (channels // LANES) * width
    rows = base + times * (in_channels // LANES) * width
    scratch = [
        pltpu.VMEM(((times + 1) * unit, LANES), jnp.float32),
        pltpu.VMEM((3 * LANES, frame_rows.shape[1]), jnp.bfloat16),
        pltpu.VMEM((frame_rows.shape[0], 3 * LANES), jnp.float32),
        pltpu.VMEM((unit, LANES), jnp.float32),
        pltpu.VMEM(((times + 2) * unit, 3 * LANES), jnp.bfloat16),
        pltpu.VMEM((2 * channels, 9 * LANES), jnp.bfloat16),
        pltpu.VMEM((times * unit, 2 * channels), jnp.float32),
        pltpu.VMEM((cot_rows.shape[1], 3 * LANES), jnp.bfloat16),
        pltpu.VMEM((cot_rows.shape[0], 3 * LANES), jnp.float32),
        pltpu.VMEM((times // 2 * unit + unit, 3 * LANES), jnp.bfloat16),
        pltpu.VMEM((times // 2 * unit, 3 * LANES), jnp.bfloat16),
        pltpu.VMEM((9 * LANES, 2 * in_channels), jnp.bfloat16),
        pltpu.VMEM((times // 2 * unit, 2 * in_channels), jnp.float32),
    ]
    kernel = functools.partial(compute_kernel, layout, width, base)
    out = (jax.ShapeDtypeStruct((rows, LANES), jnp.bfloat16),) * blocks
    return call(kernel, out, scratch, 4 * 10**9, 32, place, frame_rows, cot_rows, own, other)


def add_parts(parts, sizes):
    space = pl.BlockSpec(memory_space=pltpu.VMEM)
    return pl.pallas_call(
        functools.partial(add_kernel, sizes),
        out_shape=tuple(
            jax.ShapeDtypeStruct((times, 2, width, splits * LANES), jnp.bfloat16)
            for times, splits, width in sizes
        ),
        in_specs=[space] * len(parts),
        out_specs=(space, space),
        compiler_params=pltpu.CompilerParams(vmem_limit_bytes=8 * 2**20),
    )(*parts)


def ring(array, by):
    return lax.ppermute(array, RING, [(i, (i + by) % 4) for i in range(4)])


def flat(field):
    tiles = field.reshape(*field.shape[:3], -1, LANES)
    return tiles.transpose(0, 1, 3, 2, 4).reshape(-1, LANES)


def tiles_of(kernel):
    return kernel.reshape(-1, LANES, 2).transpose(0, 2, 1)


def shards(frames, up_kernel, mix_kernel, cotangent):
    frame_count, height, width, in_channels = frames.shape
    out_channels = mix_kernel.shape[0] // 27
    xh, xl, core = lax.axis_index("xh"), lax.axis_index("xl"), lax.axis_index("core")
    ny, nz, nx = lax.axis_size("y"), lax.axis_size("z"), lax.axis_size(RING)
    part = out_channels // nx

    raw_mix = tiles_of(mix_kernel)
    mix_other = lax.ppermute(raw_mix, RING, [(0, 3), (3, 0), (1, 2), (2, 1)])
    up_column = lax.dynamic_index_in_dim(up_kernel.T, xl, 0, keepdims=False)
    up_tiles = up_column.reshape(-1, LANES)
    up_count = up_tiles.shape[0]
    up_half = (up_count + 1) // 2
    up_part = lax.dynamic_slice_in_dim(up_tiles, core * (up_count - up_half), up_half, 0)
    up_pairs = (up_half + 1) // 2
    up_part = jnp.pad(up_part, ((0, 2 * up_pairs - up_half), (0, 0))).reshape(-1, 2, LANES)

    mix_tiles = jnp.where(xh == core, raw_mix, mix_other)
    splits = out_channels // LANES
    pick_shape = (2, out_channels, 2 * part)
    slot = lax.broadcasted_iota(jnp.int32, pick_shape, 0)
    source = lax.broadcasted_iota(jnp.int32, pick_shape, 1)
    target = lax.broadcasted_iota(jnp.int32, pick_shape, 2)
    side, spot = target // part, target % part
    wanted = (spot // nz) * (4 * nz) + xh * (2 * nz) + (spot % nz) * 2 + xl
    pick = ((source == wanted) & (slot == side)).astype(jnp.bfloat16)
    pick = pick.reshape(2, splits, LANES, 2 * part)
    taps = mix_tiles.reshape(3, 3, 3, splits, 2, LANES).transpose(0, 2, 1, 3, 4, 5)
    taps = taps.reshape(9, 3, splits, 2, LANES)
    last = jnp.pad(taps[:, 2], ((0, 1), (0, 0), (0, 0), (0, 0))).reshape(5, 2, splits, 2, LANES)
    mix_part = jnp.einsum(
        "thsjl,hslm->tjm",
        jnp.concatenate((taps[:, :2], last), axis=0),
        pick,
        preferred_element_type=jnp.float32,
    ).astype(jnp.bfloat16)

    frame_size, cot_size = 2 * (in_channels // LANES) * width, 2 * splits * width
    count = 2 * frame_count
    block = jnp.concatenate((flat(cotangent[3:]), flat(cotangent[:3]), flat(frames)), axis=0)
    early = (count - 3) * cot_size
    first = block.shape[0]
    payload, following, previous = lax.optimization_barrier(
        (
            jnp.concatenate((up_part, mix_part), axis=0),
            shift(block[early : count * cot_size + frame_size], PLANES, -1),
            shift(block[first - 2 * frame_size :], PLANES, 1),
        )
    )
    planes = spread(payload, "z")
    block = jnp.concatenate((block, following, previous), axis=0)
    blocks = (block, ring(block, 1), ring(block, -1), ring(block, 2))
    planes, block = lax.optimization_barrier((planes, block))
    blocks = jnp.stack(blocks)
    others = swap(blocks)
    last = first + 3 * cot_size + frame_size
    cot_starts = [early + time * cot_size for time in range(3)]
    cot_starts += [time * cot_size for time in range(count - 3)]
    cot_starts += [first + time * cot_size for time in range(3)]
    frame_starts = [last + time * frame_size for time in range(2)]
    frame_starts += [count * cot_size + time * frame_size for time in range(frame_count)]
    frame_starts += [first + 3 * cot_size]

    up_rows = planes[:, :up_pairs].transpose(1, 2, 0, 3).reshape(-1, LANES)
    mix_rows = planes[:, up_pairs:].transpose(1, 0, 2, 3).reshape(-1, LANES)
    own = spread(jnp.concatenate((up_rows, mix_rows), axis=0), "y")
    other = swap(own)
    layout = (nz, up_half, up_count, up_rows.shape[0])

    place = jnp.stack((xh, xl, core))
    sizes = ((tuple(frame_starts), in_channels // LANES), (tuple(cot_starts), splits))
    frame_rows, cot_rows = unfold(place, blocks, others, sizes, width)
    parts = compute(
        layout, place, frame_rows, cot_rows, own, other, width, out_channels, in_channels
    )
    parts = (parts[0], ring(parts[3], 2), ring(parts[1], -1), ring(parts[2], 1))
    outs = ((count, splits, width), (frame_count, in_channels // LANES, width))
    return add_parts(parts, outs)


def solution(mesh):
    planes, columns = mesh.devices.shape
    shape = (4, 2, planes // 8, 2, columns // 2)
    fine = Mesh(mesh.devices.reshape(shape), (*PLANES, *COLS))
    placed = P(PLANES, None, COLS, None)
    weights = P(None, PLANES)
    return jax.shard_map(
        shards,
        mesh=fine,
        in_specs=(placed, weights, weights, placed),
        out_specs=(placed, placed),
        check_vma=False,
    )
```

```python
import functools

import jax
import jax.numpy as jnp
from jax import lax
from jax.experimental import pallas as pl
from jax.experimental.pallas import tpu as pltpu
from jax.sharding import Mesh, PartitionSpec as P

PLANES = ("y", "xh", "z")
COLS = ("xl", "core")
RING = ("xh", "xl")
LANES = 128
PAD = 32


def shift(array, axis, by):
    devices = lax.axis_size(axis)
    pairs = [(i, i + by) for i in range(devices) if 0 <= i + by < devices]
    return lax.ppermute(array, axis, pairs)


def swap(array):
    return lax.ppermute(array, "core", [(0, 1), (1, 0)])


def spread(array, axis):
    count = lax.axis_size(axis)
    return lax.all_to_all(
        jnp.broadcast_to(array, (count, *array.shape)), axis, 0, 0, tiled=True
    )


def later(rows, by):
    if by == 0:
        return rows
    return pltpu.roll(rows, rows.shape[0] - by, 0)


def unfold_kernel(sizes, width, place, own, other, frame_rows, cot_rows):
    xl, core = place[1], place[2]
    blocks = own.shape[0]

    def step(block, _):
        side = (xl + (block + 1) // 2) % 2
        partner = jnp.where(xl == 0, (block + 2) % 4, block + 1 - 2 * (block % 2))
        left = jnp.where(core == 1, block, partner)
        right = jnp.where(core == 0, block, partner)
        has_left = 2 * side + core > 0
        has_right = 2 * side + core < 3
        for out, (starts, splits) in zip((frame_rows, cot_rows), sizes, strict=True):
            for time, start in enumerate(starts):
                target = pl.ds(pl.multiple_of((time * blocks + block) * PAD, PAD), PAD)
                for tile in range(2 * splits):
                    row, split = tile // splits, tile % splits
                    first = start + tile * width
                    low = other[left, first + width - 8 : first + width, :].astype(jnp.float32)
                    middle = own[block, first : first + width, :].astype(jnp.float32)
                    high = other[right, first : first + 8, :].astype(jnp.float32)
                    low = jnp.where(has_left, low, 0.0)
                    high = jnp.where(has_right, high, 0.0)
                    chunk = jnp.concatenate((low, middle, high), axis=0)
                    for tap in range(3):
                        lane = ((row * 3 + tap) * splits + split) * LANES
                        moved = chunk[6 + tap : 6 + tap + PAD].astype(jnp.bfloat16)
                        out[target, lane : lane + LANES] = moved
        return 0

    lax.fori_loop(0, blocks, step, 0)


def readers(layout, place, own, other):
    nz, up_half, up_count, up_size = layout
    lead = place[2] == 0

    def low(start, count):
        rows = slice(start, start + count)
        return jnp.where(lead, own[:, rows], other[:, rows])

    def high(start, count):
        rows = slice(start, start + count)
        return jnp.where(lead, other[:, rows], own[:, rows])

    def up_tile(kt, kh, kw, split, splits):
        tile = ((kt * 3 + kh) * 3 + kw) * splits + split
        if tile < up_half:
            value = low(tile * nz, nz)
        else:
            value = high((tile - (up_count - up_half)) * nz, nz)
        return value.reshape(-1, LANES)

    def both(tile):
        start = up_size + tile * 2 * nz
        return jnp.stack((low(start, 2 * nz), high(start, 2 * nz)), axis=1).reshape(-1, LANES)

    def mix_tile(kt, kw, pair):
        at = kt * 3 + kw
        if pair == 1:
            return both(at)
        ahead = pltpu.roll(both(at).astype(jnp.float32), LANES // 2, 1)
        last = both(9 + at // 2).astype(jnp.float32)
        if at % 2 == 0:
            last = pltpu.roll(last, LANES // 2, 1)
        lane = lax.broadcasted_iota(jnp.int32, ahead.shape, 1)
        return jnp.where(lane < LANES // 2, ahead, last).astype(jnp.bfloat16)

    return up_tile, mix_tile


def forward_kernel(
    layout, width, place, rows, own, other, outs, slope, up_w, ups, mask, hidden, mix_w, total
):
    up_tile, mix_tile = readers(layout, place, own, other)
    splits = rows.shape[1] // (6 * LANES)
    part, unit = up_w.shape[0] // 6, mask.shape[0]
    column = lax.broadcasted_iota(jnp.int32, (PAD, LANES), 0) - 1
    for block in range(len(outs)):
        side = (place[1] + (block + 1) // 2) % 2
        at = (2 * side + place[2]) * width + column
        inside = (at >= 0) & (at < 4 * width)
        mask[block * PAD : (block + 1) * PAD, :] = inside.astype(jnp.float32)
    for kt in range(3):
        for out_row in range(2):
            for row in range(2):
                for kw in range(3):
                    for split in range(splits):
                        at = kt * 2 * part + out_row * part
                        lane = ((row * 3 + kw) * splits + split) * LANES
                        up_w[at : at + part, lane : lane + LANES] = up_tile(
                            kt, row - out_row + 1, kw, split, splits
                        )
    last = rows.shape[0] - unit
    pair, single = slice(0, 2 * LANES), slice(2 * LANES, 3 * LANES)
    for first, count, lanes in ((unit, last, pair), (0, last, single)):
        for start in range(first, first + count, count // 2):
            at = slice(start, start + count // 2)
            ups[at, lanes] = lax.dot_general(
                rows[at, :],
                up_w[lanes, :],
                (((1,), (1,)), ((), ())),
                preferred_element_type=jnp.float32,
            )
    inside = mask[...] > 0
    times = 2 * (rows.shape[0] // unit - 1) - 1
    for time in range(times):
        at = time // 2 * unit
        if time % 2 == 0:
            before = ups[at + unit : at + 2 * unit, :LANES] + ups[at : at + unit, 2 * LANES :]
        else:
            before = ups[at + unit : at + 2 * unit, LANES : 2 * LANES]
        sigma = jax.nn.sigmoid(before)
        if time < times - 1:
            value = jnp.where(inside, before * sigma, 0.0)
            for kw in range(3):
                hidden[time * unit : (time + 1) * unit, kw * LANES : (kw + 1) * LANES] = later(
                    value, kw
                ).astype(jnp.bfloat16)
        if time >= 2:
            slope[(time - 2) * unit : (time - 1) * unit, :] = jnp.where(
                inside, sigma * (1.0 + before * (1.0 - sigma)), 0.0
            )
    channels = mix_w.shape[0] // 2
    for kt in range(3):
        for out_row in range(2):
            for kw in range(3):
                mix_w[
                    out_row * channels : (out_row + 1) * channels,
                    (kt * 3 + kw) * LANES : (kt * 3 + kw + 1) * LANES,
                ] = mix_tile(kt, kw, out_row)
    total[...] = jnp.zeros_like(total)
    for kt in range(3):
        total[...] += lax.dot_general(
            hidden[kt * unit : kt * unit + total.shape[0], :],
            mix_w[:, kt * 3 * LANES : (kt + 1) * 3 * LANES],
            (((1,), (1,)), ((), ())),
            preferred_element_type=jnp.float32,
        )
    store(outs, total, 0, total.shape[0] // unit, channels, width)


def store(outs, total, base, times, channels, width):
    splits = channels // LANES
    for block, out in enumerate(outs):
        for time in range(times):
            at = (time * len(outs) + block) * PAD
            for tile in range(2 * splits):
                first = base + (time * 2 * splits + tile) * width
                value = total[at : at + width, tile * LANES : (tile + 1) * LANES]
                out[first : first + width, :] = value.astype(jnp.bfloat16)


def add_kernel(sizes, *refs):
    parts, outs = refs[:4], refs[4:]
    first = 0
    for out, (times, splits, width) in zip(outs, sizes, strict=True):
        for time in range(times):
            for row in range(2):
                for split in range(splits):
                    rows = slice(first, first + width)
                    total = parts[0][rows, :].astype(jnp.float32)
                    for part in parts[1:]:
                        total = total + part[rows, :].astype(jnp.float32)
                    lanes = slice(split * LANES, (split + 1) * LANES)
                    out[time, row, :, lanes] = total.astype(jnp.bfloat16)
                    first += width


def backward_kernel(
    layout, width, place, rows, own, other, outs, base, slope, forward_w, mix_w, partial, evens, odds, up_w, total
):
    up_tile, _ = readers(layout, place, own, other)
    channels = rows.shape[1] // 6
    unit = evens.shape[0] - total.shape[0]
    splits = up_w.shape[1] // (2 * LANES)
    part = LANES // 2
    for kt in range(3):
        for row in range(2):
            for shift_w in range(3):
                at = (row * 3 + shift_w) * channels
                lane = (kt * 3 + 2 - shift_w) * LANES
                mix_w[at : at + channels, kt * LANES : (kt + 1) * LANES] = forward_w[
                    row * channels : (row + 1) * channels, lane : lane + LANES
                ]
    last = rows.shape[0] - unit
    pair, single = slice(0, 2 * LANES), slice(2 * LANES, 3 * LANES)
    for first, count, lanes in ((unit, last, pair), (0, last - unit, single)):
        for start in range(first, first + count, count // 2):
            at = slice(start, start + count // 2)
            partial[at, lanes] = jnp.dot(
                rows[at, :], mix_w[:, lanes], preferred_element_type=jnp.float32
            )
    times = rows.shape[0] // unit - 2
    for time in range(times):
        at = time * unit
        hidden_grad = (
            partial[at + 2 * unit : at + 3 * unit, :LANES]
            + partial[at + unit : at + 2 * unit, LANES : 2 * LANES]
            + partial[at : at + unit, 2 * LANES :]
        )
        value = hidden_grad * slope[at : at + unit, :]
        target = evens if time % 2 == 0 else odds
        spot = time // 2 * unit
        for shift_w in range(3):
            target[spot : spot + unit, shift_w * LANES : (shift_w + 1) * LANES] = later(
                value, shift_w
            ).astype(jnp.bfloat16)
    for kt in range(3):
        for shift_w in range(3):
            for row in range(2):
                for out_row in range(2):
                    for split in range(splits):
                        at = (kt * 3 + shift_w) * LANES + row * part
                        lane = (out_row * splits + split) * LANES
                        up_w[at : at + part, lane : lane + LANES] = up_tile(
                            kt, out_row + 1 - row, 2 - shift_w, split, splits
                        )
    count = total.shape[0]
    lhs = (evens[:count, :], odds[:count, :], evens[unit : unit + count, :])
    total[...] = jnp.zeros_like(total)
    for kt in range(3):
        total[...] += jnp.dot(
            lhs[kt],
            up_w[kt * 3 * LANES : (kt + 1) * 3 * LANES, :],
            preferred_element_type=jnp.float32,
        )
    store(outs, total, base, count // unit, splits * LANES, width)


def compute_kernel(layout, width, base, place, frame_rows, cot_rows, own, other, *refs):
    outs, slope, scratch = refs[:4], refs[4], refs[5:]
    forward_kernel(layout, width, place, frame_rows, own, other, outs, slope, *scratch[:6])
    backward_kernel(
        layout, width, place, cot_rows, own, other, outs, base, slope, scratch[4], *scratch[6:]
    )


def call(kernel, outs, scratch, flops, megabytes, place, *operands):
    space = pl.BlockSpec(memory_space=pltpu.VMEM)
    return pl.pallas_call(
        kernel,
        out_shape=outs,
        in_specs=[pl.BlockSpec(memory_space=pltpu.SMEM)] + [space] * len(operands),
        out_specs=jax.tree.map(lambda _: space, outs),
        scratch_shapes=scratch,
        compiler_params=pltpu.CompilerParams(vmem_limit_bytes=megabytes * 2**20),
        cost_estimate=pl.CostEstimate(flops=flops, bytes_accessed=8 * 2**20, transcendentals=0),
    )(place, *operands)


def unfold(place, own, other, sizes, width):
    unit = own.shape[0] * PAD
    outs = tuple(
        jax.ShapeDtypeStruct((len(starts) * unit, 6 * splits * LANES), jnp.bfloat16)
        for starts, splits in sizes
    )
    kernel = functools.partial(unfold_kernel, sizes, width)
    return call(kernel, outs, [], 10**9, 14, place, own, other)


def compute(layout, place, frame_rows, cot_rows, own, other, width, channels, in_channels):
    blocks = own.shape[0]
    unit = blocks * PAD
    times = 2 * (frame_rows.shape[0] // unit - 3)
    base = times * 2 * (channels // LANES) * width
    rows = base + times * (in_channels // LANES) * width
    scratch = [
        pltpu.VMEM(((times + 1) * unit, LANES), jnp.float32),
        pltpu.VMEM((3 * LANES, frame_rows.shape[1]), jnp.bfloat16),
        pltpu.VMEM((frame_rows.shape[0], 3 * LANES), jnp.float32),
        pltpu.VMEM((unit, LANES), jnp.float32),
        pltpu.VMEM(((times + 2) * unit, 3 * LANES), jnp.bfloat16),
        pltpu.VMEM((2 * channels, 9 * LANES), jnp.bfloat16),
        pltpu.VMEM((times * unit, 2 * channels), jnp.float32),
        pltpu.VMEM((cot_rows.shape[1], 3 * LANES), jnp.bfloat16),
        pltpu.VMEM((cot_rows.shape[0], 3 * LANES), jnp.float32),
        pltpu.VMEM((times // 2 * unit + unit, 3 * LANES), jnp.bfloat16),
        pltpu.VMEM((times // 2 * unit, 3 * LANES), jnp.bfloat16),
        pltpu.VMEM((9 * LANES, 2 * in_channels), jnp.bfloat16),
        pltpu.VMEM((times // 2 * unit, 2 * in_channels), jnp.float32),
    ]
    kernel = functools.partial(compute_kernel, layout, width, base)
    out = (jax.ShapeDtypeStruct((rows, LANES), jnp.bfloat16),) * blocks
    return call(kernel, out, scratch, 4 * 10**9, 32, place, frame_rows, cot_rows, own, other)


def add_parts(parts, sizes):
    space = pl.BlockSpec(memory_space=pltpu.VMEM)
    return pl.pallas_call(
        functools.partial(add_kernel, sizes),
        out_shape=tuple(
            jax.ShapeDtypeStruct((times, 2, width, splits * LANES), jnp.bfloat16)
            for times, splits, width in sizes
        ),
        in_specs=[space] * len(parts),
        out_specs=(space, space),
        compiler_params=pltpu.CompilerParams(vmem_limit_bytes=8 * 2**20),
    )(*parts)


def ring(array, by):
    return lax.ppermute(array, RING, [(i, (i + by) % 4) for i in range(4)])


def flat(field):
    tiles = field.reshape(*field.shape[:3], -1, LANES)
    return tiles.transpose(0, 1, 3, 2, 4).reshape(-1, LANES)


def tiles_of(kernel):
    return kernel.reshape(-1, LANES, 2).transpose(0, 2, 1)


def shards(frames, up_kernel, mix_kernel, cotangent):
    frame_count, height, width, in_channels = frames.shape
    out_channels = mix_kernel.shape[0] // 27
    xh, xl, core = lax.axis_index("xh"), lax.axis_index("xl"), lax.axis_index("core")
    ny, nz, nx = lax.axis_size("y"), lax.axis_size("z"), lax.axis_size(RING)
    part = out_channels // nx

    mix_other = lax.ppermute(mix_kernel, RING, [(0, 3), (3, 0), (1, 2), (2, 1)])
    up_column = lax.dynamic_index_in_dim(up_kernel.T, xl, 0, keepdims=False)
    up_tiles = up_column.reshape(-1, LANES)
    up_count = up_tiles.shape[0]
    up_half = (up_count + 1) // 2
    up_part = lax.dynamic_slice_in_dim(up_tiles, core * (up_count - up_half), up_half, 0)
    up_pairs = (up_half + 1) // 2
    up_part = jnp.pad(up_part, ((0, 2 * up_pairs - up_half), (0, 0))).reshape(-1, 2, LANES)

    mix_tiles = tiles_of(jnp.where(xh == core, mix_kernel, mix_other))
    splits = out_channels // LANES
    pick_shape = (2, out_channels, 2 * part)
    slot = lax.broadcasted_iota(jnp.int32, pick_shape, 0)
    source = lax.broadcasted_iota(jnp.int32, pick_shape, 1)
    target = lax.broadcasted_iota(jnp.int32, pick_shape, 2)
    side, spot = target // part, target % part
    wanted = (spot // nz) * (4 * nz) + xh * (2 * nz) + (spot % nz) * 2 + xl
    pick = ((source == wanted) & (slot == side)).astype(jnp.bfloat16)
    pick = pick.reshape(2, splits, LANES, 2 * part)
    taps = mix_tiles.reshape(3, 3, 3, splits, 2, LANES).transpose(0, 2, 1, 3, 4, 5)
    taps = taps.reshape(9, 3, splits, 2, LANES)
    last = jnp.pad(taps[:, 2], ((0, 1), (0, 0), (0, 0), (0, 0))).reshape(5, 2, splits, 2, LANES)
    mix_part = jnp.einsum(
        "thsjl,hslm->tjm",
        jnp.concatenate((taps[:, :2], last), axis=0),
        pick,
        preferred_element_type=jnp.float32,
    ).astype(jnp.bfloat16)

    frame_size, cot_size = 2 * (in_channels // LANES) * width, 2 * splits * width
    count = 2 * frame_count
    block = jnp.concatenate((flat(cotangent[3:]), flat(cotangent[:3]), flat(frames)), axis=0)
    early = (count - 3) * cot_size
    first = block.shape[0]
    payload, following, previous = lax.optimization_barrier(
        (
            jnp.concatenate((up_part, mix_part), axis=0),
            shift(block[early : count * cot_size + frame_size], PLANES, -1),
            shift(block[first - 2 * frame_size :], PLANES, 1),
        )
    )
    planes = spread(payload, "z")
    block = jnp.concatenate((block, following, previous), axis=0)
    blocks = (block, ring(block, 1), ring(block, -1), ring(block, 2))
    planes, block = lax.optimization_barrier((planes, block))
    blocks = jnp.stack(blocks)
    others = swap(blocks)
    last = first + 3 * cot_size + frame_size
    cot_starts = [early + time * cot_size for time in range(3)]
    cot_starts += [time * cot_size for time in range(count - 3)]
    cot_starts += [first + time * cot_size for time in range(3)]
    frame_starts = [last + time * frame_size for time in range(2)]
    frame_starts += [count * cot_size + time * frame_size for time in range(frame_count)]
    frame_starts += [first + 3 * cot_size]

    up_rows = planes[:, :up_pairs].transpose(1, 2, 0, 3).reshape(-1, LANES)
    mix_rows = planes[:, up_pairs:].transpose(1, 0, 2, 3).reshape(-1, LANES)
    own = spread(jnp.concatenate((up_rows, mix_rows), axis=0), "y")
    other = swap(own)
    layout = (nz, up_half, up_count, up_rows.shape[0])

    place = jnp.stack((xh, xl, core))
    sizes = ((tuple(frame_starts), in_channels // LANES), (tuple(cot_starts), splits))
    frame_rows, cot_rows = unfold(place, blocks, others, sizes, width)
    parts = compute(
        layout, place, frame_rows, cot_rows, own, other, width, out_channels, in_channels
    )
    parts = (parts[0], ring(parts[3], 2), ring(parts[1], -1), ring(parts[2], 1))
    outs = ((count, splits, width), (frame_count, in_channels // LANES, width))
    return add_parts(parts, outs)


def solution(mesh):
    planes, columns = mesh.devices.shape
    shape = (4, 2, planes // 8, 2, columns // 2)
    fine = Mesh(mesh.devices.reshape(shape), (*PLANES, *COLS))
    placed = P(PLANES, None, COLS, None)
    weights = P(None, PLANES)
    return jax.shard_map(
        shards,
        mesh=fine,
        in_specs=(placed, weights, weights, placed),
        out_specs=(placed, placed),
        check_vma=False,
    )
```

```python
import functools

import jax
import jax.numpy as jnp
from jax import lax
from jax.experimental import pallas as pl
from jax.experimental.pallas import tpu as pltpu
from jax.sharding import Mesh, PartitionSpec as P

PLANES = ("y", "xh", "z")
COLS = ("xl", "core")
RING = ("xh", "xl")
LANES = 128
PAD = 32


def shift(array, axis, by):
    devices = lax.axis_size(axis)
    pairs = [(i, i + by) for i in range(devices) if 0 <= i + by < devices]
    return lax.ppermute(array, axis, pairs)


def swap(array):
    return lax.ppermute(array, "core", [(0, 1), (1, 0)])


def spread(array, axis):
    count = lax.axis_size(axis)
    return lax.all_to_all(
        jnp.broadcast_to(array, (count, *array.shape)), axis, 0, 0, tiled=True
    )


def later(rows, by):
    if by == 0:
        return rows
    return pltpu.roll(rows, rows.shape[0] - by, 0)


def unfold_kernel(sizes, width, place, own, other, frame_rows, cot_rows):
    xl, core = place[1], place[2]
    blocks = own.shape[0]

    def step(block, _):
        side = (xl + (block + 1) // 2) % 2
        partner = jnp.where(xl == 0, (block + 2) % 4, block + 1 - 2 * (block % 2))
        left = jnp.where(core == 1, block, partner)
        right = jnp.where(core == 0, block, partner)
        has_left = 2 * side + core > 0
        has_right = 2 * side + core < 3
        for out, (starts, splits) in zip((frame_rows, cot_rows), sizes, strict=True):
            for time, start in enumerate(starts):
                target = pl.ds(pl.multiple_of((time * blocks + block) * PAD, PAD), PAD)
                for tile in range(2 * splits):
                    row, split = tile // splits, tile % splits
                    first = start + tile * width
                    low = other[left, first + width - 8 : first + width, :].astype(jnp.float32)
                    middle = own[block, first : first + width, :].astype(jnp.float32)
                    high = other[right, first : first + 8, :].astype(jnp.float32)
                    low = jnp.where(has_left, low, 0.0)
                    high = jnp.where(has_right, high, 0.0)
                    chunk = jnp.concatenate((low, middle, high), axis=0)
                    for tap in range(3):
                        lane = ((row * 3 + tap) * splits + split) * LANES
                        moved = chunk[6 + tap : 6 + tap + PAD].astype(jnp.bfloat16)
                        out[target, lane : lane + LANES] = moved
        return 0

    lax.fori_loop(0, blocks, step, 0)


def readers(layout, place, own, other):
    nz, up_half, up_count, up_size = layout
    lead = place[2] == 0

    def low(start, count):
        rows = slice(start, start + count)
        return jnp.where(lead, own[:, rows], other[:, rows])

    def high(start, count):
        rows = slice(start, start + count)
        return jnp.where(lead, other[:, rows], own[:, rows])

    def up_tile(kt, kh, kw, split, splits):
        tile = ((kt * 3 + kh) * 3 + kw) * splits + split
        if tile < up_half:
            value = low(tile * nz, nz)
        else:
            value = high((tile - (up_count - up_half)) * nz, nz)
        return value.reshape(-1, LANES)

    def both(tile):
        start = up_size + tile * 2 * nz
        return jnp.stack((low(start, 2 * nz), high(start, 2 * nz)), axis=1).reshape(-1, LANES)

    def mix_tile(kt, kw, pair):
        at = kt * 3 + kw
        if pair == 1:
            return both(at)
        ahead = pltpu.roll(both(at).astype(jnp.float32), LANES // 2, 1)
        last = both(9 + at // 2).astype(jnp.float32)
        if at % 2 == 0:
            last = pltpu.roll(last, LANES // 2, 1)
        lane = lax.broadcasted_iota(jnp.int32, ahead.shape, 1)
        return jnp.where(lane < LANES // 2, ahead, last).astype(jnp.bfloat16)

    return up_tile, mix_tile


def forward_kernel(
    layout, width, place, rows, own, other, outs, slope, up_w, ups, mask, hidden, mix_w, total
):
    up_tile, mix_tile = readers(layout, place, own, other)
    splits = rows.shape[1] // (6 * LANES)
    part, unit = up_w.shape[0] // 6, mask.shape[0]
    column = lax.broadcasted_iota(jnp.int32, (PAD, LANES), 0) - 1
    for block in range(len(outs)):
        side = (place[1] + (block + 1) // 2) % 2
        at = (2 * side + place[2]) * width + column
        inside = (at >= 0) & (at < 4 * width)
        mask[block * PAD : (block + 1) * PAD, :] = inside.astype(jnp.float32)
    for kt in range(3):
        for out_row in range(2):
            for row in range(2):
                for kw in range(3):
                    for split in range(splits):
                        at = kt * 2 * part + out_row * part
                        lane = ((row * 3 + kw) * splits + split) * LANES
                        up_w[at : at + part, lane : lane + LANES] = up_tile(
                            kt, row - out_row + 1, kw, split, splits
                        )
    last = rows.shape[0] - unit
    pair, single = slice(0, 2 * LANES), slice(2 * LANES, 3 * LANES)
    for first, count, lanes in ((unit, last, pair), (0, last, single)):
        for start in range(first, first + count, count // 2):
            at = slice(start, start + count // 2)
            ups[at, lanes] = lax.dot_general(
                rows[at, :],
                up_w[lanes, :],
                (((1,), (1,)), ((), ())),
                preferred_element_type=jnp.float32,
            )
    inside = mask[...] > 0
    times = 2 * (rows.shape[0] // unit - 1) - 1
    for time in range(times):
        at = time // 2 * unit
        if time % 2 == 0:
            before = ups[at + unit : at + 2 * unit, :LANES] + ups[at : at + unit, 2 * LANES :]
        else:
            before = ups[at + unit : at + 2 * unit, LANES : 2 * LANES]
        sigma = jax.nn.sigmoid(before)
        if time < times - 1:
            value = jnp.where(inside, before * sigma, 0.0)
            for kw in range(3):
                hidden[time * unit : (time + 1) * unit, kw * LANES : (kw + 1) * LANES] = later(
                    value, kw
                ).astype(jnp.bfloat16)
        if time >= 2:
            slope[(time - 2) * unit : (time - 1) * unit, :] = jnp.where(
                inside, sigma * (1.0 + before * (1.0 - sigma)), 0.0
            )
    channels = mix_w.shape[0] // 2
    for kt in range(3):
        for out_row in range(2):
            for kw in range(3):
                mix_w[
                    out_row * channels : (out_row + 1) * channels,
                    (kt * 3 + kw) * LANES : (kt * 3 + kw + 1) * LANES,
                ] = mix_tile(kt, kw, out_row)
    total[...] = jnp.zeros_like(total)
    for kt in range(3):
        total[...] += lax.dot_general(
            hidden[kt * unit : kt * unit + total.shape[0], :],
            mix_w[:, kt * 3 * LANES : (kt + 1) * 3 * LANES],
            (((1,), (1,)), ((), ())),
            preferred_element_type=jnp.float32,
        )
    store(outs, total, 0, total.shape[0] // unit, channels, width)


def store(outs, total, base, times, channels, width):
    splits = channels // LANES
    for block, out in enumerate(outs):
        for time in range(times):
            at = (time * len(outs) + block) * PAD
            for tile in range(2 * splits):
                first = base + (time * 2 * splits + tile) * width
                value = total[at : at + width, tile * LANES : (tile + 1) * LANES]
                out[first : first + width, :] = value.astype(jnp.bfloat16)


def add_kernel(sizes, *refs):
    parts, outs = refs[:4], refs[4:]
    first = 0
    for out, (times, splits, width) in zip(outs, sizes, strict=True):
        for time in range(times):
            for row in range(2):
                for split in range(splits):
                    rows = slice(first, first + width)
                    total = parts[0][rows, :].astype(jnp.float32)
                    for part in parts[1:]:
                        total = total + part[rows, :].astype(jnp.float32)
                    lanes = slice(split * LANES, (split + 1) * LANES)
                    out[time, row, :, lanes] = total.astype(jnp.bfloat16)
                    first += width


def backward_kernel(
    layout, width, place, rows, own, other, outs, base, slope, forward_w, mix_w, partial, evens, odds, up_w, total
):
    up_tile, _ = readers(layout, place, own, other)
    channels = rows.shape[1] // 6
    unit = evens.shape[0] - total.shape[0]
    splits = up_w.shape[1] // (2 * LANES)
    part = LANES // 2
    for kt in range(3):
        for row in range(2):
            for shift_w in range(3):
                at = (row * 3 + shift_w) * channels
                lane = (kt * 3 + 2 - shift_w) * LANES
                mix_w[at : at + channels, kt * LANES : (kt + 1) * LANES] = forward_w[
                    row * channels : (row + 1) * channels, lane : lane + LANES
                ]
    last = rows.shape[0] - unit
    pair, single = slice(0, 2 * LANES), slice(2 * LANES, 3 * LANES)
    for first, count, lanes in ((unit, last, pair), (0, last - unit, single)):
        for start in range(first, first + count, count // 2):
            at = slice(start, start + count // 2)
            partial[at, lanes] = jnp.dot(
                rows[at, :], mix_w[:, lanes], preferred_element_type=jnp.float32
            )
    times = rows.shape[0] // unit - 2
    for time in range(times):
        at = time * unit
        hidden_grad = (
            partial[at + 2 * unit : at + 3 * unit, :LANES]
            + partial[at + unit : at + 2 * unit, LANES : 2 * LANES]
            + partial[at : at + unit, 2 * LANES :]
        )
        value = hidden_grad * slope[at : at + unit, :]
        target = evens if time % 2 == 0 else odds
        spot = time // 2 * unit
        for shift_w in range(3):
            target[spot : spot + unit, shift_w * LANES : (shift_w + 1) * LANES] = later(
                value, shift_w
            ).astype(jnp.bfloat16)
    for kt in range(3):
        for shift_w in range(3):
            for row in range(2):
                for out_row in range(2):
                    for split in range(splits):
                        at = (kt * 3 + shift_w) * LANES + row * part
                        lane = (out_row * splits + split) * LANES
                        up_w[at : at + part, lane : lane + LANES] = up_tile(
                            kt, out_row + 1 - row, 2 - shift_w, split, splits
                        )
    count = total.shape[0]
    lhs = (evens[:count, :], odds[:count, :], evens[unit : unit + count, :])
    total[...] = jnp.zeros_like(total)
    for kt in range(3):
        total[...] += jnp.dot(
            lhs[kt],
            up_w[kt * 3 * LANES : (kt + 1) * 3 * LANES, :],
            preferred_element_type=jnp.float32,
        )
    store(outs, total, base, count // unit, splits * LANES, width)


def compute_kernel(layout, width, base, place, frame_rows, cot_rows, own, other, *refs):
    outs, slope, scratch = refs[:4], refs[4], refs[5:]
    forward_kernel(layout, width, place, frame_rows, own, other, outs, slope, *scratch[:6])
    backward_kernel(
        layout, width, place, cot_rows, own, other, outs, base, slope, scratch[4], *scratch[6:]
    )


def call(kernel, outs, scratch, flops, megabytes, place, *operands):
    space = pl.BlockSpec(memory_space=pltpu.VMEM)
    return pl.pallas_call(
        kernel,
        out_shape=outs,
        in_specs=[pl.BlockSpec(memory_space=pltpu.SMEM)] + [space] * len(operands),
        out_specs=jax.tree.map(lambda _: space, outs),
        scratch_shapes=scratch,
        compiler_params=pltpu.CompilerParams(vmem_limit_bytes=megabytes * 2**20),
        cost_estimate=pl.CostEstimate(flops=flops, bytes_accessed=8 * 2**20, transcendentals=0),
    )(place, *operands)


def unfold(place, own, other, sizes, width):
    unit = own.shape[0] * PAD
    outs = tuple(
        jax.ShapeDtypeStruct((len(starts) * unit, 6 * splits * LANES), jnp.bfloat16)
        for starts, splits in sizes
    )
    kernel = functools.partial(unfold_kernel, sizes, width)
    return call(kernel, outs, [], 10**9, 14, place, own, other)


def compute(layout, place, frame_rows, cot_rows, own, other, width, channels, in_channels):
    blocks = own.shape[0]
    unit = blocks * PAD
    times = 2 * (frame_rows.shape[0] // unit - 3)
    base = times * 2 * (channels // LANES) * width
    rows = base + times * (in_channels // LANES) * width
    scratch = [
        pltpu.VMEM(((times + 1) * unit, LANES), jnp.float32),
        pltpu.VMEM((3 * LANES, frame_rows.shape[1]), jnp.bfloat16),
        pltpu.VMEM((frame_rows.shape[0], 3 * LANES), jnp.float32),
        pltpu.VMEM((unit, LANES), jnp.float32),
        pltpu.VMEM(((times + 2) * unit, 3 * LANES), jnp.bfloat16),
        pltpu.VMEM((2 * channels, 9 * LANES), jnp.bfloat16),
        pltpu.VMEM((times * unit, 2 * channels), jnp.float32),
        pltpu.VMEM((cot_rows.shape[1], 3 * LANES), jnp.bfloat16),
        pltpu.VMEM((cot_rows.shape[0], 3 * LANES), jnp.float32),
        pltpu.VMEM((times // 2 * unit + unit, 3 * LANES), jnp.bfloat16),
        pltpu.VMEM((times // 2 * unit, 3 * LANES), jnp.bfloat16),
        pltpu.VMEM((9 * LANES, 2 * in_channels), jnp.bfloat16),
        pltpu.VMEM((times // 2 * unit, 2 * in_channels), jnp.float32),
    ]
    kernel = functools.partial(compute_kernel, layout, width, base)
    out = (jax.ShapeDtypeStruct((rows, LANES), jnp.bfloat16),) * blocks
    return call(kernel, out, scratch, 4 * 10**9, 32, place, frame_rows, cot_rows, own, other)


def add_parts(parts, sizes):
    space = pl.BlockSpec(memory_space=pltpu.VMEM)
    return pl.pallas_call(
        functools.partial(add_kernel, sizes),
        out_shape=tuple(
            jax.ShapeDtypeStruct((times, 2, width, splits * LANES), jnp.bfloat16)
            for times, splits, width in sizes
        ),
        in_specs=[space] * len(parts),
        out_specs=(space, space),
        compiler_params=pltpu.CompilerParams(vmem_limit_bytes=8 * 2**20),
    )(*parts)


def ring(array, by):
    return lax.ppermute(array, RING, [(i, (i + by) % 4) for i in range(4)])


def flat(field):
    tiles = field.reshape(*field.shape[:3], -1, LANES)
    return tiles.transpose(0, 1, 3, 2, 4).reshape(-1, LANES)


def tiles_of(kernel):
    return kernel.reshape(-1, LANES, 2).transpose(0, 2, 1)


def shards(frames, up_kernel, mix_kernel, cotangent):
    frame_count, height, width, in_channels = frames.shape
    out_channels = mix_kernel.shape[0] // 27
    xh, xl, core = lax.axis_index("xh"), lax.axis_index("xl"), lax.axis_index("core")
    ny, nz, nx = lax.axis_size("y"), lax.axis_size("z"), lax.axis_size(RING)
    part = out_channels // nx

    mix_other = lax.ppermute(mix_kernel, RING, [(0, 3), (3, 0), (1, 2), (2, 1)])
    up_column = lax.dynamic_index_in_dim(up_kernel.T, xl, 0, keepdims=False)
    up_tiles = up_column.reshape(-1, LANES)
    up_count = up_tiles.shape[0]
    up_half = (up_count + 1) // 2
    up_part = lax.dynamic_slice_in_dim(up_tiles, core * (up_count - up_half), up_half, 0)
    up_pairs = (up_half + 1) // 2
    up_part = jnp.pad(up_part, ((0, 2 * up_pairs - up_half), (0, 0))).reshape(-1, 2, LANES)

    mix_tiles = tiles_of(jnp.where(xh == core, mix_kernel, mix_other))
    splits = out_channels // LANES
    pick_shape = (2, out_channels, 2 * part)
    slot = lax.broadcasted_iota(jnp.int32, pick_shape, 0)
    source = lax.broadcasted_iota(jnp.int32, pick_shape, 1)
    target = lax.broadcasted_iota(jnp.int32, pick_shape, 2)
    side, spot = target // part, target % part
    wanted = (spot // nz) * (4 * nz) + xh * (2 * nz) + (spot % nz) * 2 + xl
    pick = ((source == wanted) & (slot == side)).astype(jnp.bfloat16)
    pick = pick.reshape(2, splits, LANES, 2 * part)
    taps = mix_tiles.reshape(3, 3, 3, splits, 2, LANES).transpose(0, 2, 1, 3, 4, 5)
    taps = taps.reshape(9, 3, splits, 2, LANES)
    last = jnp.pad(taps[:, 2], ((0, 1), (0, 0), (0, 0), (0, 0))).reshape(5, 2, splits, 2, LANES)
    mix_part = jnp.einsum(
        "thsjl,hslm->tjm",
        jnp.concatenate((taps[:, :2], last), axis=0),
        pick,
        preferred_element_type=jnp.float32,
    ).astype(jnp.bfloat16)

    frame_size, cot_size = 2 * (in_channels // LANES) * width, 2 * splits * width
    count = 2 * frame_count
    block = jnp.concatenate((flat(cotangent[3:]), flat(cotangent[:3]), flat(frames)), axis=0)
    early = (count - 3) * cot_size
    first = block.shape[0]
    following = shift(block[early : count * cot_size + frame_size], PLANES, -1)
    payload, previous = lax.optimization_barrier(
        (
            jnp.concatenate((up_part, mix_part), axis=0),
            shift(block[first - 2 * frame_size :], PLANES, 1),
        )
    )
    planes = spread(payload, "z")
    block = jnp.concatenate((block, following, previous), axis=0)
    blocks = (block, ring(block, 1), ring(block, -1), ring(block, 2))
    planes, block = lax.optimization_barrier((planes, block))
    blocks = jnp.stack(blocks)
    others = swap(blocks)
    last = first + 3 * cot_size + frame_size
    cot_starts = [early + time * cot_size for time in range(3)]
    cot_starts += [time * cot_size for time in range(count - 3)]
    cot_starts += [first + time * cot_size for time in range(3)]
    frame_starts = [last + time * frame_size for time in range(2)]
    frame_starts += [count * cot_size + time * frame_size for time in range(frame_count)]
    frame_starts += [first + 3 * cot_size]

    up_rows = planes[:, :up_pairs].transpose(1, 2, 0, 3).reshape(-1, LANES)
    mix_rows = planes[:, up_pairs:].transpose(1, 0, 2, 3).reshape(-1, LANES)
    own = spread(jnp.concatenate((up_rows, mix_rows), axis=0), "y")
    other = swap(own)
    layout = (nz, up_half, up_count, up_rows.shape[0])

    place = jnp.stack((xh, xl, core))
    sizes = ((tuple(frame_starts), in_channels // LANES), (tuple(cot_starts), splits))
    frame_rows, cot_rows = unfold(place, blocks, others, sizes, width)
    parts = compute(
        layout, place, frame_rows, cot_rows, own, other, width, out_channels, in_channels
    )
    parts = (parts[0], ring(parts[3], 2), ring(parts[1], -1), ring(parts[2], 1))
    outs = ((count, splits, width), (frame_count, in_channels // LANES, width))
    return add_parts(parts, outs)


def solution(mesh):
    planes, columns = mesh.devices.shape
    shape = (4, 2, planes // 8, 2, columns // 2)
    fine = Mesh(mesh.devices.reshape(shape), (*PLANES, *COLS))
    placed = P(PLANES, None, COLS, None)
    weights = P(None, PLANES)
    return jax.shard_map(
        shards,
        mesh=fine,
        in_specs=(placed, weights, weights, placed),
        out_specs=(placed, placed),
        check_vma=False,
    )
```

```python
import functools

import jax
import jax.numpy as jnp
from jax import lax
from jax.experimental import pallas as pl
from jax.experimental.pallas import tpu as pltpu
from jax.sharding import Mesh, PartitionSpec as P

PLANES = ("y", "xh", "z")
COLS = ("xl", "core")
RING = ("xh", "xl")
LANES = 128
PAD = 32


def shift(array, axis, by):
    devices = lax.axis_size(axis)
    pairs = [(i, i + by) for i in range(devices) if 0 <= i + by < devices]
    return lax.ppermute(array, axis, pairs)


def swap(array):
    return lax.ppermute(array, "core", [(0, 1), (1, 0)])


def spread(array, axis):
    count = lax.axis_size(axis)
    return lax.all_to_all(
        jnp.broadcast_to(array, (count, *array.shape)), axis, 0, 0, tiled=True
    )


def later(rows, by):
    if by == 0:
        return rows
    return pltpu.roll(rows, rows.shape[0] - by, 0)


def unfold_kernel(sizes, width, place, own, other, frame_rows, cot_rows):
    xl, core = place[1], place[2]
    blocks = own.shape[0]

    def step(block, _):
        side = (xl + (block + 1) // 2) % 2
        partner = jnp.where(xl == 0, (block + 2) % 4, block + 1 - 2 * (block % 2))
        left = jnp.where(core == 1, block, partner)
        right = jnp.where(core == 0, block, partner)
        has_left = 2 * side + core > 0
        has_right = 2 * side + core < 3
        for out, (starts, splits) in zip((frame_rows, cot_rows), sizes, strict=True):
            for time, start in enumerate(starts):
                target = pl.ds(pl.multiple_of((time * blocks + block) * PAD, PAD), PAD)
                for tile in range(2 * splits):
                    row, split = tile // splits, tile % splits
                    first = start + tile * width
                    low = other[left, first + width - 8 : first + width, :].astype(jnp.float32)
                    middle = own[block, first : first + width, :].astype(jnp.float32)
                    high = other[right, first : first + 8, :].astype(jnp.float32)
                    low = jnp.where(has_left, low, 0.0)
                    high = jnp.where(has_right, high, 0.0)
                    chunk = jnp.concatenate((low, middle, high), axis=0)
                    for tap in range(3):
                        lane = ((row * 3 + tap) * splits + split) * LANES
                        moved = chunk[6 + tap : 6 + tap + PAD].astype(jnp.bfloat16)
                        out[target, lane : lane + LANES] = moved
        return 0

    lax.fori_loop(0, blocks, step, 0)


def readers(layout, place, own, other):
    nz, up_half, up_count, up_size = layout
    lead = place[2] == 0

    def low(start, count):
        rows = slice(start, start + count)
        return jnp.where(lead, own[:, rows], other[:, rows])

    def high(start, count):
        rows = slice(start, start + count)
        return jnp.where(lead, other[:, rows], own[:, rows])

    def up_tile(kt, kh, kw, split, splits):
        tile = ((kt * 3 + kh) * 3 + kw) * splits + split
        if tile < up_half:
            value = low(tile * nz, nz)
        else:
            value = high((tile - (up_count - up_half)) * nz, nz)
        return value.reshape(-1, LANES)

    def both(tile):
        start = up_size + tile * 2 * nz
        return jnp.stack((low(start, 2 * nz), high(start, 2 * nz)), axis=1).reshape(-1, LANES)

    def mix_tile(kt, kw, pair):
        at = kt * 3 + kw
        if pair == 1:
            return both(at)
        ahead = pltpu.roll(both(at).astype(jnp.float32), LANES // 2, 1)
        last = both(9 + at // 2).astype(jnp.float32)
        if at % 2 == 0:
            last = pltpu.roll(last, LANES // 2, 1)
        lane = lax.broadcasted_iota(jnp.int32, ahead.shape, 1)
        return jnp.where(lane < LANES // 2, ahead, last).astype(jnp.bfloat16)

    return up_tile, mix_tile


def forward_kernel(
    layout, width, place, rows, own, other, outs, slope, up_w, ups, mask, hidden, mix_w, total
):
    up_tile, mix_tile = readers(layout, place, own, other)
    splits = rows.shape[1] // (6 * LANES)
    part, unit = up_w.shape[0] // 6, mask.shape[0]
    column = lax.broadcasted_iota(jnp.int32, (PAD, LANES), 0) - 1
    for block in range(len(outs)):
        side = (place[1] + (block + 1) // 2) % 2
        at = (2 * side + place[2]) * width + column
        inside = (at >= 0) & (at < 4 * width)
        mask[block * PAD : (block + 1) * PAD, :] = inside.astype(jnp.float32)
    for kt in range(3):
        for out_row in range(2):
            for row in range(2):
                for kw in range(3):
                    for split in range(splits):
                        at = kt * 2 * part + out_row * part
                        lane = ((row * 3 + kw) * splits + split) * LANES
                        up_w[at : at + part, lane : lane + LANES] = up_tile(
                            kt, row - out_row + 1, kw, split, splits
                        )
    last = rows.shape[0] - unit
    pair, single = slice(0, 2 * LANES), slice(2 * LANES, 3 * LANES)
    for first, count, lanes in ((unit, last, pair), (0, last, single)):
        for start in range(first, first + count, count // 2):
            at = slice(start, start + count // 2)
            ups[at, lanes] = lax.dot_general(
                rows[at, :],
                up_w[lanes, :],
                (((1,), (1,)), ((), ())),
                preferred_element_type=jnp.float32,
            )
    inside = mask[...] > 0
    times = 2 * (rows.shape[0] // unit - 1) - 1
    for time in range(times):
        at = time // 2 * unit
        if time % 2 == 0:
            before = ups[at + unit : at + 2 * unit, :LANES] + ups[at : at + unit, 2 * LANES :]
        else:
            before = ups[at + unit : at + 2 * unit, LANES : 2 * LANES]
        sigma = jax.nn.sigmoid(before)
        if time < times - 1:
            value = jnp.where(inside, before * sigma, 0.0)
            for kw in range(3):
                hidden[time * unit : (time + 1) * unit, kw * LANES : (kw + 1) * LANES] = later(
                    value, kw
                ).astype(jnp.bfloat16)
        if time >= 2:
            slope[(time - 2) * unit : (time - 1) * unit, :] = jnp.where(
                inside, sigma * (1.0 + before * (1.0 - sigma)), 0.0
            )
    channels = mix_w.shape[0] // 2
    for kt in range(3):
        for out_row in range(2):
            for kw in range(3):
                mix_w[
                    out_row * channels : (out_row + 1) * channels,
                    (kt * 3 + kw) * LANES : (kt * 3 + kw + 1) * LANES,
                ] = mix_tile(kt, kw, out_row)
    total[...] = jnp.zeros_like(total)
    for kt in range(3):
        total[...] += lax.dot_general(
            hidden[kt * unit : kt * unit + total.shape[0], :],
            mix_w[:, kt * 3 * LANES : (kt + 1) * 3 * LANES],
            (((1,), (1,)), ((), ())),
            preferred_element_type=jnp.float32,
        )
    store(outs, total, 0, total.shape[0] // unit, channels, width)


def store(outs, total, base, times, channels, width):
    splits = channels // LANES
    for block, out in enumerate(outs):
        for time in range(times):
            at = (time * len(outs) + block) * PAD
            for tile in range(2 * splits):
                first = base + (time * 2 * splits + tile) * width
                value = total[at : at + width, tile * LANES : (tile + 1) * LANES]
                out[first : first + width, :] = value.astype(jnp.bfloat16)


def add_kernel(sizes, *refs):
    parts, outs = refs[:4], refs[4:]
    first = 0
    for out, (times, splits, width) in zip(outs, sizes, strict=True):
        for time in range(times):
            for row in range(2):
                for split in range(splits):
                    rows = slice(first, first + width)
                    total = parts[0][rows, :].astype(jnp.float32)
                    for part in parts[1:]:
                        total = total + part[rows, :].astype(jnp.float32)
                    lanes = slice(split * LANES, (split + 1) * LANES)
                    out[time, row, :, lanes] = total.astype(jnp.bfloat16)
                    first += width


def backward_kernel(
    layout, width, place, rows, own, other, outs, base, slope, forward_w, mix_w, partial, evens, odds, up_w, total
):
    up_tile, _ = readers(layout, place, own, other)
    channels = rows.shape[1] // 6
    unit = evens.shape[0] - total.shape[0]
    splits = up_w.shape[1] // (2 * LANES)
    part = LANES // 2
    for kt in range(3):
        for row in range(2):
            for shift_w in range(3):
                at = (row * 3 + shift_w) * channels
                lane = (kt * 3 + 2 - shift_w) * LANES
                mix_w[at : at + channels, kt * LANES : (kt + 1) * LANES] = forward_w[
                    row * channels : (row + 1) * channels, lane : lane + LANES
                ]
    last = rows.shape[0] - unit
    pair, single = slice(0, 2 * LANES), slice(2 * LANES, 3 * LANES)
    for first, count, lanes in ((unit, last, pair), (0, last - unit, single)):
        for start in range(first, first + count, count // 2):
            at = slice(start, start + count // 2)
            partial[at, lanes] = jnp.dot(
                rows[at, :], mix_w[:, lanes], preferred_element_type=jnp.float32
            )
    times = rows.shape[0] // unit - 2
    for time in range(times):
        at = time * unit
        hidden_grad = (
            partial[at + 2 * unit : at + 3 * unit, :LANES]
            + partial[at + unit : at + 2 * unit, LANES : 2 * LANES]
            + partial[at : at + unit, 2 * LANES :]
        )
        value = hidden_grad * slope[at : at + unit, :]
        target = evens if time % 2 == 0 else odds
        spot = time // 2 * unit
        for shift_w in range(3):
            target[spot : spot + unit, shift_w * LANES : (shift_w + 1) * LANES] = later(
                value, shift_w
            ).astype(jnp.bfloat16)
    for kt in range(3):
        for shift_w in range(3):
            for row in range(2):
                for out_row in range(2):
                    for split in range(splits):
                        at = (kt * 3 + shift_w) * LANES + row * part
                        lane = (out_row * splits + split) * LANES
                        up_w[at : at + part, lane : lane + LANES] = up_tile(
                            kt, out_row + 1 - row, 2 - shift_w, split, splits
                        )
    count = total.shape[0]
    lhs = (evens[:count, :], odds[:count, :], evens[unit : unit + count, :])
    total[...] = jnp.zeros_like(total)
    for kt in range(3):
        total[...] += jnp.dot(
            lhs[kt],
            up_w[kt * 3 * LANES : (kt + 1) * 3 * LANES, :],
            preferred_element_type=jnp.float32,
        )
    store(outs, total, base, count // unit, splits * LANES, width)


def compute_kernel(layout, width, base, place, frame_rows, cot_rows, own, other, *refs):
    outs, slope, scratch = refs[:4], refs[4], refs[5:]
    forward_kernel(layout, width, place, frame_rows, own, other, outs, slope, *scratch[:6])
    backward_kernel(
        layout, width, place, cot_rows, own, other, outs, base, slope, scratch[4], *scratch[6:]
    )


def call(kernel, outs, scratch, flops, megabytes, place, *operands):
    space = pl.BlockSpec(memory_space=pltpu.VMEM)
    return pl.pallas_call(
        kernel,
        out_shape=outs,
        in_specs=[pl.BlockSpec(memory_space=pltpu.SMEM)] + [space] * len(operands),
        out_specs=jax.tree.map(lambda _: space, outs),
        scratch_shapes=scratch,
        compiler_params=pltpu.CompilerParams(vmem_limit_bytes=megabytes * 2**20),
        cost_estimate=pl.CostEstimate(flops=flops, bytes_accessed=8 * 2**20, transcendentals=0),
    )(place, *operands)


def unfold(place, own, other, sizes, width):
    unit = own.shape[0] * PAD
    outs = tuple(
        jax.ShapeDtypeStruct((len(starts) * unit, 6 * splits * LANES), jnp.bfloat16)
        for starts, splits in sizes
    )
    kernel = functools.partial(unfold_kernel, sizes, width)
    return call(kernel, outs, [], 10**9, 14, place, own, other)


def compute(layout, place, frame_rows, cot_rows, own, other, width, channels, in_channels):
    blocks = own.shape[0]
    unit = blocks * PAD
    times = 2 * (frame_rows.shape[0] // unit - 3)
    base = times * 2 * (channels // LANES) * width
    rows = base + times * (in_channels // LANES) * width
    scratch = [
        pltpu.VMEM(((times + 1) * unit, LANES), jnp.float32),
        pltpu.VMEM((3 * LANES, frame_rows.shape[1]), jnp.bfloat16),
        pltpu.VMEM((frame_rows.shape[0], 3 * LANES), jnp.float32),
        pltpu.VMEM((unit, LANES), jnp.float32),
        pltpu.VMEM(((times + 2) * unit, 3 * LANES), jnp.bfloat16),
        pltpu.VMEM((2 * channels, 9 * LANES), jnp.bfloat16),
        pltpu.VMEM((times * unit, 2 * channels), jnp.float32),
        pltpu.VMEM((cot_rows.shape[1], 3 * LANES), jnp.bfloat16),
        pltpu.VMEM((cot_rows.shape[0], 3 * LANES), jnp.float32),
        pltpu.VMEM((times // 2 * unit + unit, 3 * LANES), jnp.bfloat16),
        pltpu.VMEM((times // 2 * unit, 3 * LANES), jnp.bfloat16),
        pltpu.VMEM((9 * LANES, 2 * in_channels), jnp.bfloat16),
        pltpu.VMEM((times // 2 * unit, 2 * in_channels), jnp.float32),
    ]
    kernel = functools.partial(compute_kernel, layout, width, base)
    out = (jax.ShapeDtypeStruct((rows, LANES), jnp.bfloat16),) * blocks
    return call(kernel, out, scratch, 4 * 10**9, 32, place, frame_rows, cot_rows, own, other)


def add_parts(parts, sizes):
    space = pl.BlockSpec(memory_space=pltpu.VMEM)
    return pl.pallas_call(
        functools.partial(add_kernel, sizes),
        out_shape=tuple(
            jax.ShapeDtypeStruct((times, 2, width, splits * LANES), jnp.bfloat16)
            for times, splits, width in sizes
        ),
        in_specs=[space] * len(parts),
        out_specs=(space, space),
        compiler_params=pltpu.CompilerParams(vmem_limit_bytes=8 * 2**20),
    )(*parts)


def ring(array, by):
    return lax.ppermute(array, RING, [(i, (i + by) % 4) for i in range(4)])


def flat(field):
    tiles = field.reshape(*field.shape[:3], -1, LANES)
    return tiles.transpose(0, 1, 3, 2, 4).reshape(-1, LANES)


def tiles_of(kernel):
    return kernel.reshape(-1, LANES, 2).transpose(0, 2, 1)


def shards(frames, up_kernel, mix_kernel, cotangent):
    frame_count, height, width, in_channels = frames.shape
    out_channels = mix_kernel.shape[0] // 27
    xh, xl, core = lax.axis_index("xh"), lax.axis_index("xl"), lax.axis_index("core")
    ny, nz, nx = lax.axis_size("y"), lax.axis_size("z"), lax.axis_size(RING)
    part = out_channels // nx

    mix_other = lax.ppermute(mix_kernel, RING, [(0, 3), (3, 0), (1, 2), (2, 1)])
    up_column = lax.dynamic_index_in_dim(up_kernel.T, xl, 0, keepdims=False)
    up_tiles = up_column.reshape(-1, LANES)
    up_count = up_tiles.shape[0]
    up_half = (up_count + 1) // 2
    up_part = lax.dynamic_slice_in_dim(up_tiles, core * (up_count - up_half), up_half, 0)
    up_pairs = (up_half + 1) // 2
    up_part = jnp.pad(up_part, ((0, 2 * up_pairs - up_half), (0, 0))).reshape(-1, 2, LANES)

    mix_tiles = tiles_of(jnp.where(xh == core, mix_kernel, mix_other))
    splits = out_channels // LANES
    pick_shape = (2, out_channels, 2 * part)
    slot = lax.broadcasted_iota(jnp.int32, pick_shape, 0)
    source = lax.broadcasted_iota(jnp.int32, pick_shape, 1)
    target = lax.broadcasted_iota(jnp.int32, pick_shape, 2)
    side, spot = target // part, target % part
    wanted = (spot // nz) * (4 * nz) + xh * (2 * nz) + (spot % nz) * 2 + xl
    pick = ((source == wanted) & (slot == side)).astype(jnp.bfloat16)
    pick = pick.reshape(2, splits, LANES, 2 * part)
    taps = mix_tiles.reshape(3, 3, 3, splits, 2, LANES).transpose(0, 2, 1, 3, 4, 5)
    taps = taps.reshape(9, 3, splits, 2, LANES)
    last = jnp.pad(taps[:, 2], ((0, 1), (0, 0), (0, 0), (0, 0))).reshape(5, 2, splits, 2, LANES)
    mix_part = jnp.einsum(
        "thsjl,hslm->tjm",
        jnp.concatenate((taps[:, :2], last), axis=0),
        pick,
        preferred_element_type=jnp.float32,
    ).astype(jnp.bfloat16)

    frame_size, cot_size = 2 * (in_channels // LANES) * width, 2 * splits * width
    count = 2 * frame_count
    block = jnp.concatenate((flat(cotangent[3:]), flat(cotangent[:3]), flat(frames)), axis=0)
    early = (count - 3) * cot_size
    first = block.shape[0]
    previous = shift(block[first - 2 * frame_size :], PLANES, 1)
    following = shift(block[early : count * cot_size + frame_size], PLANES, -1)
    payload, previous, following = lax.optimization_barrier(
        (jnp.concatenate((up_part, mix_part), axis=0), previous, following)
    )
    planes = spread(payload, "z")
    block = jnp.concatenate((block, following, previous), axis=0)
    blocks = (block, ring(block, 1), ring(block, -1), ring(block, 2))
    planes, block = lax.optimization_barrier((planes, block))
    blocks = jnp.stack(blocks)
    others = swap(blocks)
    last = first + 3 * cot_size + frame_size
    cot_starts = [early + time * cot_size for time in range(3)]
    cot_starts += [time * cot_size for time in range(count - 3)]
    cot_starts += [first + time * cot_size for time in range(3)]
    frame_starts = [last + time * frame_size for time in range(2)]
    frame_starts += [count * cot_size + time * frame_size for time in range(frame_count)]
    frame_starts += [first + 3 * cot_size]

    up_rows = planes[:, :up_pairs].transpose(1, 2, 0, 3).reshape(-1, LANES)
    mix_rows = planes[:, up_pairs:].transpose(1, 0, 2, 3).reshape(-1, LANES)
    own = spread(jnp.concatenate((up_rows, mix_rows), axis=0), "y")
    other = swap(own)
    layout = (nz, up_half, up_count, up_rows.shape[0])

    place = jnp.stack((xh, xl, core))
    sizes = ((tuple(frame_starts), in_channels // LANES), (tuple(cot_starts), splits))
    frame_rows, cot_rows = unfold(place, blocks, others, sizes, width)
    parts = compute(
        layout, place, frame_rows, cot_rows, own, other, width, out_channels, in_channels
    )
    parts = (parts[0], ring(parts[3], 2), ring(parts[1], -1), ring(parts[2], 1))
    outs = ((count, splits, width), (frame_count, in_channels // LANES, width))
    return add_parts(parts, outs)


def solution(mesh):
    planes, columns = mesh.devices.shape
    shape = (4, 2, planes // 8, 2, columns // 2)
    fine = Mesh(mesh.devices.reshape(shape), (*PLANES, *COLS))
    placed = P(PLANES, None, COLS, None)
    weights = P(None, PLANES)
    return jax.shard_map(
        shards,
        mesh=fine,
        in_specs=(placed, weights, weights, placed),
        out_specs=(placed, placed),
        check_vma=False,
    )
```

```python
import functools

import jax
import jax.numpy as jnp
from jax import lax
from jax.experimental import pallas as pl
from jax.experimental.pallas import tpu as pltpu
from jax.sharding import Mesh, PartitionSpec as P

PLANES = ("y", "xh", "z")
COLS = ("xl", "core")
RING = ("xh", "xl")
LANES = 128
PAD = 32


def shift(array, axis, by):
    devices = lax.axis_size(axis)
    pairs = [(i, i + by) for i in range(devices) if 0 <= i + by < devices]
    return lax.ppermute(array, axis, pairs)


def swap(array):
    return lax.ppermute(array, "core", [(0, 1), (1, 0)])


def spread(array, axis):
    count = lax.axis_size(axis)
    return lax.all_to_all(
        jnp.broadcast_to(array, (count, *array.shape)), axis, 0, 0, tiled=True
    )


def later(rows, by):
    if by == 0:
        return rows
    return pltpu.roll(rows, rows.shape[0] - by, 0)


def unfold_kernel(sizes, width, place, own, other, frame_rows, cot_rows):
    xl, core = place[1], place[2]
    blocks = own.shape[0]

    def step(block, _):
        side = (xl + (block + 1) // 2) % 2
        partner = jnp.where(xl == 0, (block + 2) % 4, block + 1 - 2 * (block % 2))
        left = jnp.where(core == 1, block, partner)
        right = jnp.where(core == 0, block, partner)
        has_left = 2 * side + core > 0
        has_right = 2 * side + core < 3
        for out, (starts, splits) in zip((frame_rows, cot_rows), sizes, strict=True):
            for time, start in enumerate(starts):
                target = pl.ds(pl.multiple_of((time * blocks + block) * PAD, PAD), PAD)
                for tile in range(2 * splits):
                    row, split = tile // splits, tile % splits
                    first = start + tile * width
                    low = other[left, first + width - 8 : first + width, :].astype(jnp.float32)
                    middle = own[block, first : first + width, :].astype(jnp.float32)
                    high = other[right, first : first + 8, :].astype(jnp.float32)
                    low = jnp.where(has_left, low, 0.0)
                    high = jnp.where(has_right, high, 0.0)
                    chunk = jnp.concatenate((low, middle, high), axis=0)
                    for tap in range(3):
                        lane = ((row * 3 + tap) * splits + split) * LANES
                        moved = chunk[6 + tap : 6 + tap + PAD].astype(jnp.bfloat16)
                        out[target, lane : lane + LANES] = moved
        return 0

    lax.fori_loop(0, blocks, step, 0)


def readers(layout, place, own, other):
    nz, up_half, up_count, up_size = layout
    lead = place[2] == 0

    def low(start, count):
        rows = slice(start, start + count)
        return jnp.where(lead, own[:, rows], other[:, rows])

    def high(start, count):
        rows = slice(start, start + count)
        return jnp.where(lead, other[:, rows], own[:, rows])

    def up_tile(kt, kh, kw, split, splits):
        tile = ((kt * 3 + kh) * 3 + kw) * splits + split
        if tile < up_half:
            value = low(tile * nz, nz)
        else:
            value = high((tile - (up_count - up_half)) * nz, nz)
        return value.reshape(-1, LANES)

    def both(tile):
        start = up_size + tile * 2 * nz
        return jnp.stack((low(start, 2 * nz), high(start, 2 * nz)), axis=1).reshape(-1, LANES)

    def mix_tile(kt, kw, pair):
        at = kt * 3 + kw
        if pair == 1:
            return both(at)
        ahead = pltpu.roll(both(at).astype(jnp.float32), LANES // 2, 1)
        last = both(9 + at // 2).astype(jnp.float32)
        if at % 2 == 0:
            last = pltpu.roll(last, LANES // 2, 1)
        lane = lax.broadcasted_iota(jnp.int32, ahead.shape, 1)
        return jnp.where(lane < LANES // 2, ahead, last).astype(jnp.bfloat16)

    return up_tile, mix_tile


def forward_kernel(
    layout, width, place, rows, own, other, outs, slope, up_w, ups, mask, hidden, mix_w, total
):
    up_tile, mix_tile = readers(layout, place, own, other)
    splits = rows.shape[1] // (6 * LANES)
    part, unit = up_w.shape[0] // 6, mask.shape[0]
    column = lax.broadcasted_iota(jnp.int32, (PAD, LANES), 0) - 1
    for block in range(len(outs)):
        side = (place[1] + (block + 1) // 2) % 2
        at = (2 * side + place[2]) * width + column
        inside = (at >= 0) & (at < 4 * width)
        mask[block * PAD : (block + 1) * PAD, :] = inside.astype(jnp.float32)
    for kt in range(3):
        for out_row in range(2):
            for row in range(2):
                for kw in range(3):
                    for split in range(splits):
                        at = kt * 2 * part + out_row * part
                        lane = ((row * 3 + kw) * splits + split) * LANES
                        up_w[at : at + part, lane : lane + LANES] = up_tile(
                            kt, row - out_row + 1, kw, split, splits
                        )
    last = rows.shape[0] - unit
    pair, single = slice(0, 2 * LANES), slice(2 * LANES, 3 * LANES)
    for first, count, lanes in ((unit, last, pair), (0, last, single)):
        for start in range(first, first + count, count // 2):
            at = slice(start, start + count // 2)
            ups[at, lanes] = lax.dot_general(
                rows[at, :],
                up_w[lanes, :],
                (((1,), (1,)), ((), ())),
                preferred_element_type=jnp.float32,
            )
    inside = mask[...] > 0
    times = 2 * (rows.shape[0] // unit - 1) - 1
    for time in range(times):
        at = time // 2 * unit
        if time % 2 == 0:
            before = ups[at + unit : at + 2 * unit, :LANES] + ups[at : at + unit, 2 * LANES :]
        else:
            before = ups[at + unit : at + 2 * unit, LANES : 2 * LANES]
        sigma = jax.nn.sigmoid(before)
        if time < times - 1:
            value = jnp.where(inside, before * sigma, 0.0)
            for kw in range(3):
                hidden[time * unit : (time + 1) * unit, kw * LANES : (kw + 1) * LANES] = later(
                    value, kw
                ).astype(jnp.bfloat16)
        if time >= 2:
            slope[(time - 2) * unit : (time - 1) * unit, :] = jnp.where(
                inside, sigma * (1.0 + before * (1.0 - sigma)), 0.0
            )
    channels = mix_w.shape[0] // 2
    for kt in range(3):
        for out_row in range(2):
            for kw in range(3):
                mix_w[
                    out_row * channels : (out_row + 1) * channels,
                    (kt * 3 + kw) * LANES : (kt * 3 + kw + 1) * LANES,
                ] = mix_tile(kt, kw, out_row)
    total[...] = jnp.zeros_like(total)
    for kt in range(3):
        total[...] += lax.dot_general(
            hidden[kt * unit : kt * unit + total.shape[0], :],
            mix_w[:, kt * 3 * LANES : (kt + 1) * 3 * LANES],
            (((1,), (1,)), ((), ())),
            preferred_element_type=jnp.float32,
        )
    store(outs, total, 0, total.shape[0] // unit, channels, width)


def store(outs, total, base, times, channels, width):
    splits = channels // LANES
    for block, out in enumerate(outs):
        for time in range(times):
            at = (time * len(outs) + block) * PAD
            for tile in range(2 * splits):
                first = base + (time * 2 * splits + tile) * width
                value = total[at : at + width, tile * LANES : (tile + 1) * LANES]
                out[first : first + width, :] = value.astype(jnp.bfloat16)


def add_kernel(sizes, *refs):
    parts, outs = refs[:4], refs[4:]
    first = 0
    for out, (times, splits, width) in zip(outs, sizes, strict=True):
        for time in range(times):
            for row in range(2):
                for split in range(splits):
                    rows = slice(first, first + width)
                    total = parts[0][rows, :].astype(jnp.float32)
                    for part in parts[1:]:
                        total = total + part[rows, :].astype(jnp.float32)
                    lanes = slice(split * LANES, (split + 1) * LANES)
                    out[time, row, :, lanes] = total.astype(jnp.bfloat16)
                    first += width


def backward_kernel(
    layout, width, place, rows, own, other, outs, base, slope, forward_w, mix_w, partial, evens, odds, up_w, total
):
    up_tile, _ = readers(layout, place, own, other)
    channels = rows.shape[1] // 6
    unit = evens.shape[0] - total.shape[0]
    splits = up_w.shape[1] // (2 * LANES)
    part = LANES // 2
    for kt in range(3):
        for row in range(2):
            for shift_w in range(3):
                at = (row * 3 + shift_w) * channels
                lane = (kt * 3 + 2 - shift_w) * LANES
                mix_w[at : at + channels, kt * LANES : (kt + 1) * LANES] = forward_w[
                    row * channels : (row + 1) * channels, lane : lane + LANES
                ]
    last = rows.shape[0] - unit
    pair, single = slice(0, 2 * LANES), slice(2 * LANES, 3 * LANES)
    for first, count, lanes in ((unit, last, pair), (0, last - unit, single)):
        for start in range(first, first + count, count // 2):
            at = slice(start, start + count // 2)
            partial[at, lanes] = jnp.dot(
                rows[at, :], mix_w[:, lanes], preferred_element_type=jnp.float32
            )
    times = rows.shape[0] // unit - 2
    for time in range(times):
        at = time * unit
        hidden_grad = (
            partial[at + 2 * unit : at + 3 * unit, :LANES]
            + partial[at + unit : at + 2 * unit, LANES : 2 * LANES]
            + partial[at : at + unit, 2 * LANES :]
        )
        value = hidden_grad * slope[at : at + unit, :]
        target = evens if time % 2 == 0 else odds
        spot = time // 2 * unit
        for shift_w in range(3):
            target[spot : spot + unit, shift_w * LANES : (shift_w + 1) * LANES] = later(
                value, shift_w
            ).astype(jnp.bfloat16)
    for kt in range(3):
        for shift_w in range(3):
            for row in range(2):
                for out_row in range(2):
                    for split in range(splits):
                        at = (kt * 3 + shift_w) * LANES + row * part
                        lane = (out_row * splits + split) * LANES
                        up_w[at : at + part, lane : lane + LANES] = up_tile(
                            kt, out_row + 1 - row, 2 - shift_w, split, splits
                        )
    count = total.shape[0]
    lhs = (evens[:count, :], odds[:count, :], evens[unit : unit + count, :])
    total[...] = jnp.zeros_like(total)
    for kt in range(3):
        total[...] += jnp.dot(
            lhs[kt],
            up_w[kt * 3 * LANES : (kt + 1) * 3 * LANES, :],
            preferred_element_type=jnp.float32,
        )
    store(outs, total, base, count // unit, splits * LANES, width)


def compute_kernel(layout, width, base, place, frame_rows, cot_rows, own, other, *refs):
    outs, slope, scratch = refs[:4], refs[4], refs[5:]
    forward_kernel(layout, width, place, frame_rows, own, other, outs, slope, *scratch[:6])
    backward_kernel(
        layout, width, place, cot_rows, own, other, outs, base, slope, scratch[4], *scratch[6:]
    )


def call(kernel, outs, scratch, flops, megabytes, place, *operands):
    space = pl.BlockSpec(memory_space=pltpu.VMEM)
    return pl.pallas_call(
        kernel,
        out_shape=outs,
        in_specs=[pl.BlockSpec(memory_space=pltpu.SMEM)] + [space] * len(operands),
        out_specs=jax.tree.map(lambda _: space, outs),
        scratch_shapes=scratch,
        compiler_params=pltpu.CompilerParams(vmem_limit_bytes=megabytes * 2**20),
        cost_estimate=pl.CostEstimate(flops=flops, bytes_accessed=8 * 2**20, transcendentals=0),
    )(place, *operands)


def unfold(place, own, other, sizes, width):
    unit = own.shape[0] * PAD
    outs = tuple(
        jax.ShapeDtypeStruct((len(starts) * unit, 6 * splits * LANES), jnp.bfloat16)
        for starts, splits in sizes
    )
    kernel = functools.partial(unfold_kernel, sizes, width)
    return call(kernel, outs, [], 10**9, 14, place, own, other)


def compute(layout, place, frame_rows, cot_rows, own, other, width, channels, in_channels):
    blocks = own.shape[0]
    unit = blocks * PAD
    times = 2 * (frame_rows.shape[0] // unit - 3)
    base = times * 2 * (channels // LANES) * width
    rows = base + times * (in_channels // LANES) * width
    scratch = [
        pltpu.VMEM(((times + 1) * unit, LANES), jnp.float32),
        pltpu.VMEM((3 * LANES, frame_rows.shape[1]), jnp.bfloat16),
        pltpu.VMEM((frame_rows.shape[0], 3 * LANES), jnp.float32),
        pltpu.VMEM((unit, LANES), jnp.float32),
        pltpu.VMEM(((times + 2) * unit, 3 * LANES), jnp.bfloat16),
        pltpu.VMEM((2 * channels, 9 * LANES), jnp.bfloat16),
        pltpu.VMEM((times * unit, 2 * channels), jnp.float32),
        pltpu.VMEM((cot_rows.shape[1], 3 * LANES), jnp.bfloat16),
        pltpu.VMEM((cot_rows.shape[0], 3 * LANES), jnp.float32),
        pltpu.VMEM((times // 2 * unit + unit, 3 * LANES), jnp.bfloat16),
        pltpu.VMEM((times // 2 * unit, 3 * LANES), jnp.bfloat16),
        pltpu.VMEM((9 * LANES, 2 * in_channels), jnp.bfloat16),
        pltpu.VMEM((times // 2 * unit, 2 * in_channels), jnp.float32),
    ]
    kernel = functools.partial(compute_kernel, layout, width, base)
    out = (jax.ShapeDtypeStruct((rows, LANES), jnp.bfloat16),) * blocks
    return call(kernel, out, scratch, 4 * 10**9, 32, place, frame_rows, cot_rows, own, other)


def stack_kernel(*refs):
    for member, ref in enumerate(refs[:-1]):
        refs[-1][member] = ref[...]


def gathered(*blocks):
    space = pl.BlockSpec(memory_space=pltpu.VMEM)
    return pl.pallas_call(
        stack_kernel,
        out_shape=jax.ShapeDtypeStruct((len(blocks), *blocks[0].shape), blocks[0].dtype),
        in_specs=[space] * len(blocks),
        out_specs=space,
        compiler_params=pltpu.CompilerParams(vmem_limit_bytes=8 * 2**20),
    )(*blocks)


def add_parts(parts, sizes):
    space = pl.BlockSpec(memory_space=pltpu.VMEM)
    return pl.pallas_call(
        functools.partial(add_kernel, sizes),
        out_shape=tuple(
            jax.ShapeDtypeStruct((times, 2, width, splits * LANES), jnp.bfloat16)
            for times, splits, width in sizes
        ),
        in_specs=[space] * len(parts),
        out_specs=(space, space),
        compiler_params=pltpu.CompilerParams(vmem_limit_bytes=8 * 2**20),
    )(*parts)


def ring(array, by):
    return lax.ppermute(array, RING, [(i, (i + by) % 4) for i in range(4)])


def flat(field):
    tiles = field.reshape(*field.shape[:3], -1, LANES)
    return tiles.transpose(0, 1, 3, 2, 4).reshape(-1, LANES)


def tiles_of(kernel):
    return kernel.reshape(-1, LANES, 2).transpose(0, 2, 1)


def shards(frames, up_kernel, mix_kernel, cotangent):
    frame_count, height, width, in_channels = frames.shape
    out_channels = mix_kernel.shape[0] // 27
    xh, xl, core = lax.axis_index("xh"), lax.axis_index("xl"), lax.axis_index("core")
    ny, nz, nx = lax.axis_size("y"), lax.axis_size("z"), lax.axis_size(RING)
    part = out_channels // nx

    mix_other = lax.ppermute(mix_kernel, RING, [(0, 3), (3, 0), (1, 2), (2, 1)])
    up_column = lax.dynamic_index_in_dim(up_kernel.T, xl, 0, keepdims=False)
    up_tiles = up_column.reshape(-1, LANES)
    up_count = up_tiles.shape[0]
    up_half = (up_count + 1) // 2
    up_part = lax.dynamic_slice_in_dim(up_tiles, core * (up_count - up_half), up_half, 0)
    up_pairs = (up_half + 1) // 2
    up_part = jnp.pad(up_part, ((0, 2 * up_pairs - up_half), (0, 0))).reshape(-1, 2, LANES)

    mix_tiles = tiles_of(jnp.where(xh == core, mix_kernel, mix_other))
    splits = out_channels // LANES
    pick_shape = (2, out_channels, 2 * part)
    slot = lax.broadcasted_iota(jnp.int32, pick_shape, 0)
    source = lax.broadcasted_iota(jnp.int32, pick_shape, 1)
    target = lax.broadcasted_iota(jnp.int32, pick_shape, 2)
    side, spot = target // part, target % part
    wanted = (spot // nz) * (4 * nz) + xh * (2 * nz) + (spot % nz) * 2 + xl
    pick = ((source == wanted) & (slot == side)).astype(jnp.bfloat16)
    pick = pick.reshape(2, splits, LANES, 2 * part)
    taps = mix_tiles.reshape(3, 3, 3, splits, 2, LANES).transpose(0, 2, 1, 3, 4, 5)
    taps = taps.reshape(9, 3, splits, 2, LANES)
    last = jnp.pad(taps[:, 2], ((0, 1), (0, 0), (0, 0), (0, 0))).reshape(5, 2, splits, 2, LANES)
    mix_part = jnp.einsum(
        "thsjl,hslm->tjm",
        jnp.concatenate((taps[:, :2], last), axis=0),
        pick,
        preferred_element_type=jnp.float32,
    ).astype(jnp.bfloat16)

    frame_size, cot_size = 2 * (in_channels // LANES) * width, 2 * splits * width
    count = 2 * frame_count
    block = jnp.concatenate((flat(cotangent[3:]), flat(cotangent[:3]), flat(frames)), axis=0)
    early = (count - 3) * cot_size
    first = block.shape[0]
    previous = shift(block[first - 2 * frame_size :], PLANES, 1)
    following = shift(block[early : count * cot_size + frame_size], PLANES, -1)
    payload, previous, following = lax.optimization_barrier(
        (jnp.concatenate((up_part, mix_part), axis=0), previous, following)
    )
    planes = spread(payload, "z")
    block = jnp.concatenate((block, following, previous), axis=0)
    blocks = (block, ring(block, 1), ring(block, -1), ring(block, 2))
    planes, block = lax.optimization_barrier((planes, block))
    blocks = gathered(block, *blocks[1:])
    others = swap(blocks)
    last = first + 3 * cot_size + frame_size
    cot_starts = [early + time * cot_size for time in range(3)]
    cot_starts += [time * cot_size for time in range(count - 3)]
    cot_starts += [first + time * cot_size for time in range(3)]
    frame_starts = [last + time * frame_size for time in range(2)]
    frame_starts += [count * cot_size + time * frame_size for time in range(frame_count)]
    frame_starts += [first + 3 * cot_size]

    up_rows = planes[:, :up_pairs].transpose(1, 2, 0, 3).reshape(-1, LANES)
    mix_rows = planes[:, up_pairs:].transpose(1, 0, 2, 3).reshape(-1, LANES)
    own = spread(jnp.concatenate((up_rows, mix_rows), axis=0), "y")
    other = swap(own)
    layout = (nz, up_half, up_count, up_rows.shape[0])

    place = jnp.stack((xh, xl, core))
    sizes = ((tuple(frame_starts), in_channels // LANES), (tuple(cot_starts), splits))
    frame_rows, cot_rows = unfold(place, blocks, others, sizes, width)
    parts = compute(
        layout, place, frame_rows, cot_rows, own, other, width, out_channels, in_channels
    )
    parts = (parts[0], ring(parts[3], 2), ring(parts[1], -1), ring(parts[2], 1))
    outs = ((count, splits, width), (frame_count, in_channels // LANES, width))
    return add_parts(parts, outs)


def solution(mesh):
    planes, columns = mesh.devices.shape
    shape = (4, 2, planes // 8, 2, columns // 2)
    fine = Mesh(mesh.devices.reshape(shape), (*PLANES, *COLS))
    placed = P(PLANES, None, COLS, None)
    weights = P(None, PLANES)
    return jax.shard_map(
        shards,
        mesh=fine,
        in_specs=(placed, weights, weights, placed),
        out_specs=(placed, placed),
        check_vma=False,
    )
```
